32 devices in a mesh: groups: 2 (over x), shard: 16 (over z, y, core).
Axes of the slice: x: 2, y: 2, z: 4, core: 2. Of those that a mesh axis runs over, the one named last changes fastest.
Arguments:
- hidden: bfloat16 [8192, 2048], P(('groups', 'shard')), parts along dimension 0, may hold values from -10 to 10
- query_rows: bfloat16 [8192, 4096], P(('groups', 'shard')), parts along dimension 0, may hold values from -9 to 9
- key_rows: bfloat16 [8192, 512], P(('groups', 'shard')), parts along dimension 0, may hold values from -9 to 9
- value_rows: bfloat16 [8192, 512], P(('groups', 'shard')), parts along dimension 0, may hold values from -6 to 6
- counts: int32 [2], P('groups'), parts along dimension 0, may hold values from 1024 to 4096
- out_weight: bfloat16 [4096, 2048], P('shard'), may hold values from -0.09375 to 0.09375
- norm_gain: bfloat16 [2048], replicated, may hold values from 0.099609375 to 1.8984375
- route_ids: int32 [8192, 8], P(('groups', 'shard')), parts along dimension 0, may hold values from 0 to 31, all different within a row; in each aligned block of 256 rows (0 to 255, 256 to 511, ...) at most 80 rows name the same one
- route_weights: bfloat16 [8192, 8], P(('groups', 'shard')), parts along dimension 0, may hold values from 0.099609375 to 0.3984375
- w_gate: bfloat16 [32, 2048, 768], P('shard'), may hold values from -0.125 to 0.125
- w_up: bfloat16 [32, 2048, 768], P('shard'), may hold values from -0.125 to 0.125
- w_down: bfloat16 [32, 768, 2048], P('shard'), may hold values from -0.21875 to 0.21875
Outputs:
- layer_out: bfloat16 [8192, 2048], P(('groups', 'shard')), parts along dimension 0
The draws below stay inside these ranges and needn't reach their ends.
There are 2 independent parts, one for each index of `groups`. The reference program is written for one: setup_inputs(seed, part) draws one part's arguments, and reference() takes and returns one part's arrays. A program takes and returns all parts, laid end to end along the dimension named above; an argument that names none is the same for every part. Nothing has to cross between parts.
Inputs may be any that keep to these rules, and one draw needn't show every extreme that they name: `route_ids`: each row names 8 different experts; in the rows of one device no expert is named by more than 80 rows, a bound that some block reaches.
All inputs are finite; a program needn't handle non-finite values.
Results may differ from the reference program's by a relative error of at most 0.008.
Values may be sent and summed in bfloat16 or wider, within the bound.
A program may use at most 384 MiB of HBM per device.

```python
import math
import jax
import jax.numpy as jnp
import numpy as np
from jax import lax

D = 2048
HEADS = 32
KV_HEADS = 4
HD = 128
FF = 768
TOPK = 8
SEQS = 1
SEQ_LEN = 4096
EXPERTS = 32
TOKENS = 4096
TOK_DEV = 256
CAP = 80
N_SHARD = 16


def draw_query_rows(key, part):
    result = jnp.clip(jax.random.normal(jax.random.fold_in(key, 1), (TOKENS, HEADS, HD), jnp.float32), -5.0, 5.0)
    return result.reshape(TOKENS, HEADS * HD).astype(jnp.bfloat16)


def draw_key_rows(key, part):
    result = jnp.clip(jax.random.normal(jax.random.fold_in(key, 2), (TOKENS, KV_HEADS, HD), jnp.float32), -5.0, 5.0)
    return result.reshape(TOKENS, KV_HEADS * HD).astype(jnp.bfloat16)


def draw_hidden(key, part):
    result = jnp.clip(jax.random.normal(jax.random.fold_in(key, 3), (TOKENS, D), jnp.float32), -5.0, 5.0)
    return result.astype(jnp.bfloat16)


def block_scale(rng, dims, shards, least, top_value):
    gain = 1.0
    for axis_at, shards_of in shards:
        heights = jax.random.uniform(jax.random.fold_in(jax.random.fold_in(rng, 6), axis_at), (shards_of,), jnp.float32, least / len(shards), top_value / len(shards))
        gain = gain * jnp.repeat(jnp.exp(heights), dims[axis_at] // shards_of).reshape((-1,) + (1,) * (len(dims) - 1 - axis_at))
    return gain


def shared_out(stream_key, own, number, rows, count, top, most, slope):
    sequence = jax.random.permutation(stream_key, count)
    heavy_load, usual = load_shares(count, rows * top, most, slope, True), load_shares(count, rows * top, most, slope, False)
    places = jnp.arange(count)

    def named(sizes, rotation):
        used = int((sizes > 0).sum())
        fixed = max(1, used // 4)
        shifted = fixed + (places - fixed + rotation * (used - fixed)) % max(1, count - fixed)
        return jnp.zeros((count,), jnp.int32).at[sequence[jnp.where(places < fixed, places, shifted)]].set(jnp.asarray(sizes, jnp.int32))

    sizes = jnp.where(number % 4 == 0, named(heavy_load, number // 4), named(usual, number - number // 4 - 1))
    mixed = jax.random.permutation(jax.random.fold_in(own, 3), count)
    giver, receiver = mixed[0:count // 2 * 2:2], mixed[1:count // 2 * 2:2]
    margin = jnp.minimum(sizes[giver] - 1, most - sizes[receiver]) // 2
    margin = jnp.where((giver == sequence[0]) | (receiver == sequence[0]) | (sizes[receiver] == 0), 0, jnp.maximum(margin, 0))
    shifted = jax.random.randint(jax.random.fold_in(own, 4), (count // 2,), 0, 1 << 20) % (margin + 1)
    sizes = sizes.at[giver].add(-shifted).at[receiver].add(shifted)
    members = jnp.searchsorted(jnp.cumsum(sizes), jnp.arange(rows * top), side="right").astype(jnp.int32)
    listing = members.reshape(top, rows).T
    listing = listing[jax.random.permutation(jax.random.fold_in(own, 1), rows)]
    rotation = jax.random.randint(jax.random.fold_in(own, 2), (rows, 1), 0, top)
    return jnp.take_along_axis(listing, (jnp.arange(top)[None, :] + rotation) % top, axis=1)


def load_shares(amount, total, reach, slope, full):
    portions = [(1 << 20) // math.isqrt(rank ** slope) + 1 for rank in range(1, amount + 1)]
    largest = reach if full else min(reach, max(-(-total // amount), total * portions[0] // sum(portions)))
    least = 1 if total - largest >= amount - 1 else 0
    given, surplus = [largest] + [least] * (amount - 1), total - largest - least * (amount - 1)
    while surplus > 0:
        free = [i for i in range(1, amount) if given[i] < largest] or [i for i in range(1, amount) if given[i] < reach]
        mass, budget = sum([portions[i] for i in free]), surplus
        for i in free:
            extra = min(reach - given[i], max(1, budget * portions[i] // mass), surplus)
            given[i] = given[i] + extra
            surplus = surplus - extra
    return np.array(given)


def normal_values(key, dims, width, reach, cuts=(), kind=jnp.bfloat16):
    values = jax.random.normal(key, dims, jnp.float32) * width
    if len(cuts) > 0:
        values = block_scale(key, dims, cuts, -0.22, 0.18) * values
    return jnp.clip(values, min=-reach, max=reach).astype(kind)


def setup_inputs(seed: int = 0, part: int = 0) -> dict:
    streams_of = jax.random.split(jax.random.key(seed), 13)
    part_splits = jax.random.split(jax.random.fold_in(streams_of[12], part), 13)
    hidden = draw_hidden(jax.random.fold_in(jax.random.fold_in(streams_of[12], part), 71), part)
    query_rows = draw_query_rows(jax.random.fold_in(jax.random.fold_in(streams_of[12], part), 71), part)
    key_rows = draw_key_rows(jax.random.fold_in(jax.random.fold_in(streams_of[12], part), 71), part)
    value_rows = normal_values(part_splits[3], (TOKENS, KV_HEADS * HD), 1.0, 6.0, ((0, 16),))
    counts = jax.random.randint(part_splits[4], (SEQS,), SEQ_LEN // 4, SEQ_LEN + 1).astype(jnp.int32)
    out_weight = normal_values(streams_of[5], (HEADS * HD, D), (HEADS * HD) ** -0.5, 0.09375, ((0, 16),))
    norm_gain = jnp.clip(1.0 + 0.18 * jax.random.normal(streams_of[6], (D,), jnp.float32), 0.099609375, 1.8984375).astype(jnp.bfloat16)
    route_ids_keys = jax.random.split(jax.random.fold_in(part_splits[7], 1), TOKENS // TOK_DEV)
    route_ids_turns = jax.random.permutation(jax.random.fold_in(part_splits[7], 3), TOKENS // TOK_DEV)
    route_ids = jax.vmap(lambda own, number: shared_out(jax.random.fold_in(part_splits[7], 2), own, number, TOK_DEV, EXPERTS, TOPK, CAP, 2))(route_ids_keys, route_ids_turns).reshape((TOKENS, TOPK))
    route_weights = jnp.clip(0.099609375 + 0.29882812 * jax.random.uniform(part_splits[8], (TOKENS, TOPK), jnp.float32) ** block_scale(part_splits[8], (TOKENS, TOPK), ((0, 16),), -0.2, 0.2), 0.099609375, 0.3984375).astype(jnp.bfloat16)
    w_gate = normal_values(streams_of[9], (EXPERTS, D, FF), D ** -0.5, 0.125, ((0, 16),))
    w_up = normal_values(streams_of[10], (EXPERTS, D, FF), D ** -0.5, 0.125, ((0, 16),))
    w_down = normal_values(streams_of[11], (EXPERTS, FF, D), FF ** -0.5, 0.21875, ((0, 16),))
    return dict(hidden=hidden, query_rows=query_rows, key_rows=key_rows, value_rows=value_rows, counts=counts, out_weight=out_weight, norm_gain=norm_gain, route_ids=route_ids, route_weights=route_weights, w_gate=w_gate, w_up=w_up, w_down=w_down)


def attend_sequence(query_seq, key_seq, value_seq, live_count):
    length = query_seq.shape[0]
    group_size = HEADS // KV_HEADS
    score_scale = 1.0 / HD ** 0.5
    row_pos = jnp.arange(length)[:, None]
    col_pos = jnp.arange(length)[None, :]
    visible = (col_pos <= row_pos) & (col_pos < live_count)
    live_rows = jnp.arange(length) < live_count
    query_heads = query_seq.reshape(length, HEADS, HD).transpose(1, 0, 2)
    key_heads = key_seq.reshape(length, KV_HEADS, HD).transpose(1, 0, 2)
    value_heads = value_seq.reshape(length, KV_HEADS, HD).transpose(1, 0, 2)

    def one_head(head_index):
        query_here = query_heads[head_index]
        key_here = key_heads[head_index // group_size]
        value_here = value_heads[head_index // group_size]
        scores = jnp.dot(query_here, key_here.T, preferred_element_type=jnp.float32) * score_scale
        row_max = lax.optimization_barrier(jnp.max(jnp.where(visible, scores, -1e+30), axis=1, keepdims=True))
        expo = jnp.where(visible, jnp.exp(scores - row_max), 0.0)
        denom = lax.optimization_barrier(jnp.sum(expo, axis=1, keepdims=True))
        summed = jnp.dot(expo.astype(jnp.bfloat16), value_here, preferred_element_type=jnp.float32)
        result = jnp.where(live_rows[:, None], summed / denom, 0.0)
        return result.astype(jnp.bfloat16)
    outputs = lax.map(one_head, jnp.arange(HEADS))
    return outputs.transpose(1, 0, 2).reshape(length, HEADS * HD)

def reference(hidden, query_rows, key_rows, value_rows, counts, out_weight, norm_gain, route_ids, route_weights, w_gate, w_up, w_down):
    pieces = []
    for seq_number in range(SEQS):
        row_start = seq_number * SEQ_LEN
        pieces.append(attend_sequence(query_rows[row_start:row_start + SEQ_LEN], key_rows[row_start:row_start + SEQ_LEN], value_rows[row_start:row_start + SEQ_LEN], counts[seq_number]))
    attended = jnp.concatenate(pieces, axis=0)
    group_cols = HEADS // N_SHARD * HD

    def add_group(total, group_index):
        col_start = (group_index * group_cols).astype(jnp.int32)
        cols = lax.dynamic_slice_in_dim(attended, col_start, group_cols, 1)
        rows = lax.dynamic_slice_in_dim(out_weight, col_start, group_cols, 0)
        part = jnp.dot(cols, rows, preferred_element_type=jnp.float32).astype(jnp.bfloat16)
        part = lax.optimization_barrier(part)
        return (total + part.astype(jnp.float32), None)
    head_total, _ = lax.scan(add_group, jnp.zeros((TOKENS, D), jnp.float32), jnp.arange(N_SHARD, dtype=jnp.int32))
    mixed_rows = hidden.astype(jnp.float32) + head_total
    mean_square = lax.optimization_barrier(jnp.mean(mixed_rows * mixed_rows, axis=1, keepdims=True))
    normed = (mixed_rows * lax.rsqrt(mean_square + 1e-06) * norm_gain.astype(jnp.float32)).astype(jnp.bfloat16)
    token_index = jnp.arange(TOKENS)
    token_live = token_index % SEQ_LEN < counts[token_index // SEQ_LEN]
    route_live = jnp.where(token_live[:, None], route_weights.astype(jnp.float32), jnp.float32(0.0))
    limit = N_SHARD * CAP

    def expert_step(expert_sum, expert):
        matches = route_ids == expert
        weight_row = lax.optimization_barrier(jnp.sum(jnp.where(matches, route_live, jnp.float32(0.0)), axis=1))
        hit_row = jnp.any(matches, axis=1)
        chosen = jnp.nonzero(hit_row, size=limit, fill_value=0)[0]
        valid = jnp.arange(limit) < jnp.sum(hit_row.astype(jnp.int32))
        chosen_rows = normed[chosen]
        gate_proj = jnp.dot(chosen_rows, w_gate[expert], preferred_element_type=jnp.float32)
        up_proj = jnp.dot(chosen_rows, w_up[expert], preferred_element_type=jnp.float32)
        activated = (jax.nn.silu(gate_proj) * up_proj).astype(jnp.bfloat16)
        output = jnp.dot(activated, w_down[expert], preferred_element_type=jnp.float32)
        contribution = (weight_row[chosen][:, None] * output).astype(jnp.bfloat16)
        contribution = lax.optimization_barrier(contribution).astype(jnp.float32)
        contribution = jnp.where(valid[:, None], contribution, jnp.float32(0.0))
        return (expert_sum.at[chosen].add(contribution), None)
    expert_sum, _ = lax.scan(expert_step, jnp.zeros((TOKENS, D), jnp.float32), jnp.arange(EXPERTS))
    return (mixed_rows + expert_sum).astype(jnp.bfloat16)
```

```python
import functools
import math

import jax
import jax.numpy as jnp
from jax import lax
from jax.experimental import pallas as pl
from jax.experimental.pallas import tpu as pltpu
from jax.sharding import PartitionSpec as P

HD = 128
SEQ_LEN = 4096
NEG = -1e30
MESH = pl.DeviceIdType.MESH


def ring_place(chips, index):
    if chips == 8:
        z, y = index // 2, index % 2
        return z + y * (7 - 2 * z)
    return index


def ring_chip(chips, place):
    if chips == 8:
        half = place // 4
        z = place + half * (7 - 2 * place)
        return 2 * z + half
    return place


def gather_moves(devices, pieces, x_ref, o_ref, local_sem, near_send, near_recv, send, recv):
    chips = devices // 2
    me = lax.axis_index("shard")
    group = lax.axis_index("groups")
    core = me % 2
    place = ring_place(chips, me // 2)

    def device_at(offset):
        return ring_chip(chips, (place + offset + 2 * chips) % chips) * 2 + core

    right, left, sibling = device_at(1), device_at(-1), me + 1 - 2 * core
    rows = x_ref.shape[0] // (2 * pieces)

    def part(ref, way, piece):
        return ref.at[pl.ds((way * pieces + piece) * rows, rows)]

    def hop(step, way, piece):
        origin = device_at(-step if way == 0 else step)
        src = part(x_ref if step == 0 else o_ref.at[origin], way, piece)
        return pltpu.make_async_remote_copy(
            src_ref=src,
            dst_ref=part(o_ref.at[origin], way, piece),
            send_sem=send.at[step, way, piece],
            recv_sem=recv.at[step, way, piece],
            device_id=(group, right if way == 0 else left),
            device_id_type=MESH,
        )

    def landing(step, way, piece):
        origin = device_at(-step - 1 if way == 0 else step + 1)
        place_of = part(o_ref.at[origin], way, piece)
        return pltpu.make_async_remote_copy(
            src_ref=place_of,
            dst_ref=place_of,
            send_sem=send.at[step, way, piece],
            recv_sem=recv.at[step, way, piece],
            device_id=(group, right if way == 0 else left),
            device_id_type=MESH,
        )

    def near(step, way, piece):
        if step < 0:
            src, origin = part(x_ref, way, piece), me
        else:
            origin = device_at(-step - 1 if way == 0 else step + 1)
            src = part(o_ref.at[origin], way, piece)
        return pltpu.make_async_remote_copy(
            src_ref=src,
            dst_ref=part(o_ref.at[origin], way, piece),
            send_sem=near_send.at[step + 1, way, piece],
            recv_sem=near_recv.at[step + 1, way, piece],
            device_id=(group, sibling),
            device_id_type=MESH,
        )

    def near_landing(step, way, piece):
        if step < 0:
            origin = sibling
        else:
            origin = device_at(-step - 1 if way == 0 else step + 1) + 1 - 2 * core
        place_of = part(o_ref.at[origin], way, piece)
        return pltpu.make_async_remote_copy(
            src_ref=place_of,
            dst_ref=place_of,
            send_sem=near_send.at[step + 1, way, piece],
            recv_sem=near_recv.at[step + 1, way, piece],
            device_id=(group, sibling),
            device_id_type=MESH,
        )

    every = [(way, piece) for piece in range(pieces) for way in range(2)]
    own = pltpu.make_async_copy(x_ref, o_ref.at[me], local_sem)

    def begin():
        barrier = pltpu.get_barrier_semaphore()
        for other in (right, left, sibling):
            pl.semaphore_signal(barrier, inc=1, device_id=(group, other), device_id_type=MESH)
        pl.semaphore_wait(barrier, 3)
        for way, piece in every:
            hop(0, way, piece).start()
        own.start()
        for way, piece in every:
            near(-1, way, piece).start()

    def stage(step):
        for way, piece in every:
            landing(step, way, piece).wait_recv()
            if step + 1 < chips - 1:
                hop(step + 1, way, piece).start()
            near(step, way, piece).start()

    def finish():
        own.wait()
        for step in range(chips - 1):
            for way, piece in every:
                hop(step, way, piece).wait_send()
        for step in range(-1, chips - 1):
            for way, piece in every:
                near(step, way, piece).wait_send()
                near_landing(step, way, piece).wait_recv()

    return begin, stage, finish


def gather_kernel(devices, pieces, x_ref, o_ref, *sems):
    begin, stage, finish = gather_moves(devices, pieces, x_ref, o_ref, *sems)
    begin()
    for step in range(devices // 2 - 1):
        stage(step)
    finish()


def gather_scratch(devices, pieces):
    dma = pltpu.SemaphoreType.DMA
    return [dma] + [dma((devices // 2, 2, pieces))] * 4


def ring_gather(x, devices, collective_id, pieces=2):
    return pl.pallas_call(
        functools.partial(gather_kernel, devices, pieces),
        out_shape=jax.ShapeDtypeStruct((devices,) + x.shape, x.dtype),
        in_specs=[pl.BlockSpec(memory_space=pltpu.HBM)],
        out_specs=pl.BlockSpec(memory_space=pltpu.HBM),
        scratch_shapes=gather_scratch(devices, pieces),
        compiler_params=pltpu.CompilerParams(collective_id=collective_id, has_side_effects=True),
    )(x)


def attend_kernel(
    devices, pieces, step_rows, heads, groups,
    count_ref, q_ref, k_ref, v_ref, w_ref, o_ref, all_ref, qs, top, total, *sems
):
    begin, stage, finish = gather_moves(devices, pieces, w_ref, all_ref, *sems)
    rows = q_ref.shape[0]
    scale = math.log2(math.e) / math.sqrt(HD)
    count = count_ref[0]
    first = lax.axis_index("shard") * rows
    blocks = (first + rows + step_rows - 1) // step_rows
    j = pl.program_id(1)
    steps = k_ref.shape[0] // step_rows
    at_step = pl.program_id(0) * steps + j
    all_steps = groups * steps

    @pl.when(at_step == 0)
    def _():
        begin()

    @pl.when(j == 0)
    def _():
        for h in range(heads):
            qs[h * rows : (h + 1) * rows, :] = q_ref[:, h * HD : (h + 1) * HD]
        top[...] = jnp.full(top.shape, NEG, jnp.float32)
        total[...] = jnp.zeros(total.shape, jnp.float32)

    def fold(masked):
        start = pl.multiple_of(j * step_rows, step_rows)
        keys = k_ref[pl.ds(start, step_rows), :]
        ones = jnp.ones((step_rows, HD), jnp.bfloat16)
        values = jnp.concatenate([v_ref[pl.ds(start, step_rows), :], ones], axis=1)
        if masked:
            at_row = first + lax.broadcasted_iota(jnp.int32, (rows, step_rows), 0)
            at_col = start + lax.broadcasted_iota(jnp.int32, (rows, step_rows), 1)
            visible = (at_col <= at_row) & (at_col < count)
        for h in range(heads):
            span = slice(h * rows, (h + 1) * rows)
            scores = lax.dot_general(
                qs[span, :], keys, (((1,), (1,)), ((), ())), preferred_element_type=jnp.float32
            )
            if masked:
                scores = jnp.where(visible, scores, NEG)
            old = top[span, :]
            new = jnp.maximum(old, jnp.max(scores, axis=1, keepdims=True) * scale)
            expo = jnp.exp2(scores * scale - new[:, :1]).astype(jnp.bfloat16)
            factor = jnp.exp2(old - new)
            part = jnp.dot(expo, values, preferred_element_type=jnp.float32)
            total[span, :] = total[span, :] * jnp.concatenate([factor, factor], axis=1) + part
            top[span, :] = new

    @pl.when(j < blocks - 1)
    def _():
        fold(False)

    @pl.when(j == blocks - 1)
    def _():
        fold(True)

        live = first + lax.broadcasted_iota(jnp.int32, (rows, HD), 0) < count
        for h in range(heads):
            both = total[h * rows : (h + 1) * rows, :]
            result = jnp.where(live, both[:, :HD] / jnp.where(live, both[:, HD:], 1.0), 0.0)
            o_ref[:, h * HD : (h + 1) * HD] = result.astype(jnp.bfloat16)

    stages = devices // 2 - 1
    for number in range(stages):

        @pl.when(at_step == (number + 1) * all_steps // stages - 1)
        def _(number=number):
            stage(number)

    @pl.when(at_step == all_steps - 1)
    def _():
        finish()


def attend(count, queries, keys_values, out_weight, kv_count, devices, collective_id, pieces=2):
    rows, width = queries.shape
    length = keys_values.shape[0]
    heads = width // HD // kv_count
    step_rows = math.gcd(length, 512)
    hbm = pl.BlockSpec(memory_space=pltpu.HBM)
    return pl.pallas_call(
        functools.partial(attend_kernel, devices, pieces, step_rows, heads, kv_count),
        grid=(kv_count, length // step_rows),
        out_shape=(
            jax.ShapeDtypeStruct((rows, width), jnp.bfloat16),
            jax.ShapeDtypeStruct((devices,) + out_weight.shape, jnp.bfloat16),
        ),
        in_specs=[
            pl.BlockSpec(memory_space=pltpu.SMEM),
            pl.BlockSpec((rows, heads * HD), lambda g, j: (0, g)),
            pl.BlockSpec((length, HD), lambda g, j: (0, g)),
            pl.BlockSpec((length, HD), lambda g, j: (0, kv_count + g)),
            hbm,
        ],
        out_specs=(pl.BlockSpec((rows, heads * HD), lambda g, j: (0, g)), hbm),
        scratch_shapes=[
            pltpu.VMEM((heads * rows, HD), jnp.bfloat16),
            pltpu.VMEM((heads * rows, HD), jnp.float32),
            pltpu.VMEM((heads * rows, 2 * HD), jnp.float32),
        ]
        + gather_scratch(devices, pieces),
        compiler_params=pltpu.CompilerParams(
            collective_id=collective_id, has_side_effects=True, vmem_limit_bytes=40 << 20
        ),
    )(count, queries, keys_values, keys_values, out_weight)


def moe_kernel(
    devices, live, cap, pieces,
    x_ref, info_ref, wg_ref, wu_ref, wd_ref, o_ref, all_ref,
    wg, wu, wd, xb, picked, chosen, part, away, near_in, ring_in,
    w_sem, x_sem, g_send, g_recv, n_send, n_recv, s_send, s_recv, a_send, a_recv,
):
    chips = devices // 2
    me = lax.axis_index("shard")
    group = lax.axis_index("groups")
    core = me % 2
    way = 1 - 2 * core
    place = ring_place(chips, me // 2)
    rows, depth = x_ref.shape
    local = wg.shape[0]

    def chip_at(offset):
        return ring_chip(chips, (place + offset + 2 * chips) % chips)

    def own_origin(t):
        return chip_at(-way * t) * 2 + core

    def sib_origin(t):
        return chip_at(way * t) * 2 + 1 - core

    def when_live(origin, action):
        if live == chips:
            action()
        else:
            pl.when(origin // 2 < live)(action)

    ahead, behind, sibling = own_origin(-1), own_origin(1), me + way

    def span(piece):
        size = rows // pieces
        return pl.ds(piece * size, size)

    def remote(src, dst, send, recv, to):
        return pltpu.make_async_remote_copy(
            src_ref=src, dst_ref=dst, send_sem=send, recv_sem=recv,
            device_id=(group, to), device_id_type=MESH,
        )

    def hop(t, piece, src=None):
        place_of = all_ref.at[own_origin(t), span(piece)]
        src = place_of if src is None else src.at[span(piece)]
        return remote(src, place_of, g_send.at[t, piece], g_recv.at[t, piece], ahead)

    def near(t, piece, src=None):
        place_of = all_ref.at[own_origin(t), span(piece)]
        src = place_of if src is None else src.at[span(piece)]
        return remote(src, place_of, n_send.at[t, piece], n_recv.at[t, piece], sibling)

    def near_landing(t, piece):
        place_of = all_ref.at[sib_origin(t), span(piece)]
        return remote(place_of, place_of, n_send.at[t, piece], n_recv.at[t, piece], sibling)

    def landing(t, piece):
        place_of = all_ref.at[own_origin(t + 1), span(piece)]
        return remote(place_of, place_of, g_send.at[t, piece], g_recv.at[t, piece], ahead)

    def give(t):
        return remote(away.at[t % 2], near_in.at[t], a_send.at[t], a_recv.at[t], sibling)

    def pass_on(t, piece):
        return remote(
            part.at[t + 1, span(piece)], ring_in.at[t, span(piece)],
            s_send.at[t, piece], s_recv.at[t, piece], ahead,
        )

    loads = [
        pltpu.make_async_copy(src, dst, w_sem.at[i])
        for i, (src, dst) in enumerate(((wg_ref, wg), (wu_ref, wu), (wd_ref, wd)))
    ]

    barrier = pltpu.get_barrier_semaphore()
    for other in (ahead, behind, sibling):
        pl.semaphore_signal(barrier, inc=1, device_id=(group, other), device_id_type=MESH)
    pl.semaphore_wait(barrier, 3)

    def begin():
        for piece in range(pieces):
            hop(0, piece, x_ref).start()
        for piece in range(pieces):
            near(0, piece, x_ref).start()

    when_live(me, begin)
    for load in loads:
        load.start()

    def tick(t):
        def move():
            for piece in range(pieces):
                landing(t, piece).wait_recv()

                @pl.when(t + 1 < chips - 1)
                def _(piece=piece):
                    hop(t + 1, piece).start()

                near(t + 1, piece).start()

        when_live(own_origin(t + 1), move)

    def pick(t):
        parity = (t // 2) % 2

        def fetch(k, origin):
            return pltpu.make_async_copy(all_ref.at[origin], xb.at[k], x_sem.at[k])

        def fetch_own():
            @pl.when(t == 0)
            def _():
                pltpu.make_async_copy(x_ref, xb.at[0], x_sem.at[0]).start()

            @pl.when(t > 0)
            def _():
                fetch(0, own_origin(t)).start()

        def fetch_sib():
            for piece in range(pieces):
                near_landing(t, piece).wait_recv()
            fetch(1, sib_origin(t)).start()

        when_live(own_origin(t), fetch_own)
        when_live(sib_origin(t), fetch_sib)
        before = (
            lax.broadcasted_iota(jnp.int32, (rows, rows), 0)
            < lax.broadcasted_iota(jnp.int32, (rows, rows), 1)
        ).astype(jnp.bfloat16)
        slot_at = lax.broadcasted_iota(jnp.int32, (cap, rows), 0).astype(jnp.float32)
        for k, origin in ((0, own_origin(t)), (1, sib_origin(t))):
            q = 2 * (t % 2) + k
            place_of = pl.ds(pl.multiple_of(q * cap, 16), cap)

            def choose(k=k, origin=origin, q=q, place_of=place_of):
                fetch(k, origin).wait()
                info = info_ref[origin]
                slots = jnp.dot(
                    info.astype(jnp.bfloat16), before, preferred_element_type=jnp.float32
                )
                mine, weighted = [], []
                for e in range(local):
                    hit = (slot_at == slots[e : e + 1]) & (info[e : e + 1] > 0.5)
                    mine.append(jnp.where(hit, 1.0, 0.0))
                    weighted.append(jnp.where(hit, info[local + e : local + e + 1], 0.0))
                choice = jnp.concatenate(mine, axis=0).astype(jnp.bfloat16)
                chosen[parity, q] = jnp.concatenate(weighted, axis=0).astype(jnp.bfloat16)
                rows_here = jnp.dot(choice, xb[k], preferred_element_type=jnp.float32)
                rows_here = rows_here.astype(jnp.bfloat16)
                for e in range(local):
                    picked[parity, e, place_of, :] = rows_here[e * cap : (e + 1) * cap]

            when_live(origin, choose)
            if live < chips:

                @pl.when(origin // 2 >= live)
                def _(place_of=place_of):
                    for e in range(local):
                        picked[parity, e, place_of, :] = jnp.zeros((cap, depth), jnp.bfloat16)

    def expert(b, e):
        parity = b % 2
        mine = picked[parity, e]
        gate = jnp.dot(mine, wg[e], preferred_element_type=jnp.float32)
        up = jnp.dot(mine, wu[e], preferred_element_type=jnp.float32)
        act = (gate / (1.0 + jnp.exp(-gate)) * up).astype(jnp.bfloat16)
        down = jnp.dot(act, wd[e], preferred_element_type=jnp.float32)
        picked[parity, e] = down.astype(jnp.bfloat16)

    def back(b):
        parity = b % 2
        for q in range(4):
            t = 2 * b + q // 2
            origin = own_origin(t) if q % 2 == 0 else sib_origin(t)

            def put(t=t, q=q):
                rows_here = jnp.concatenate(
                    [picked[parity, e, q * cap : (q + 1) * cap, :] for e in range(local)], axis=0
                )
                total = lax.dot_general(
                    chosen[parity, q], rows_here, (((0,), (0,)), ((), ())),
                    preferred_element_type=jnp.float32,
                ).astype(jnp.bfloat16)
                if q % 2 == 0:
                    part[t] = total
                else:

                    @pl.when(t >= 2)
                    def _():
                        when_live(sib_origin(t - 2), give(t - 2).wait_send)

                    away[t % 2] = total
                    give(t).start()

            if q % 2 == 1 and live < chips:

                @pl.when((origin // 2 >= live) & (t >= 2))
                def _(t=t):
                    when_live(sib_origin(t - 2), give(t - 2).wait_send)

            when_live(origin, put)

    def scatter(t):
        slot = (t + 1) % chips

        def move():
            give(slot).wait_recv()
            for piece in range(pieces):
                here = span(piece)
                total = part[slot, here, :].astype(jnp.float32) + near_in[slot, here, :].astype(
                    jnp.float32
                )
                if not (isinstance(t, int) and t == 0):
                    pass_on(t - 1, piece).wait_recv()
                    total = total + ring_in[t - 1, here, :].astype(jnp.float32)
                if isinstance(t, int) and t == chips - 1:
                    o_ref[here, :] = total.astype(o_ref.dtype)
                else:
                    part[slot, here, :] = total.astype(part.dtype)
                    pass_on(t, piece).start()

        when_live(own_origin(slot), move)

    def unit(u, carry):
        @pl.when(u == chips - 2)
        def _():
            scatter(0)

        @pl.when(u < chips - 1)
        def _():
            tick(u)

        @pl.when(u < chips)
        def _():
            pick(u)

        @pl.when(u == 1)
        def _():
            for load in loads:
                load.wait()

        @pl.when(u >= 1)
        def _():
            expert((u - 1) // 2, (u - 1) % 2)

        @pl.when((u >= 1) & (u % 2 == 0))
        def _():
            back((u - 1) // 2)

        @pl.when(u == chips - 1)
        def _():
            scatter(1)

        @pl.when(u == chips)
        def _():
            scatter(2)

        return carry

    lax.fori_loop(0, chips + 1, unit, 0)

    def later(t, carry):
        scatter(t)
        return carry

    lax.fori_loop(3, chips - 1, later, 0)
    if live < chips:
        o_ref[...] = jnp.zeros(o_ref.shape, o_ref.dtype)
    scatter(chips - 1)

    def settle(t, carry):
        def own():
            for piece in range(pieces):
                near(t, piece).wait_send()

                @pl.when(t < chips - 1)
                def _(piece=piece):
                    hop(t, piece).wait_send()

                @pl.when(t > 0)
                def _(piece=piece):
                    pass_on(t - 1, piece).wait_send()

        def sib():
            @pl.when(t >= chips - 2)
            def _():
                give(t).wait_send()

        when_live(own_origin(t), own)
        when_live(sib_origin(t), sib)
        return carry

    lax.fori_loop(0, chips, settle, 0)


def moe(x, info, w_gate, w_up, w_down, devices, cap, live, collective_id, pieces=2):
    rows, depth = x.shape
    chips = devices // 2
    local = w_gate.shape[0]
    dma = pltpu.SemaphoreType.DMA
    both = dma((chips, pieces))
    hbm = pl.BlockSpec(memory_space=pltpu.HBM)
    vmem = pl.BlockSpec(memory_space=pltpu.VMEM)
    block = (rows, depth)
    half = jnp.bfloat16
    return pl.pallas_call(
        functools.partial(moe_kernel, devices, live, cap, pieces),
        out_shape=(
            jax.ShapeDtypeStruct(block, half),
            jax.ShapeDtypeStruct((devices,) + block, half),
        ),
        in_specs=[hbm, vmem, hbm, hbm, hbm],
        out_specs=(vmem, hbm),
        scratch_shapes=[
            pltpu.VMEM(w_gate.shape, half),
            pltpu.VMEM(w_up.shape, half),
            pltpu.VMEM(w_down.shape, half),
            pltpu.VMEM((2,) + block, half),
            pltpu.VMEM((2, local, 4 * cap, depth), half),
            pltpu.VMEM((2, 4, local * cap, rows), half),
            pltpu.VMEM((chips,) + block, half),
            pltpu.VMEM((2,) + block, half),
            pltpu.VMEM((chips,) + block, half),
            pltpu.VMEM((chips - 1,) + block, half),
            dma((3,)),
            dma((2,)),
            both, both, both, both, both, both,
            dma((chips,)),
            dma((chips,)),
        ],
        compiler_params=pltpu.CompilerParams(
            collective_id=collective_id, has_side_effects=True, vmem_limit_bytes=63 << 20
        ),
    )(x, info, w_gate, w_up, w_down)[0]


def per_device(
    hidden,
    query_rows,
    key_rows,
    value_rows,
    counts,
    out_weight,
    norm_gain,
    route_ids,
    route_weights,
    w_gate,
    w_up,
    w_down,
):
    devices = lax.axis_size("shard")
    me = lax.axis_index("shard")
    tok_dev, depth = hidden.shape
    topk = route_ids.shape[1]
    local = w_gate.shape[0]
    experts = local * devices
    capacity = max(2, tok_dev * topk * 5 // (4 * experts))
    capacity = -(-capacity // 16) * 16

    kv_width = 2 * key_rows.shape[1]
    routing = jnp.concatenate([route_ids.astype(jnp.bfloat16), route_weights], axis=1)
    routing = jnp.pad(routing, ((0, 0), (0, HD - 2 * topk)))
    both = ring_gather(jnp.concatenate([key_rows, value_rows, routing], axis=1), devices, 0)
    ids_all = both[:, :, kv_width : kv_width + topk].astype(jnp.int32)
    weights_all = both[:, :, kv_width + topk : kv_width + 2 * topk]
    live_all = jnp.arange(devices * tok_dev, dtype=jnp.int32).reshape(devices, tok_dev) < counts[0]
    info = []
    for e in range(local):
        info.append(jnp.sum((ids_all == me * local + e).astype(jnp.float32), axis=2))
    for e in range(local):
        matched = jnp.where(ids_all == me * local + e, weights_all.astype(jnp.float32), 0.0)
        info.append(jnp.where(live_all, jnp.sum(matched, axis=2), 0.0))
    info = jnp.stack(info, axis=1)
    info = jnp.pad(info, ((0, 0), (0, -info.shape[1] % 8), (0, 0)))

    both = both.reshape(devices * tok_dev, both.shape[2])
    attended, out_all = attend(
        counts, query_rows, both, out_weight, key_rows.shape[1] // HD, devices, 1
    )
    out_all = out_all.reshape(-1, depth)
    mixed_rows = hidden.astype(jnp.float32) + jnp.dot(
        attended, out_all, preferred_element_type=jnp.float32
    )
    mean_square = jnp.mean(mixed_rows * mixed_rows, axis=1, keepdims=True)
    normed = (mixed_rows * lax.rsqrt(mean_square + 1e-06) * norm_gain.astype(jnp.float32)).astype(
        jnp.bfloat16
    )
    summed = moe(normed, info, w_gate, w_up, w_down, devices, capacity, devices // 2, 2)
    return (mixed_rows + summed.astype(jnp.float32)).astype(jnp.bfloat16)


def solution(mesh):
    rows = P(("groups", "shard"), None)
    weights = P("shard", None, None)
    return jax.shard_map(
        per_device,
        mesh=mesh,
        in_specs=(
            rows,
            rows,
            rows,
            rows,
            P("groups"),
            P("shard", None),
            P(),
            rows,
            rows,
            weights,
            weights,
            weights,
        ),
        out_specs=rows,
        check_vma=False,
    )
```

```python
import functools
import math

import jax
import jax.numpy as jnp
from jax import lax
from jax.experimental import pallas as pl
from jax.experimental.pallas import tpu as pltpu
from jax.sharding import PartitionSpec as P

HD = 128
SEQ_LEN = 4096
NEG = -1e30
MESH = pl.DeviceIdType.MESH


def ring_place(chips, index):
    if chips == 8:
        z, y = index // 2, index % 2
        return z + y * (7 - 2 * z)
    return index


def ring_chip(chips, place):
    if chips == 8:
        half = place // 4
        z = place + half * (7 - 2 * place)
        return 2 * z + half
    return place


def gather_moves(devices, pieces, x_ref, o_ref, local_sem, near_send, near_recv, send, recv, tell=False):
    chips = devices // 2
    me = lax.axis_index("shard")
    group = lax.axis_index("groups")
    core = me % 2
    place = ring_place(chips, me // 2)

    def device_at(offset):
        return ring_chip(chips, (place + offset + 2 * chips) % chips) * 2 + core

    right, left, sibling = device_at(1), device_at(-1), me + 1 - 2 * core
    rows = x_ref.shape[0] // (2 * pieces)

    def part(ref, way, piece):
        return ref.at[pl.ds((way * pieces + piece) * rows, rows)]

    def hop(step, way, piece):
        origin = device_at(-step if way == 0 else step)
        src = part(x_ref if step == 0 else o_ref.at[origin], way, piece)
        return pltpu.make_async_remote_copy(
            src_ref=src,
            dst_ref=part(o_ref.at[origin], way, piece),
            send_sem=send.at[step, way, piece],
            recv_sem=recv.at[step, way, piece],
            device_id=(group, right if way == 0 else left),
            device_id_type=MESH,
        )

    def landing(step, way, piece):
        origin = device_at(-step - 1 if way == 0 else step + 1)
        place_of = part(o_ref.at[origin], way, piece)
        return pltpu.make_async_remote_copy(
            src_ref=place_of,
            dst_ref=place_of,
            send_sem=send.at[step, way, piece],
            recv_sem=recv.at[step, way, piece],
            device_id=(group, right if way == 0 else left),
            device_id_type=MESH,
        )

    def near(step, way, piece):
        if step < 0:
            src, origin = part(x_ref, way, piece), me
        else:
            origin = device_at(-step - 1 if way == 0 else step + 1)
            src = part(o_ref.at[origin], way, piece)
        return pltpu.make_async_remote_copy(
            src_ref=src,
            dst_ref=part(o_ref.at[origin], way, piece),
            send_sem=near_send.at[step + 1, way, piece],
            recv_sem=near_recv.at[step + 1, way, piece],
            device_id=(group, sibling),
            device_id_type=MESH,
        )

    def near_landing(step, way, piece):
        if step < 0:
            origin = sibling
        else:
            origin = device_at(-step - 1 if way == 0 else step + 1) + 1 - 2 * core
        place_of = part(o_ref.at[origin], way, piece)
        return pltpu.make_async_remote_copy(
            src_ref=place_of,
            dst_ref=place_of,
            send_sem=near_send.at[step + 1, way, piece],
            recv_sem=near_recv.at[step + 1, way, piece],
            device_id=(group, sibling),
            device_id_type=MESH,
        )

    every = [(way, piece) for piece in range(pieces) for way in range(2)]
    own = pltpu.make_async_copy(x_ref, o_ref.at[me], local_sem)

    def begin():
        barrier = pltpu.get_barrier_semaphore()
        for other in (right, left, sibling):
            pl.semaphore_signal(barrier, inc=1, device_id=(group, other), device_id_type=MESH)
        groups = lax.axis_size("groups") if tell else 1
        for other in range(1, groups):
            to = (group + other) % groups
            pl.semaphore_signal(barrier, inc=1, device_id=(to, me), device_id_type=MESH)
        pl.semaphore_wait(barrier, 2 + groups)
        for way, piece in every:
            hop(0, way, piece).start()
        own.start()
        for way, piece in every:
            near(-1, way, piece).start()

    def stage(step):
        for way, piece in every:
            landing(step, way, piece).wait_recv()
            if step + 1 < chips - 1:
                hop(step + 1, way, piece).start()
            near(step, way, piece).start()

    def finish():
        own.wait()
        for step in range(chips - 1):
            for way, piece in every:
                hop(step, way, piece).wait_send()
        for step in range(-1, chips - 1):
            for way, piece in every:
                near(step, way, piece).wait_send()
                near_landing(step, way, piece).wait_recv()

    return begin, stage, finish


def gather_kernel(devices, pieces, x_ref, count_ref, o_ref, counts_ref, c_send, c_recv, *sems):
    begin, stage, finish = gather_moves(devices, pieces, x_ref, o_ref, *sems, tell=True)
    me = lax.axis_index("shard")
    group = lax.axis_index("groups")
    groups = counts_ref.shape[0]
    begin()
    tells = []
    for other in range(1, groups):
        to = (group + other) % groups
        tells.append(
            pltpu.make_async_remote_copy(
                src_ref=count_ref,
                dst_ref=counts_ref.at[other],
                send_sem=c_send.at[other],
                recv_sem=c_recv.at[other],
                device_id=(to, me),
                device_id_type=MESH,
            )
        )
    for copy in tells:
        copy.start()
    counts_ref[0] = count_ref[...]
    for step in range(devices // 2 - 1):
        stage(step)
    finish()
    for copy in tells:
        copy.wait()


def gather_scratch(devices, pieces):
    dma = pltpu.SemaphoreType.DMA
    return [dma] + [dma((devices // 2, 2, pieces))] * 4


def ring_gather(x, count, devices, collective_id, pieces=2):
    groups = lax.axis_size("groups")
    dma = pltpu.SemaphoreType.DMA
    hbm = pl.BlockSpec(memory_space=pltpu.HBM)
    vmem = pl.BlockSpec(memory_space=pltpu.VMEM)
    return pl.pallas_call(
        functools.partial(gather_kernel, devices, pieces),
        out_shape=(
            jax.ShapeDtypeStruct((devices,) + x.shape, x.dtype),
            jax.ShapeDtypeStruct((groups,) + count.shape, count.dtype),
        ),
        in_specs=[hbm, vmem],
        out_specs=(hbm, vmem),
        scratch_shapes=[dma((groups,)), dma((groups,))] + gather_scratch(devices, pieces),
        compiler_params=pltpu.CompilerParams(collective_id=collective_id, has_side_effects=True),
    )(x, count)


def attend_kernel(
    devices, pieces, step_rows, heads, groups,
    count_ref, q_ref, k_ref, v_ref, w_ref, o_ref, all_ref, qs, top, total, *sems
):
    begin, stage, finish = gather_moves(devices, pieces, w_ref, all_ref, *sems)
    rows = q_ref.shape[0]
    scale = math.log2(math.e) / math.sqrt(HD)
    count = count_ref[0]
    first = lax.axis_index("shard") * rows
    blocks = (first + rows + step_rows - 1) // step_rows
    j = pl.program_id(1)
    steps = k_ref.shape[0] // step_rows
    at_step = pl.program_id(0) * steps + j
    all_steps = groups * steps

    @pl.when(at_step == 0)
    def _():
        begin()

    @pl.when(j == 0)
    def _():
        for h in range(heads):
            qs[h * rows : (h + 1) * rows, :] = q_ref[:, h * HD : (h + 1) * HD]
        top[...] = jnp.full(top.shape, NEG, jnp.float32)
        total[...] = jnp.zeros(total.shape, jnp.float32)

    def fold(masked):
        start = pl.multiple_of(j * step_rows, step_rows)
        keys = k_ref[pl.ds(start, step_rows), :]
        ones = jnp.ones((step_rows, HD), jnp.bfloat16)
        values = jnp.concatenate([v_ref[pl.ds(start, step_rows), :], ones], axis=1)
        if masked:
            at_row = first + lax.broadcasted_iota(jnp.int32, (rows, step_rows), 0)
            at_col = start + lax.broadcasted_iota(jnp.int32, (rows, step_rows), 1)
            visible = (at_col <= at_row) & (at_col < count)
        for h in range(heads):
            span = slice(h * rows, (h + 1) * rows)
            scores = lax.dot_general(
                qs[span, :], keys, (((1,), (1,)), ((), ())), preferred_element_type=jnp.float32
            )
            if masked:
                scores = jnp.where(visible, scores, NEG)
            old = top[span, :]
            new = jnp.maximum(old, jnp.max(scores, axis=1, keepdims=True) * scale)
            expo = jnp.exp2(scores * scale - new[:, :1]).astype(jnp.bfloat16)
            factor = jnp.exp2(old - new)
            part = jnp.dot(expo, values, preferred_element_type=jnp.float32)
            total[span, :] = total[span, :] * jnp.concatenate([factor, factor], axis=1) + part
            top[span, :] = new

    @pl.when(j < blocks - 1)
    def _():
        fold(False)

    @pl.when(j == blocks - 1)
    def _():
        fold(True)

        live = first + lax.broadcasted_iota(jnp.int32, (rows, HD), 0) < count
        for h in range(heads):
            both = total[h * rows : (h + 1) * rows, :]
            result = jnp.where(live, both[:, :HD] / jnp.where(live, both[:, HD:], 1.0), 0.0)
            o_ref[:, h * HD : (h + 1) * HD] = result.astype(jnp.bfloat16)

    stages = devices // 2 - 1
    for number in range(stages):

        @pl.when(at_step == (number + 1) * all_steps // stages - 1)
        def _(number=number):
            stage(number)

    @pl.when(at_step == all_steps - 1)
    def _():
        finish()


def attend(count, queries, keys_values, out_weight, kv_count, devices, collective_id, pieces=2):
    rows, width = queries.shape
    length = keys_values.shape[0]
    heads = width // HD // kv_count
    step_rows = math.gcd(length, 512)
    hbm = pl.BlockSpec(memory_space=pltpu.HBM)
    return pl.pallas_call(
        functools.partial(attend_kernel, devices, pieces, step_rows, heads, kv_count),
        grid=(kv_count, length // step_rows),
        out_shape=(
            jax.ShapeDtypeStruct((rows, width), jnp.bfloat16),
            jax.ShapeDtypeStruct((devices,) + out_weight.shape, jnp.bfloat16),
        ),
        in_specs=[
            pl.BlockSpec(memory_space=pltpu.SMEM),
            pl.BlockSpec((rows, heads * HD), lambda g, j: (0, g)),
            pl.BlockSpec((length, HD), lambda g, j: (0, g)),
            pl.BlockSpec((length, HD), lambda g, j: (0, kv_count + g)),
            hbm,
        ],
        out_specs=(pl.BlockSpec((rows, heads * HD), lambda g, j: (0, g)), hbm),
        scratch_shapes=[
            pltpu.VMEM((heads * rows, HD), jnp.bfloat16),
            pltpu.VMEM((heads * rows, HD), jnp.float32),
            pltpu.VMEM((heads * rows, 2 * HD), jnp.float32),
        ]
        + gather_scratch(devices, pieces),
        compiler_params=pltpu.CompilerParams(
            collective_id=collective_id, has_side_effects=True, vmem_limit_bytes=40 << 20
        ),
    )(count, queries, keys_values, keys_values, out_weight)


def moe_kernel(
    devices, live, cap, pieces,
    x_ref, info_ref, wg_ref, wu_ref, wd_ref, o_ref, all_ref,
    wg, wu, wd, xb, picked, chosen, part, away, near_in, ring_in,
    w_sem, x_sem, g_send, g_recv, n_send, n_recv, s_send, s_recv, a_send, a_recv,
):
    chips = devices // 2
    me = lax.axis_index("shard")
    group = lax.axis_index("groups")
    core = me % 2
    way = 1 - 2 * core
    place = ring_place(chips, me // 2)
    rows, depth = x_ref.shape
    local = wg.shape[0]

    def chip_at(offset):
        return ring_chip(chips, (place + offset + 2 * chips) % chips)

    def own_origin(t):
        return chip_at(-way * t) * 2 + core

    def sib_origin(t):
        return chip_at(way * t) * 2 + 1 - core

    def when_live(origin, action):
        if live == chips:
            action()
        else:
            pl.when(origin // 2 < live)(action)

    ahead, behind, sibling = own_origin(-1), own_origin(1), me + way

    def span(piece):
        size = rows // pieces
        return pl.ds(piece * size, size)

    def remote(src, dst, send, recv, to):
        return pltpu.make_async_remote_copy(
            src_ref=src, dst_ref=dst, send_sem=send, recv_sem=recv,
            device_id=(group, to), device_id_type=MESH,
        )

    def hop(t, piece, src=None):
        place_of = all_ref.at[own_origin(t), span(piece)]
        src = place_of if src is None else src.at[span(piece)]
        return remote(src, place_of, g_send.at[t, piece], g_recv.at[t, piece], ahead)

    def near(t, piece, src=None):
        place_of = all_ref.at[own_origin(t), span(piece)]
        src = place_of if src is None else src.at[span(piece)]
        return remote(src, place_of, n_send.at[t, piece], n_recv.at[t, piece], sibling)

    def near_landing(t, piece):
        place_of = all_ref.at[sib_origin(t), span(piece)]
        return remote(place_of, place_of, n_send.at[t, piece], n_recv.at[t, piece], sibling)

    def landing(t, piece):
        place_of = all_ref.at[own_origin(t + 1), span(piece)]
        return remote(place_of, place_of, g_send.at[t, piece], g_recv.at[t, piece], ahead)

    def give(t):
        return remote(away.at[t % 2], near_in.at[t], a_send.at[t], a_recv.at[t], sibling)

    def pass_on(t, piece):
        return remote(
            part.at[t + 1, span(piece)], ring_in.at[t, span(piece)],
            s_send.at[t, piece], s_recv.at[t, piece], ahead,
        )

    loads = [
        pltpu.make_async_copy(src, dst, w_sem.at[i])
        for i, (src, dst) in enumerate(((wg_ref, wg), (wu_ref, wu), (wd_ref, wd)))
    ]

    barrier = pltpu.get_barrier_semaphore()
    for other in (ahead, behind, sibling):
        pl.semaphore_signal(barrier, inc=1, device_id=(group, other), device_id_type=MESH)
    pl.semaphore_wait(barrier, 3)

    def begin():
        for piece in range(pieces):
            hop(0, piece, x_ref).start()
        for piece in range(pieces):
            near(0, piece, x_ref).start()

    when_live(me, begin)
    for load in loads:
        load.start()

    def tick(t):
        def move():
            for piece in range(pieces):
                landing(t, piece).wait_recv()

                @pl.when(t + 1 < chips - 1)
                def _(piece=piece):
                    hop(t + 1, piece).start()

                near(t + 1, piece).start()

        when_live(own_origin(t + 1), move)

    def pick(t):
        parity = (t // 2) % 2

        def fetch(k, origin):
            return pltpu.make_async_copy(all_ref.at[origin], xb.at[k], x_sem.at[k])

        def fetch_own():
            @pl.when(t == 0)
            def _():
                pltpu.make_async_copy(x_ref, xb.at[0], x_sem.at[0]).start()

            @pl.when(t > 0)
            def _():
                fetch(0, own_origin(t)).start()

        def fetch_sib():
            for piece in range(pieces):
                near_landing(t, piece).wait_recv()
            fetch(1, sib_origin(t)).start()

        when_live(own_origin(t), fetch_own)
        when_live(sib_origin(t), fetch_sib)
        before = (
            lax.broadcasted_iota(jnp.int32, (rows, rows), 0)
            < lax.broadcasted_iota(jnp.int32, (rows, rows), 1)
        ).astype(jnp.bfloat16)
        slot_at = lax.broadcasted_iota(jnp.int32, (cap, rows), 0).astype(jnp.float32)
        for k, origin in ((0, own_origin(t)), (1, sib_origin(t))):
            q = 2 * (t % 2) + k
            place_of = pl.ds(pl.multiple_of(q * cap, 16), cap)

            def choose(k=k, origin=origin, q=q, place_of=place_of):
                fetch(k, origin).wait()
                info = info_ref[origin]
                slots = jnp.dot(
                    info.astype(jnp.bfloat16), before, preferred_element_type=jnp.float32
                )
                mine, weighted = [], []
                for e in range(local):
                    hit = (slot_at == slots[e : e + 1]) & (info[e : e + 1] > 0.5)
                    mine.append(jnp.where(hit, 1.0, 0.0))
                    weighted.append(jnp.where(hit, info[local + e : local + e + 1], 0.0))
                choice = jnp.concatenate(mine, axis=0).astype(jnp.bfloat16)
                chosen[parity, q] = jnp.concatenate(weighted, axis=0).astype(jnp.bfloat16)
                rows_here = jnp.dot(choice, xb[k], preferred_element_type=jnp.float32)
                rows_here = rows_here.astype(jnp.bfloat16)
                for e in range(local):
                    picked[parity, e, place_of, :] = rows_here[e * cap : (e + 1) * cap]

            when_live(origin, choose)
            if live < chips:

                @pl.when(origin // 2 >= live)
                def _(place_of=place_of):
                    for e in range(local):
                        picked[parity, e, place_of, :] = jnp.zeros((cap, depth), jnp.bfloat16)

    def expert(b, e):
        parity = b % 2
        mine = picked[parity, e]
        gate = jnp.dot(mine, wg[e], preferred_element_type=jnp.float32)
        up = jnp.dot(mine, wu[e], preferred_element_type=jnp.float32)
        act = (gate / (1.0 + jnp.exp(-gate)) * up).astype(jnp.bfloat16)
        down = jnp.dot(act, wd[e], preferred_element_type=jnp.float32)
        picked[parity, e] = down.astype(jnp.bfloat16)

    def back(b):
        parity = b % 2
        for q in range(4):
            t = 2 * b + q // 2
            origin = own_origin(t) if q % 2 == 0 else sib_origin(t)

            def put(t=t, q=q):
                rows_here = jnp.concatenate(
                    [picked[parity, e, q * cap : (q + 1) * cap, :] for e in range(local)], axis=0
                )
                total = lax.dot_general(
                    chosen[parity, q], rows_here, (((0,), (0,)), ((), ())),
                    preferred_element_type=jnp.float32,
                ).astype(jnp.bfloat16)
                if q % 2 == 0:
                    part[t] = total
                else:

                    @pl.when(t >= 2)
                    def _():
                        when_live(sib_origin(t - 2), give(t - 2).wait_send)

                    away[t % 2] = total
                    give(t).start()

            if q % 2 == 1 and live < chips:

                @pl.when((origin // 2 >= live) & (t >= 2))
                def _(t=t):
                    when_live(sib_origin(t - 2), give(t - 2).wait_send)

            when_live(origin, put)

    def scatter(t):
        slot = (t + 1) % chips

        def move():
            give(slot).wait_recv()
            for piece in range(pieces):
                here = span(piece)
                total = part[slot, here, :].astype(jnp.float32) + near_in[slot, here, :].astype(
                    jnp.float32
                )
                if not (isinstance(t, int) and t == 0):
                    pass_on(t - 1, piece).wait_recv()
                    total = total + ring_in[t - 1, here, :].astype(jnp.float32)
                if isinstance(t, int) and t == chips - 1:
                    o_ref[here, :] = total.astype(o_ref.dtype)
                else:
                    part[slot, here, :] = total.astype(part.dtype)
                    pass_on(t, piece).start()

        when_live(own_origin(slot), move)

    def unit(u, carry):
        @pl.when(u == chips - 2)
        def _():
            scatter(0)

        @pl.when(u < chips - 1)
        def _():
            tick(u)

        @pl.when(u < chips)
        def _():
            pick(u)

        @pl.when(u == 1)
        def _():
            for load in loads:
                load.wait()

        @pl.when(u >= 1)
        def _():
            expert((u - 1) // 2, (u - 1) % 2)

        @pl.when((u >= 1) & (u % 2 == 0))
        def _():
            back((u - 1) // 2)

        @pl.when(u == chips - 1)
        def _():
            scatter(1)

        @pl.when(u == chips)
        def _():
            scatter(2)

        return carry

    lax.fori_loop(0, chips + 1, unit, 0)

    def later(t, carry):
        scatter(t)
        return carry

    lax.fori_loop(3, chips - 1, later, 0)
    if live < chips:
        o_ref[...] = jnp.zeros(o_ref.shape, o_ref.dtype)
    scatter(chips - 1)

    def settle(t, carry):
        def own():
            for piece in range(pieces):
                near(t, piece).wait_send()

                @pl.when(t < chips - 1)
                def _(piece=piece):
                    hop(t, piece).wait_send()

                @pl.when(t > 0)
                def _(piece=piece):
                    pass_on(t - 1, piece).wait_send()

        def sib():
            @pl.when(t >= chips - 2)
            def _():
                give(t).wait_send()

        when_live(own_origin(t), own)
        when_live(sib_origin(t), sib)
        return carry

    lax.fori_loop(0, chips, settle, 0)


def moe(x, info, w_gate, w_up, w_down, devices, cap, live, collective_id, pieces=2):
    rows, depth = x.shape
    chips = devices // 2
    local = w_gate.shape[0]
    dma = pltpu.SemaphoreType.DMA
    both = dma((chips, pieces))
    hbm = pl.BlockSpec(memory_space=pltpu.HBM)
    vmem = pl.BlockSpec(memory_space=pltpu.VMEM)
    block = (rows, depth)
    half = jnp.bfloat16
    return pl.pallas_call(
        functools.partial(moe_kernel, devices, live, cap, pieces),
        out_shape=(
            jax.ShapeDtypeStruct(block, half),
            jax.ShapeDtypeStruct((devices,) + block, half),
        ),
        in_specs=[hbm, vmem, hbm, hbm, hbm],
        out_specs=(vmem, hbm),
        scratch_shapes=[
            pltpu.VMEM(w_gate.shape, half),
            pltpu.VMEM(w_up.shape, half),
            pltpu.VMEM(w_down.shape, half),
            pltpu.VMEM((2,) + block, half),
            pltpu.VMEM((2, local, 4 * cap, depth), half),
            pltpu.VMEM((2, 4, local * cap, rows), half),
            pltpu.VMEM((chips,) + block, half),
            pltpu.VMEM((2,) + block, half),
            pltpu.VMEM((chips,) + block, half),
            pltpu.VMEM((chips - 1,) + block, half),
            dma((3,)),
            dma((2,)),
            both, both, both, both, both, both,
            dma((chips,)),
            dma((chips,)),
        ],
        compiler_params=pltpu.CompilerParams(
            collective_id=collective_id, has_side_effects=True, vmem_limit_bytes=63 << 20
        ),
    )(x, info, w_gate, w_up, w_down)[0]


def per_device(
    hidden,
    query_rows,
    key_rows,
    value_rows,
    counts,
    out_weight,
    norm_gain,
    route_ids,
    route_weights,
    w_gate,
    w_up,
    w_down,
):
    devices = lax.axis_size("shard")
    me = lax.axis_index("shard")
    tok_dev, depth = hidden.shape
    topk = route_ids.shape[1]
    local = w_gate.shape[0]
    experts = local * devices
    capacity = max(2, tok_dev * topk * 5 // (4 * experts))
    capacity = -(-capacity // 16) * 16

    kv_width = 2 * key_rows.shape[1]
    routing = jnp.concatenate([route_ids.astype(jnp.bfloat16), route_weights], axis=1)
    routing = jnp.pad(routing, ((0, 0), (0, HD - 2 * topk)))
    both, counts_all = ring_gather(
        jnp.concatenate([key_rows, value_rows, routing], axis=1),
        jnp.broadcast_to(counts[None, :], (8, HD)),
        devices,
        0,
    )
    ids_all = both[:, :, kv_width : kv_width + topk].astype(jnp.int32)
    weights_all = both[:, :, kv_width + topk : kv_width + 2 * topk]
    live_all = jnp.arange(devices * tok_dev, dtype=jnp.int32).reshape(devices, tok_dev) < counts[0]
    info = []
    for e in range(local):
        info.append(jnp.sum((ids_all == me * local + e).astype(jnp.float32), axis=2))
    for e in range(local):
        matched = jnp.where(ids_all == me * local + e, weights_all.astype(jnp.float32), 0.0)
        info.append(jnp.where(live_all, jnp.sum(matched, axis=2), 0.0))
    info = jnp.stack(info, axis=1)
    info = jnp.pad(info, ((0, 0), (0, -info.shape[1] % 8), (0, 0)))

    both = both.reshape(devices * tok_dev, both.shape[2])
    attended, out_all = attend(
        counts, query_rows, both, out_weight, key_rows.shape[1] // HD, devices, 1
    )
    out_all = out_all.reshape(-1, depth)
    mixed_rows = hidden.astype(jnp.float32) + jnp.dot(
        attended, out_all, preferred_element_type=jnp.float32
    )
    mean_square = jnp.mean(mixed_rows * mixed_rows, axis=1, keepdims=True)
    normed = (mixed_rows * lax.rsqrt(mean_square + 1e-06) * norm_gain.astype(jnp.float32)).astype(
        jnp.bfloat16
    )
    chips = devices // 2
    variants = [chips * part // 8 for part in (5, 6, 7, 8)]
    live = (jnp.max(counts_all) + 2 * tok_dev - 1) // (2 * tok_dev)
    chosen = sum((live > most).astype(jnp.int32) for most in variants[:-1])

    def branch(number):
        def run(*operands):
            return moe(*operands, devices, capacity, variants[number], 2 + number)

        return run

    summed = lax.switch(
        chosen, [branch(i) for i in range(len(variants))], normed, info, w_gate, w_up, w_down
    )
    return (mixed_rows + summed.astype(jnp.float32)).astype(jnp.bfloat16)


def solution(mesh):
    rows = P(("groups", "shard"), None)
    weights = P("shard", None, None)
    return jax.shard_map(
        per_device,
        mesh=mesh,
        in_specs=(
            rows,
            rows,
            rows,
            rows,
            P("groups"),
            P("shard", None),
            P(),
            rows,
            rows,
            weights,
            weights,
            weights,
        ),
        out_specs=rows,
        check_vma=False,
    )
```

```python
import functools
import math

import jax
import jax.numpy as jnp
from jax import lax
from jax.experimental import pallas as pl
from jax.experimental.pallas import tpu as pltpu
from jax.sharding import PartitionSpec as P

HD = 128
SEQ_LEN = 4096
NEG = -1e30
MESH = pl.DeviceIdType.MESH


def ring_place(chips, index):
    if chips == 8:
        z, y = index // 2, index % 2
        return z + y * (7 - 2 * z)
    return index


def ring_chip(chips, place):
    if chips == 8:
        half = place // 4
        z = place + half * (7 - 2 * place)
        return 2 * z + half
    return place


def front_kernel(
    devices, kv_count, heads,
    count_ref, q_ref, k_ref, v_ref, r_ref, w_ref, hidden_ref, gain_ref,
    normed_ref, mixed_ref, allr,
    allk, allv, allw, top, total, att,
    own_sem, kv_send, kv_recv, kn_send, kn_recv,
    w_send, w_recv, n_send, n_recv, x_send, x_recv, m_send, m_recv,
):
    chips = devices // 2
    me = lax.axis_index("shard")
    group = lax.axis_index("groups")
    core = me % 2
    way = 1 - 2 * core
    place = ring_place(chips, me // 2)
    rows = q_ref.shape[0]
    depth = w_ref.shape[1]
    scale = math.log2(math.e) / math.sqrt(HD)
    half_rows = w_ref.shape[0] // 2
    side = group % 2
    partner = group + 1 - 2 * side

    def chip_at(offset):
        return ring_chip(chips, (place + offset + 2 * chips) % chips)

    def own_origin(t):
        return chip_at(-way * t) * 2 + core

    def sib_origin(t):
        return chip_at(way * t) * 2 + 1 - core

    ahead, behind, sibling = own_origin(-1), own_origin(1), me + way
    mine, theirs = pl.ds(side * half_rows, half_rows), pl.ds((1 - side) * half_rows, half_rows)
    small = ((k_ref, allk), (v_ref, allv), (r_ref, allr))

    def remote(src, dst, send, recv, to, to_group=None):
        return pltpu.make_async_remote_copy(
            src_ref=src, dst_ref=dst, send_sem=send, recv_sem=recv,
            device_id=(group if to_group is None else to_group, to), device_id_type=MESH,
        )

    def kv_hop(t, i, src=None):
        at = small[i][1].at[own_origin(t)]
        return remote(at if src is None else src, at, kv_send.at[t, i], kv_recv.at[t, i], ahead)

    def kv_landing(t, i):
        at = small[i][1].at[own_origin(t)]
        return remote(at, at, kv_send.at[t - 1, i], kv_recv.at[t - 1, i], ahead)

    def kv_near(t, i, src=None):
        at = small[i][1].at[own_origin(t)]
        return remote(at if src is None else src, at, kn_send.at[t, i], kn_recv.at[t, i], sibling)

    def kv_near_landing(t, i):
        at = small[i][1].at[sib_origin(t)]
        return remote(at, at, kn_send.at[t, i], kn_recv.at[t, i], sibling)

    def w_hop(t, src=None):
        at = allw.at[own_origin(t), mine]
        src = at if src is None else src.at[mine]
        return remote(src, at, w_send.at[t], w_recv.at[t], ahead)

    def w_landing(t):
        at = allw.at[own_origin(t), mine]
        return remote(at, at, w_send.at[t - 1], w_recv.at[t - 1], ahead)

    def w_near(t):
        at = allw.at[own_origin(t), mine]
        return remote(at, at, n_send.at[t], n_recv.at[t], sibling)

    def w_near_landing(t):
        at = allw.at[sib_origin(t), mine]
        return remote(at, at, n_send.at[t], n_recv.at[t], sibling)

    def w_near_all(origin, src):
        return remote(src, allw.at[origin], n_send.at[0], n_recv.at[0], sibling)

    def cross(t):
        at = allw.at[own_origin(t), mine]
        return remote(at, at, x_send.at[t], x_recv.at[t], me, partner)

    def cross_landing(t):
        at = allw.at[own_origin(t), theirs]
        return remote(at, at, x_send.at[t], x_recv.at[t], me, partner)

    def cross_near(t):
        at = allw.at[own_origin(t), theirs]
        return remote(at, at, m_send.at[t], m_recv.at[t], sibling)

    def cross_near_landing(t):
        at = allw.at[sib_origin(t), theirs]
        return remote(at, at, m_send.at[t], m_recv.at[t], sibling)

    own = [
        pltpu.make_async_copy(src, dst.at[me], own_sem.at[i])
        for i, (src, dst) in enumerate(small + ((w_ref, allw),))
    ]

    barrier = pltpu.get_barrier_semaphore()
    for other in (ahead, behind, sibling):
        pl.semaphore_signal(barrier, inc=1, device_id=(group, other), device_id_type=MESH)
    pl.semaphore_signal(barrier, inc=1, device_id=(partner, me), device_id_type=MESH)
    pl.semaphore_wait(barrier, 4)

    for i in range(3):
        kv_hop(0, i, small[i][0]).start()
    for i in range(3):
        kv_near(0, i, small[i][0]).start()
    for copy in own:
        copy.start()
    w_near_all(me, w_ref).start()

    def kv_tick(t):
        for i in range(3):
            kv_landing(t, i).wait_recv()

            @pl.when(t < chips - 1)
            def _(i=i):
                kv_hop(t, i).start()

            kv_near(t, i).start()

    def w_tick(t):
        w_landing(t).wait_recv()

        @pl.when(t < chips - 1)
        def _():
            w_hop(t).start()

        cross(t).start()
        w_near(t).start()

        @pl.when(t > 1)
        def _():
            cross_tick(t - 1)

    def cross_tick(t):
        cross_landing(t).wait_recv()
        cross_near(t).start()

    apart = lax.broadcasted_iota(jnp.int32, (rows, rows), 1) - lax.broadcasted_iota(
        jnp.int32, (rows, rows), 0
    )
    cut = 2
    part_heads = heads // cut
    per_set = kv_count * cut

    def fold(n, g, part, first, masked):
        origins = []
        for t in (2 * n, 2 * n + 1):
            origins += [own_origin(t), sib_origin(t)]
        lanes = pl.ds(pl.multiple_of(g * HD, HD), HD)
        keys = jnp.concatenate([allk[o, :, lanes] for o in origins], axis=0)
        values = jnp.concatenate([allv[o, :, lanes] for o in origins], axis=0)
        values = jnp.concatenate([values, jnp.ones(values.shape, jnp.bfloat16)], axis=1)
        width = part_heads * HD
        q_here = q_ref[:, pl.ds(pl.multiple_of((g * cut + part) * width, width), width)]

        def scores_of(h):
            scores = lax.dot_general(
                q_here[:, h * HD : (h + 1) * HD], keys, (((1,), (1,)), ((), ())),
                preferred_element_type=jnp.float32,
            )
            if not masked:
                return scores
            return jnp.concatenate(
                [
                    jnp.where(apart <= (me - o) * rows, scores[:, j * rows : (j + 1) * rows], NEG)
                    for j, o in enumerate(origins)
                ],
                axis=1,
            )

        later = scores_of(0)
        for h in range(part_heads):
            at = (g * cut + part) * part_heads + h
            scores = later
            if h + 1 < part_heads:
                later = scores_of(h + 1)
            new = jnp.max(scores, axis=1, keepdims=True) * scale
            if first:
                new = jnp.broadcast_to(new, (rows, HD))
            else:
                old = top[at]
                new = jnp.maximum(old, new)
            expo = jnp.exp2(scores * scale - new[:, :1]).astype(jnp.bfloat16)
            both = jnp.dot(expo, values, preferred_element_type=jnp.float32)
            if not first:
                factor = jnp.exp2(old - new)
                both = total[at] * jnp.concatenate([factor, factor], axis=1) + both
            total[at] = both
            top[at] = new

    w_first = 3 * (chips - 2) + 2
    segments = chips // 2 * per_set

    kv_tick(1)
    for copy in own:
        copy.wait()

    def segment(i, carry):
        n = i // per_set
        g = (i % per_set) // cut
        part = i % cut

        @pl.when((i > 0) & (i % 3 == 0) & (i <= 3 * (chips - 2)))
        def _():
            kv_tick(i // 3 + 1)

        @pl.when(i == w_first - 3)
        def _():
            w_hop(0, w_ref).start()

        @pl.when((i >= w_first) & ((i - w_first) % 3 == 0))
        def _():
            w_tick((i - w_first) // 3 + 1)

        @pl.when(i % per_set == 0)
        def _():
            for t in (2 * n, 2 * n + 1):
                for k in range(3):
                    kv_near_landing(t, k).wait_recv()

        some, every = False, True
        for t in (2 * n, 2 * n + 1):
            for o in (own_origin(t), sib_origin(t)):
                some = (o <= me) | some
                every = (o < me) & every

        @pl.when(n == 0)
        def _():
            fold(n, g, part, True, True)

        @pl.when((n > 0) & every)
        def _():
            fold(n, g, part, False, False)

        @pl.when((n > 0) & some & jnp.logical_not(every))
        def _():
            fold(n, g, part, False, True)

        return carry

    lax.fori_loop(0, segments, segment, 0)

    alive = me * rows + lax.broadcasted_iota(jnp.int32, (rows, HD), 0) < count_ref[0]

    def close(at, carry):
        both = total[at]
        result = jnp.where(alive, both[:, :HD] / jnp.where(alive, both[:, HD:], 1.0), 0.0)
        att[:, pl.ds(pl.multiple_of(at * HD, HD), HD)] = result.astype(jnp.bfloat16)
        return carry

    w_next = -(-(segments - w_first) // 3) + 1
    sets = chips // 2
    tile = 256
    deep = w_ref.shape[0]

    def project(b):
        for t in (2 * b, 2 * b + 1):

            @pl.when(t == 0)
            def _():
                w_near_all(sibling, allw.at[sibling]).wait_recv()

            @pl.when(t > 0)
            def _(t=t):
                w_near_landing(t).wait_recv()
                cross_near_landing(t).wait_recv()

        origins = []
        for t in (2 * b, 2 * b + 1):
            origins += [own_origin(t), sib_origin(t)]
        left = jnp.concatenate(
            [att[:, pl.ds(pl.multiple_of(o * deep, deep), deep)] for o in origins], axis=1
        )

        def column(c, carry):
            lanes = pl.ds(pl.multiple_of(c * tile, tile), tile)
            right = jnp.concatenate([allw[o, :, lanes] for o in origins], axis=0)
            mixed_ref[:, lanes] += jnp.dot(left, right, preferred_element_type=jnp.float32)
            return carry

        lax.fori_loop(0, depth // tile, column, 0)

    lax.fori_loop(0, kv_count * heads, close, 0)
    mixed_ref[...] = hidden_ref[...].astype(jnp.float32)

    def tail(b, carry):
        @pl.when(w_next + b <= chips - 1)
        def _():
            w_tick(w_next + b)

        @pl.when(b == sets - 1)
        def _():
            cross_tick(chips - 1)

        project(b)
        return carry

    lax.fori_loop(0, sets, tail, 0)

    step = 32
    gain = gain_ref[...].astype(jnp.float32)

    def norm(c, carry):
        here = pl.ds(pl.multiple_of(c * step, step), step)
        mixed = mixed_ref[here, :]
        mean_square = jnp.mean(mixed * mixed, axis=1, keepdims=True)
        normed_ref[here, :] = (mixed * lax.rsqrt(mean_square + 1e-06) * gain).astype(jnp.bfloat16)
        return carry

    lax.fori_loop(0, rows // step, norm, 0)

    w_near_all(sibling, w_ref).wait_send()
    w_hop(0, w_ref).wait_send()
    for i in range(3):
        kv_hop(0, i).wait_send()
        kv_near(0, i).wait_send()

    def settle(t, carry):
        for i in range(3):
            kv_near(t, i).wait_send()
        cross(t).wait_send()
        w_near(t).wait_send()
        cross_near(t).wait_send()

        @pl.when(t < chips - 1)
        def _():
            for i in range(3):
                kv_hop(t, i).wait_send()
            w_hop(t).wait_send()

        return carry

    lax.fori_loop(1, chips, settle, 0)


def front(count, q, k, v, routes, w, hidden, gain, devices, collective_id):
    rows, width = q.shape
    depth = w.shape[1]
    chips = devices // 2
    kv_count = k.shape[1] // HD
    all_heads = width // HD
    half = jnp.bfloat16
    dma = pltpu.SemaphoreType.DMA
    hbm = pl.BlockSpec(memory_space=pltpu.HBM)
    vmem = pl.BlockSpec(memory_space=pltpu.VMEM)
    return pl.pallas_call(
        functools.partial(front_kernel, devices, kv_count, all_heads // kv_count),
        out_shape=(
            jax.ShapeDtypeStruct(hidden.shape, half),
            jax.ShapeDtypeStruct(hidden.shape, jnp.float32),
            jax.ShapeDtypeStruct((devices,) + routes.shape, half),
        ),
        in_specs=[pl.BlockSpec(memory_space=pltpu.SMEM), vmem, hbm, hbm, hbm, hbm, vmem, vmem],
        out_specs=(vmem, vmem, vmem),
        scratch_shapes=[
            pltpu.VMEM((devices,) + k.shape, half),
            pltpu.VMEM((devices,) + v.shape, half),
            pltpu.VMEM((devices,) + w.shape, half),
            pltpu.VMEM((all_heads, rows, HD), jnp.float32),
            pltpu.VMEM((all_heads, rows, 2 * HD), jnp.float32),
            pltpu.VMEM((rows, width), half),
            dma((4,)),
        ]
        + [dma((chips, 3))] * 4
        + [dma((chips,))] * 8,
        compiler_params=pltpu.CompilerParams(
            collective_id=collective_id, has_side_effects=True, vmem_limit_bytes=62 << 20
        ),
    )(count, q, k, v, routes, w, hidden, gain)


def moe_kernel(
    devices, live, cap, pieces,
    count_ref, x_ref, route_ref, wg_ref, wu_ref, wd_ref, o_ref, all_ref,
    wg, wu, wd, xb, picked, chosen, part, away, near_in, ring_in,
    w_sem, x_sem, g_send, g_recv, n_send, n_recv, s_send, s_recv, a_send, a_recv,
):
    chips = devices // 2
    me = lax.axis_index("shard")
    group = lax.axis_index("groups")
    core = me % 2
    way = 1 - 2 * core
    place = ring_place(chips, me // 2)
    rows, depth = x_ref.shape
    local = wg.shape[0]
    topk = route_ref.shape[1] // 2

    def chip_at(offset):
        return ring_chip(chips, (place + offset + 2 * chips) % chips)

    def own_origin(t):
        return chip_at(-way * t) * 2 + core

    def sib_origin(t):
        return chip_at(way * t) * 2 + 1 - core

    def when_live(origin, action):
        if live == chips:
            action()
        else:
            pl.when(origin // 2 < live)(action)

    ahead, behind, sibling = own_origin(-1), own_origin(1), me + way

    def span(piece):
        size = rows // pieces
        return pl.ds(piece * size, size)

    def remote(src, dst, send, recv, to):
        return pltpu.make_async_remote_copy(
            src_ref=src, dst_ref=dst, send_sem=send, recv_sem=recv,
            device_id=(group, to), device_id_type=MESH,
        )

    def hop(t, piece, src=None):
        place_of = all_ref.at[own_origin(t), span(piece)]
        src = place_of if src is None else src.at[span(piece)]
        return remote(src, place_of, g_send.at[t, piece], g_recv.at[t, piece], ahead)

    def near(t, piece, src=None):
        place_of = all_ref.at[own_origin(t), span(piece)]
        src = place_of if src is None else src.at[span(piece)]
        return remote(src, place_of, n_send.at[t, piece], n_recv.at[t, piece], sibling)

    def near_landing(t, piece):
        place_of = all_ref.at[sib_origin(t), span(piece)]
        return remote(place_of, place_of, n_send.at[t, piece], n_recv.at[t, piece], sibling)

    def landing(t, piece):
        place_of = all_ref.at[own_origin(t + 1), span(piece)]
        return remote(place_of, place_of, g_send.at[t, piece], g_recv.at[t, piece], ahead)

    def give(t):
        return remote(away.at[t % 2], near_in.at[t], a_send.at[t], a_recv.at[t], sibling)

    def pass_on(t, piece):
        return remote(
            part.at[t + 1, span(piece)], ring_in.at[t, span(piece)],
            s_send.at[t, piece], s_recv.at[t, piece], ahead,
        )

    loads = [
        pltpu.make_async_copy(src, dst, w_sem.at[i])
        for i, (src, dst) in enumerate(((wg_ref, wg), (wu_ref, wu), (wd_ref, wd)))
    ]

    barrier = pltpu.get_barrier_semaphore()
    for other in (ahead, behind, sibling):
        pl.semaphore_signal(barrier, inc=1, device_id=(group, other), device_id_type=MESH)
    pl.semaphore_wait(barrier, 3)

    def begin():
        for piece in range(pieces):
            hop(0, piece, x_ref).start()
        for piece in range(pieces):
            near(0, piece, x_ref).start()

    when_live(me, begin)
    for load in loads:
        load.start()

    def tick(t):
        def move():
            for piece in range(pieces):
                landing(t, piece).wait_recv()

                @pl.when(t + 1 < chips - 1)
                def _(piece=piece):
                    hop(t + 1, piece).start()

                near(t + 1, piece).start()

        when_live(own_origin(t + 1), move)

    def pick(t):
        parity = (t // 2) % 2

        def fetch(k, origin):
            return pltpu.make_async_copy(all_ref.at[origin], xb.at[k], x_sem.at[k])

        def fetch_own():
            @pl.when(t == 0)
            def _():
                pltpu.make_async_copy(x_ref, xb.at[0], x_sem.at[0]).start()

            @pl.when(t > 0)
            def _():
                fetch(0, own_origin(t)).start()

        def fetch_sib():
            for piece in range(pieces):
                near_landing(t, piece).wait_recv()
            fetch(1, sib_origin(t)).start()

        when_live(own_origin(t), fetch_own)
        when_live(sib_origin(t), fetch_sib)
        before = (
            lax.broadcasted_iota(jnp.int32, (rows, rows), 0)
            < lax.broadcasted_iota(jnp.int32, (rows, rows), 1)
        ).astype(jnp.bfloat16)
        slot_at = lax.broadcasted_iota(jnp.int32, (cap, rows), 0).astype(jnp.float32)
        for k, origin in ((0, own_origin(t)), (1, sib_origin(t))):
            q = 2 * (t % 2) + k
            place_of = pl.ds(pl.multiple_of(q * cap, 16), cap)

            def choose(k=k, origin=origin, q=q, place_of=place_of):
                fetch(k, origin).wait()
                route = route_ref[origin].astype(jnp.float32)
                ids, weights = route[:topk], route[topk:]
                at = origin * rows + lax.broadcasted_iota(jnp.int32, (1, rows), 1)
                alive = at < count_ref[0]
                hits, gains = [], []
                for e in range(local):
                    match = ids == (me * local + e).astype(jnp.float32)
                    hits.append(jnp.sum(jnp.where(match, 1.0, 0.0), axis=0, keepdims=True))
                    gain = jnp.sum(jnp.where(match, weights, 0.0), axis=0, keepdims=True)
                    gains.append(jnp.where(alive, gain, 0.0))
                rest = jnp.zeros((-local % 8, rows), jnp.float32)
                slots = jnp.dot(
                    jnp.concatenate(hits + [rest], axis=0).astype(jnp.bfloat16),
                    before,
                    preferred_element_type=jnp.float32,
                )
                mine, weighted = [], []
                for e in range(local):
                    hit = (slot_at == slots[e : e + 1]) & (hits[e] > 0.5)
                    mine.append(jnp.where(hit, 1.0, 0.0))
                    weighted.append(jnp.where(hit, gains[e], 0.0))
                choice = jnp.concatenate(mine, axis=0).astype(jnp.bfloat16)
                chosen[parity, q] = jnp.concatenate(weighted, axis=0).astype(jnp.bfloat16)
                rows_here = jnp.dot(choice, xb[k], preferred_element_type=jnp.float32)
                rows_here = rows_here.astype(jnp.bfloat16)
                for e in range(local):
                    picked[parity, e, place_of, :] = rows_here[e * cap : (e + 1) * cap]

            when_live(origin, choose)
            if live < chips:

                @pl.when(origin // 2 >= live)
                def _(place_of=place_of):
                    for e in range(local):
                        picked[parity, e, place_of, :] = jnp.zeros((cap, depth), jnp.bfloat16)

    def expert(b, e):
        parity = b % 2
        mine = picked[parity, e]
        gate = jnp.dot(mine, wg[e], preferred_element_type=jnp.float32)
        up = jnp.dot(mine, wu[e], preferred_element_type=jnp.float32)
        act = (gate / (1.0 + jnp.exp(-gate)) * up).astype(jnp.bfloat16)
        down = jnp.dot(act, wd[e], preferred_element_type=jnp.float32)
        picked[parity, e] = down.astype(jnp.bfloat16)

    def back(b):
        parity = b % 2
        for q in range(4):
            t = 2 * b + q // 2
            origin = own_origin(t) if q % 2 == 0 else sib_origin(t)

            def put(t=t, q=q):
                rows_here = jnp.concatenate(
                    [picked[parity, e, q * cap : (q + 1) * cap, :] for e in range(local)], axis=0
                )
                total = lax.dot_general(
                    chosen[parity, q], rows_here, (((0,), (0,)), ((), ())),
                    preferred_element_type=jnp.float32,
                ).astype(jnp.bfloat16)
                if q % 2 == 0:
                    part[t] = total
                else:

                    @pl.when(t >= 2)
                    def _():
                        when_live(sib_origin(t - 2), give(t - 2).wait_send)

                    away[t % 2] = total
                    give(t).start()

            if q % 2 == 1 and live < chips:

                @pl.when((origin // 2 >= live) & (t >= 2))
                def _(t=t):
                    when_live(sib_origin(t - 2), give(t - 2).wait_send)

            when_live(origin, put)

    def scatter(t):
        slot = (t + 1) % chips

        def move():
            give(slot).wait_recv()
            for piece in range(pieces):
                here = span(piece)
                total = part[slot, here, :].astype(jnp.float32) + near_in[slot, here, :].astype(
                    jnp.float32
                )
                if not (isinstance(t, int) and t == 0):
                    pass_on(t - 1, piece).wait_recv()
                    total = total + ring_in[t - 1, here, :].astype(jnp.float32)
                if isinstance(t, int) and t == chips - 1:
                    o_ref[here, :] = total.astype(o_ref.dtype)
                else:
                    part[slot, here, :] = total.astype(part.dtype)
                    pass_on(t, piece).start()

        when_live(own_origin(slot), move)

    def unit(u, carry):
        @pl.when(u == chips - 2)
        def _():
            scatter(0)

        @pl.when(u < chips - 1)
        def _():
            tick(u)

        @pl.when(u < chips)
        def _():
            pick(u)

        @pl.when(u == 1)
        def _():
            for load in loads:
                load.wait()

        @pl.when(u >= 1)
        def _():
            expert((u - 1) // 2, (u - 1) % 2)

        @pl.when((u >= 1) & (u % 2 == 0))
        def _():
            back((u - 1) // 2)

        @pl.when(u == chips - 1)
        def _():
            scatter(1)

        @pl.when(u == chips)
        def _():
            scatter(2)

        return carry

    lax.fori_loop(0, chips + 1, unit, 0)

    def later(t, carry):
        scatter(t)
        return carry

    lax.fori_loop(3, chips - 1, later, 0)
    if live < chips:
        o_ref[...] = jnp.zeros(o_ref.shape, o_ref.dtype)
    scatter(chips - 1)

    def settle(t, carry):
        def own():
            for piece in range(pieces):
                near(t, piece).wait_send()

                @pl.when(t < chips - 1)
                def _(piece=piece):
                    hop(t, piece).wait_send()

                @pl.when(t > 0)
                def _(piece=piece):
                    pass_on(t - 1, piece).wait_send()

        def sib():
            @pl.when(t >= chips - 2)
            def _():
                give(t).wait_send()

        when_live(own_origin(t), own)
        when_live(sib_origin(t), sib)
        return carry

    lax.fori_loop(0, chips, settle, 0)


def moe(count, x, routes, w_gate, w_up, w_down, devices, cap, live, collective_id, pieces=2):
    rows, depth = x.shape
    chips = devices // 2
    local = w_gate.shape[0]
    dma = pltpu.SemaphoreType.DMA
    both = dma((chips, pieces))
    hbm = pl.BlockSpec(memory_space=pltpu.HBM)
    vmem = pl.BlockSpec(memory_space=pltpu.VMEM)
    block = (rows, depth)
    half = jnp.bfloat16
    return pl.pallas_call(
        functools.partial(moe_kernel, devices, live, cap, pieces),
        out_shape=(
            jax.ShapeDtypeStruct(block, half),
            jax.ShapeDtypeStruct((devices,) + block, half),
        ),
        in_specs=[pl.BlockSpec(memory_space=pltpu.SMEM), hbm, vmem, hbm, hbm, hbm],
        out_specs=(vmem, hbm),
        scratch_shapes=[
            pltpu.VMEM(w_gate.shape, half),
            pltpu.VMEM(w_up.shape, half),
            pltpu.VMEM(w_down.shape, half),
            pltpu.VMEM((2,) + block, half),
            pltpu.VMEM((2, local, 4 * cap, depth), half),
            pltpu.VMEM((2, 4, local * cap, rows), half),
            pltpu.VMEM((chips,) + block, half),
            pltpu.VMEM((2,) + block, half),
            pltpu.VMEM((chips,) + block, half),
            pltpu.VMEM((chips - 1,) + block, half),
            dma((3,)),
            dma((2,)),
            both, both, both, both, both, both,
            dma((chips,)),
            dma((chips,)),
        ],
        compiler_params=pltpu.CompilerParams(
            collective_id=collective_id, has_side_effects=True, vmem_limit_bytes=63 << 20
        ),
    )(count, x, routes, w_gate, w_up, w_down)[0]


def per_device(
    hidden,
    query_rows,
    key_rows,
    value_rows,
    counts,
    out_weight,
    norm_gain,
    route_ids,
    route_weights,
    w_gate,
    w_up,
    w_down,
):
    devices = lax.axis_size("shard")
    me = lax.axis_index("shard")
    tok_dev, depth = hidden.shape
    topk = route_ids.shape[1]
    local = w_gate.shape[0]
    experts = local * devices
    capacity = max(2, tok_dev * topk * 5 // (4 * experts))
    capacity = -(-capacity // 16) * 16

    routes = jnp.concatenate([route_ids.astype(jnp.bfloat16), route_weights], axis=1).T
    normed, mixed_rows, routes_all = front(
        counts, query_rows, key_rows, value_rows, routes, out_weight, hidden, norm_gain[None, :],
        devices, 1,
    )
    summed = moe(
        counts, normed, routes_all, w_gate, w_up, w_down, devices, capacity, devices // 2, 2
    )
    return (mixed_rows + summed.astype(jnp.float32)).astype(jnp.bfloat16)


def solution(mesh):
    rows = P(("groups", "shard"), None)
    weights = P("shard", None, None)
    return jax.shard_map(
        per_device,
        mesh=mesh,
        in_specs=(
            rows,
            rows,
            rows,
            rows,
            P("groups"),
            P("shard", None),
            P(),
            rows,
            rows,
            weights,
            weights,
            weights,
        ),
        out_specs=rows,
        check_vma=False,
    )
```

```python
import functools
import math

import jax
import jax.numpy as jnp
from jax import lax
from jax.experimental import pallas as pl
from jax.experimental.pallas import tpu as pltpu
from jax.sharding import PartitionSpec as P

HD = 128
SEQ_LEN = 4096
NEG = -1e30
MESH = pl.DeviceIdType.MESH


def ring_place(chips, index):
    if chips == 8:
        z, y = index // 2, index % 2
        return z + y * (7 - 2 * z)
    return index


def ring_chip(chips, place):
    if chips == 8:
        half = place // 4
        z = place + half * (7 - 2 * place)
        return 2 * z + half
    return place


def front_kernel(
    devices, kv_count, heads,
    count_ref, q_ref, k_ref, v_ref, r_ref, w_ref, hidden_ref, gain_ref,
    normed_ref, mixed_ref, allr,
    allk, allv, allw, top, total, att,
    own_sem, kv_send, kv_recv, kn_send, kn_recv,
    w_send, w_recv, n_send, n_recv, x_send, x_recv, m_send, m_recv,
):
    chips = devices // 2
    me = lax.axis_index("shard")
    group = lax.axis_index("groups")
    core = me % 2
    way = 1 - 2 * core
    place = ring_place(chips, me // 2)
    rows = q_ref.shape[0]
    depth = w_ref.shape[1]
    scale = math.log2(math.e) / math.sqrt(HD)
    deep = w_ref.shape[0]
    lone = deep * 3 // 8 // 16 * 16
    shared = deep - 2 * lone
    side = group % 2
    partner = group + 1 - 2 * side

    def chip_at(offset):
        return ring_chip(chips, (place + offset + 2 * chips) % chips)

    def own_origin(t):
        return chip_at(-way * t) * 2 + core

    def sib_origin(t):
        return chip_at(way * t) * 2 + 1 - core

    ahead, behind, sibling = own_origin(-1), own_origin(1), me + way
    edge = deep - lone
    pieces = (pl.ds(pl.multiple_of(side * edge, 16), lone), pl.ds(lone, shared))
    theirs = pl.ds(pl.multiple_of((1 - side) * edge, 16), lone)
    small = ((k_ref, allk), (v_ref, allv), (r_ref, allr))

    def remote(src, dst, send, recv, to, to_group=None):
        return pltpu.make_async_remote_copy(
            src_ref=src, dst_ref=dst, send_sem=send, recv_sem=recv,
            device_id=(group if to_group is None else to_group, to), device_id_type=MESH,
        )

    def kv_hop(t, i, src=None):
        at = small[i][1].at[own_origin(t)]
        return remote(at if src is None else src, at, kv_send.at[t, i], kv_recv.at[t, i], ahead)

    def kv_landing(t, i):
        at = small[i][1].at[own_origin(t)]
        return remote(at, at, kv_send.at[t - 1, i], kv_recv.at[t - 1, i], ahead)

    def kv_near(t, i, src=None):
        at = small[i][1].at[own_origin(t)]
        return remote(at if src is None else src, at, kn_send.at[t, i], kn_recv.at[t, i], sibling)

    def kv_near_landing(t, i):
        at = small[i][1].at[sib_origin(t)]
        return remote(at, at, kn_send.at[t, i], kn_recv.at[t, i], sibling)

    def w_hop(t, i, src=None):
        at = allw.at[own_origin(t), pieces[i]]
        src = at if src is None else src.at[pieces[i]]
        return remote(src, at, w_send.at[t, i], w_recv.at[t, i], ahead)

    def w_landing(t, i):
        at = allw.at[own_origin(t), pieces[i]]
        return remote(at, at, w_send.at[t - 1, i], w_recv.at[t - 1, i], ahead)

    def w_near(t, i):
        at = allw.at[own_origin(t), pieces[i]]
        return remote(at, at, n_send.at[t, i], n_recv.at[t, i], sibling)

    def w_near_landing(t, i):
        at = allw.at[sib_origin(t), pieces[i]]
        return remote(at, at, n_send.at[t, i], n_recv.at[t, i], sibling)

    def w_near_all(origin, src):
        return remote(src, allw.at[origin], n_send.at[0, 0], n_recv.at[0, 0], sibling)

    def cross(t):
        at = allw.at[own_origin(t), pieces[0]]
        return remote(at, at, x_send.at[t], x_recv.at[t], me, partner)

    def cross_landing(t):
        at = allw.at[own_origin(t), theirs]
        return remote(at, at, x_send.at[t], x_recv.at[t], me, partner)

    def cross_near(t):
        at = allw.at[own_origin(t), theirs]
        return remote(at, at, m_send.at[t], m_recv.at[t], sibling)

    def cross_near_landing(t):
        at = allw.at[sib_origin(t), theirs]
        return remote(at, at, m_send.at[t], m_recv.at[t], sibling)

    own = [
        pltpu.make_async_copy(src, dst.at[me], own_sem.at[i])
        for i, (src, dst) in enumerate(small + ((w_ref, allw),))
    ]

    barrier = pltpu.get_barrier_semaphore()
    for other in (ahead, behind, sibling):
        pl.semaphore_signal(barrier, inc=1, device_id=(group, other), device_id_type=MESH)
    pl.semaphore_signal(barrier, inc=1, device_id=(partner, me), device_id_type=MESH)
    pl.semaphore_wait(barrier, 4)

    for i in range(3):
        kv_hop(0, i, small[i][0]).start()
    for i in range(3):
        kv_near(0, i, small[i][0]).start()
    for copy in own:
        copy.start()
    w_near_all(me, w_ref).start()

    def kv_tick(t):
        for i in range(3):
            kv_landing(t, i).wait_recv()

            @pl.when(t < chips - 1)
            def _(i=i):
                kv_hop(t, i).start()

            kv_near(t, i).start()

    def w_tick(t):
        for i in range(2):
            w_landing(t, i).wait_recv()

            @pl.when(t < chips - 1)
            def _(i=i):
                w_hop(t, i).start()

            if i == 0:
                cross(t).start()
            w_near(t, i).start()

        @pl.when(t > 1)
        def _():
            cross_tick(t - 1)

    def cross_tick(t):
        cross_landing(t).wait_recv()
        cross_near(t).start()

    apart = lax.broadcasted_iota(jnp.int32, (rows, rows), 1) - lax.broadcasted_iota(
        jnp.int32, (rows, rows), 0
    )
    cut = 2
    part_heads = heads // cut
    per_set = kv_count * cut

    def fold(n, g, part, first, masked):
        origins = []
        for t in (2 * n, 2 * n + 1):
            origins += [own_origin(t), sib_origin(t)]
        lanes = pl.ds(pl.multiple_of(g * HD, HD), HD)
        keys = jnp.concatenate([allk[o, :, lanes] for o in origins], axis=0)
        values = jnp.concatenate([allv[o, :, lanes] for o in origins], axis=0)
        values = jnp.concatenate([values, jnp.ones(values.shape, jnp.bfloat16)], axis=1)
        width = part_heads * HD
        q_here = q_ref[:, pl.ds(pl.multiple_of((g * cut + part) * width, width), width)]

        def scores_of(h):
            scores = lax.dot_general(
                q_here[:, h * HD : (h + 1) * HD], keys, (((1,), (1,)), ((), ())),
                preferred_element_type=jnp.float32,
            )
            if not masked:
                return scores
            return jnp.concatenate(
                [
                    jnp.where(apart <= (me - o) * rows, scores[:, j * rows : (j + 1) * rows], NEG)
                    for j, o in enumerate(origins)
                ],
                axis=1,
            )

        later = scores_of(0)
        for h in range(part_heads):
            at = (g * cut + part) * part_heads + h
            scores = later
            if h + 1 < part_heads:
                later = scores_of(h + 1)
            new = jnp.max(scores, axis=1, keepdims=True) * scale
            if first:
                new = jnp.broadcast_to(new, (rows, HD))
            else:
                old = top[at]
                new = jnp.maximum(old, new)
            expo = jnp.exp2(scores * scale - new[:, :1]).astype(jnp.bfloat16)
            both = jnp.dot(expo, values, preferred_element_type=jnp.float32)
            if not first:
                factor = jnp.exp2(old - new)
                both = total[at] * jnp.concatenate([factor, factor], axis=1) + both
            total[at] = both
            top[at] = new

    segments = chips // 2 * per_set
    lag = 3

    kv_tick(1)
    for copy in own:
        copy.wait()

    def segment(i, carry):
        n = i // per_set
        g = (i % per_set) // cut
        part = i % cut

        turn = i % per_set
        early, late = per_set // 2 - 1, per_set - 1
        t = jnp.where(turn == late, 2 * n + 3, 2 * n + 2)
        ticks = (turn == early) | (turn == late)

        @pl.when(ticks & (t < chips))
        def _():
            kv_tick(t)

        @pl.when(ticks & (t == lag))
        def _():
            for k in range(2):
                w_hop(0, k, w_ref).start()

        @pl.when(ticks & (t > lag))
        def _():
            w_tick(t - lag)

        @pl.when(i % per_set == 0)
        def _():
            for slot in (2 * n, 2 * n + 1):
                for k in range(3):
                    kv_near_landing(slot, k).wait_recv()

        some, every = False, True
        for slot in (2 * n, 2 * n + 1):
            for o in (own_origin(slot), sib_origin(slot)):
                some = (o <= me) | some
                every = (o < me) & every

        @pl.when(n == 0)
        def _():
            fold(n, g, part, True, True)

        @pl.when((n > 0) & every)
        def _():
            fold(n, g, part, False, False)

        @pl.when((n > 0) & some & jnp.logical_not(every))
        def _():
            fold(n, g, part, False, True)

        return carry

    lax.fori_loop(0, segments, segment, 0)

    alive = me * rows + lax.broadcasted_iota(jnp.int32, (rows, HD), 0) < count_ref[0]

    def close(at, carry):
        both = total[at]
        result = jnp.where(alive, both[:, :HD] / jnp.where(alive, both[:, HD:], 1.0), 0.0)
        att[:, pl.ds(pl.multiple_of(at * HD, HD), HD)] = result.astype(jnp.bfloat16)
        return carry

    sets = chips // 2
    tile = 256

    def project(b):
        for t in (2 * b, 2 * b + 1):

            @pl.when(t == 0)
            def _():
                w_near_all(sibling, allw.at[sibling]).wait_recv()

            @pl.when(t > 0)
            def _(t=t):
                for i in range(2):
                    w_near_landing(t, i).wait_recv()
                cross_near_landing(t).wait_recv()

        origins = []
        for t in (2 * b, 2 * b + 1):
            origins += [own_origin(t), sib_origin(t)]
        left = jnp.concatenate(
            [att[:, pl.ds(pl.multiple_of(o * deep, deep), deep)] for o in origins], axis=1
        )

        def column(c, carry):
            lanes = pl.ds(pl.multiple_of(c * tile, tile), tile)
            right = jnp.concatenate([allw[o, :, lanes] for o in origins], axis=0)
            mixed_ref[:, lanes] += jnp.dot(left, right, preferred_element_type=jnp.float32)
            return carry

        lax.fori_loop(0, depth // tile, column, 0)

    lax.fori_loop(0, kv_count * heads, close, 0)
    mixed_ref[...] = hidden_ref[...].astype(jnp.float32)

    def tail(b, carry):
        @pl.when(b == sets - 2)
        def _():
            w_tick(chips - 1)

        @pl.when(b == sets - 1)
        def _():
            cross_tick(chips - 1)

        project(b)
        return carry

    lax.fori_loop(0, sets, tail, 0)

    step = 32
    gain = gain_ref[...].astype(jnp.float32)

    def norm(c, carry):
        here = pl.ds(pl.multiple_of(c * step, step), step)
        mixed = mixed_ref[here, :]
        mean_square = jnp.mean(mixed * mixed, axis=1, keepdims=True)
        normed_ref[here, :] = (mixed * lax.rsqrt(mean_square + 1e-06) * gain).astype(jnp.bfloat16)
        return carry

    lax.fori_loop(0, rows // step, norm, 0)

    w_near_all(sibling, w_ref).wait_send()
    for i in range(2):
        w_hop(0, i, w_ref).wait_send()
    for i in range(3):
        kv_hop(0, i).wait_send()
        kv_near(0, i).wait_send()

    def settle(t, carry):
        for i in range(3):
            kv_near(t, i).wait_send()
        cross(t).wait_send()
        for i in range(2):
            w_near(t, i).wait_send()
        cross_near(t).wait_send()

        @pl.when(t < chips - 1)
        def _():
            for i in range(3):
                kv_hop(t, i).wait_send()
            for i in range(2):
                w_hop(t, i).wait_send()

        return carry

    lax.fori_loop(1, chips, settle, 0)


def front(count, q, k, v, routes, w, hidden, gain, devices, collective_id):
    rows, width = q.shape
    depth = w.shape[1]
    chips = devices // 2
    kv_count = k.shape[1] // HD
    all_heads = width // HD
    half = jnp.bfloat16
    dma = pltpu.SemaphoreType.DMA
    hbm = pl.BlockSpec(memory_space=pltpu.HBM)
    vmem = pl.BlockSpec(memory_space=pltpu.VMEM)
    return pl.pallas_call(
        functools.partial(front_kernel, devices, kv_count, all_heads // kv_count),
        out_shape=(
            jax.ShapeDtypeStruct(hidden.shape, half),
            jax.ShapeDtypeStruct(hidden.shape, jnp.float32),
            jax.ShapeDtypeStruct((devices,) + routes.shape, half),
        ),
        in_specs=[pl.BlockSpec(memory_space=pltpu.SMEM), vmem, hbm, hbm, hbm, hbm, vmem, vmem],
        out_specs=(vmem, vmem, vmem),
        scratch_shapes=[
            pltpu.VMEM((devices,) + k.shape, half),
            pltpu.VMEM((devices,) + v.shape, half),
            pltpu.VMEM((devices,) + w.shape, half),
            pltpu.VMEM((all_heads, rows, HD), jnp.float32),
            pltpu.VMEM((all_heads, rows, 2 * HD), jnp.float32),
            pltpu.VMEM((rows, width), half),
            dma((4,)),
        ]
        + [dma((chips, 3))] * 4
        + [dma((chips, 2))] * 4
        + [dma((chips,))] * 4,
        compiler_params=pltpu.CompilerParams(
            collective_id=collective_id, has_side_effects=True, vmem_limit_bytes=62 << 20
        ),
    )(count, q, k, v, routes, w, hidden, gain)


def moe_kernel(
    devices, live, cap, pieces,
    count_ref, x_ref, route_ref, wg_ref, wu_ref, wd_ref, o_ref, all_ref,
    wg, wu, wd, xb, picked, chosen, part, away, near_in, ring_in,
    w_sem, x_sem, g_send, g_recv, n_send, n_recv, s_send, s_recv, a_send, a_recv,
):
    chips = devices // 2
    me = lax.axis_index("shard")
    group = lax.axis_index("groups")
    core = me % 2
    way = 1 - 2 * core
    place = ring_place(chips, me // 2)
    rows, depth = x_ref.shape
    local = wg.shape[0]
    topk = route_ref.shape[1] // 2

    def chip_at(offset):
        return ring_chip(chips, (place + offset + 2 * chips) % chips)

    def own_origin(t):
        return chip_at(-way * t) * 2 + core

    def sib_origin(t):
        return chip_at(way * t) * 2 + 1 - core

    def when_live(origin, action):
        if live == chips:
            action()
        else:
            pl.when(origin // 2 < live)(action)

    ahead, behind, sibling = own_origin(-1), own_origin(1), me + way

    def span(piece):
        size = rows // pieces
        return pl.ds(piece * size, size)

    def remote(src, dst, send, recv, to):
        return pltpu.make_async_remote_copy(
            src_ref=src, dst_ref=dst, send_sem=send, recv_sem=recv,
            device_id=(group, to), device_id_type=MESH,
        )

    def hop(t, piece, src=None):
        place_of = all_ref.at[own_origin(t), span(piece)]
        src = place_of if src is None else src.at[span(piece)]
        return remote(src, place_of, g_send.at[t, piece], g_recv.at[t, piece], ahead)

    def near(t, piece, src=None):
        place_of = all_ref.at[own_origin(t), span(piece)]
        src = place_of if src is None else src.at[span(piece)]
        return remote(src, place_of, n_send.at[t, piece], n_recv.at[t, piece], sibling)

    def near_landing(t, piece):
        place_of = all_ref.at[sib_origin(t), span(piece)]
        return remote(place_of, place_of, n_send.at[t, piece], n_recv.at[t, piece], sibling)

    def landing(t, piece):
        place_of = all_ref.at[own_origin(t + 1), span(piece)]
        return remote(place_of, place_of, g_send.at[t, piece], g_recv.at[t, piece], ahead)

    def give(t):
        return remote(away.at[t % 2], near_in.at[t], a_send.at[t], a_recv.at[t], sibling)

    def pass_on(t, piece):
        return remote(
            part.at[t + 1, span(piece)], ring_in.at[t, span(piece)],
            s_send.at[t, piece], s_recv.at[t, piece], ahead,
        )

    loads = [
        pltpu.make_async_copy(src, dst, w_sem.at[i])
        for i, (src, dst) in enumerate(((wg_ref, wg), (wu_ref, wu), (wd_ref, wd)))
    ]

    barrier = pltpu.get_barrier_semaphore()
    for other in (ahead, behind, sibling):
        pl.semaphore_signal(barrier, inc=1, device_id=(group, other), device_id_type=MESH)
    pl.semaphore_wait(barrier, 3)

    def begin():
        for piece in range(pieces):
            hop(0, piece, x_ref).start()
        for piece in range(pieces):
            near(0, piece, x_ref).start()

    when_live(me, begin)
    for load in loads:
        load.start()

    def tick(t):
        def move():
            for piece in range(pieces):
                landing(t, piece).wait_recv()

                @pl.when(t + 1 < chips - 1)
                def _(piece=piece):
                    hop(t + 1, piece).start()

                near(t + 1, piece).start()

        when_live(own_origin(t + 1), move)

    def pick(t):
        parity = (t // 2) % 2

        def fetch(k, origin):
            return pltpu.make_async_copy(all_ref.at[origin], xb.at[k], x_sem.at[k])

        def fetch_own():
            @pl.when(t == 0)
            def _():
                pltpu.make_async_copy(x_ref, xb.at[0], x_sem.at[0]).start()

            @pl.when(t > 0)
            def _():
                fetch(0, own_origin(t)).start()

        def fetch_sib():
            for piece in range(pieces):
                near_landing(t, piece).wait_recv()
            fetch(1, sib_origin(t)).start()

        when_live(own_origin(t), fetch_own)
        when_live(sib_origin(t), fetch_sib)
        before = (
            lax.broadcasted_iota(jnp.int32, (rows, rows), 0)
            < lax.broadcasted_iota(jnp.int32, (rows, rows), 1)
        ).astype(jnp.bfloat16)
        slot_at = lax.broadcasted_iota(jnp.int32, (cap, rows), 0).astype(jnp.float32)
        for k, origin in ((0, own_origin(t)), (1, sib_origin(t))):
            q = 2 * (t % 2) + k
            place_of = pl.ds(pl.multiple_of(q * cap, 16), cap)

            def choose(k=k, origin=origin, q=q, place_of=place_of):
                fetch(k, origin).wait()
                route = route_ref[origin].astype(jnp.float32)
                ids, weights = route[:topk], route[topk:]
                at = origin * rows + lax.broadcasted_iota(jnp.int32, (1, rows), 1)
                alive = at < count_ref[0]
                hits, gains = [], []
                for e in range(local):
                    match = ids == (me * local + e).astype(jnp.float32)
                    hits.append(jnp.sum(jnp.where(match, 1.0, 0.0), axis=0, keepdims=True))
                    gain = jnp.sum(jnp.where(match, weights, 0.0), axis=0, keepdims=True)
                    gains.append(jnp.where(alive, gain, 0.0))
                rest = jnp.zeros((-local % 8, rows), jnp.float32)
                slots = jnp.dot(
                    jnp.concatenate(hits + [rest], axis=0).astype(jnp.bfloat16),
                    before,
                    preferred_element_type=jnp.float32,
                )
                mine, weighted = [], []
                for e in range(local):
                    hit = (slot_at == slots[e : e + 1]) & (hits[e] > 0.5)
                    mine.append(jnp.where(hit, 1.0, 0.0))
                    weighted.append(jnp.where(hit, gains[e], 0.0))
                choice = jnp.concatenate(mine, axis=0).astype(jnp.bfloat16)
                chosen[parity, q] = jnp.concatenate(weighted, axis=0).astype(jnp.bfloat16)
                rows_here = jnp.dot(choice, xb[k], preferred_element_type=jnp.float32)
                rows_here = rows_here.astype(jnp.bfloat16)
                for e in range(local):
                    picked[parity, e, place_of, :] = rows_here[e * cap : (e + 1) * cap]

            when_live(origin, choose)
            if live < chips:

                @pl.when(origin // 2 >= live)
                def _(place_of=place_of):
                    for e in range(local):
                        picked[parity, e, place_of, :] = jnp.zeros((cap, depth), jnp.bfloat16)

    def expert(b, e):
        parity = b % 2
        mine = picked[parity, e]
        gate = jnp.dot(mine, wg[e], preferred_element_type=jnp.float32)
        up = jnp.dot(mine, wu[e], preferred_element_type=jnp.float32)
        act = (gate / (1.0 + jnp.exp(-gate)) * up).astype(jnp.bfloat16)
        down = jnp.dot(act, wd[e], preferred_element_type=jnp.float32)
        picked[parity, e] = down.astype(jnp.bfloat16)

    def back(b):
        parity = b % 2
        for q in range(4):
            t = 2 * b + q // 2
            origin = own_origin(t) if q % 2 == 0 else sib_origin(t)

            def put(t=t, q=q):
                rows_here = jnp.concatenate(
                    [picked[parity, e, q * cap : (q + 1) * cap, :] for e in range(local)], axis=0
                )
                total = lax.dot_general(
                    chosen[parity, q], rows_here, (((0,), (0,)), ((), ())),
                    preferred_element_type=jnp.float32,
                ).astype(jnp.bfloat16)
                if q % 2 == 0:
                    part[t] = total
                else:

                    @pl.when(t >= 2)
                    def _():
                        when_live(sib_origin(t - 2), give(t - 2).wait_send)

                    away[t % 2] = total
                    give(t).start()

            if q % 2 == 1 and live < chips:

                @pl.when((origin // 2 >= live) & (t >= 2))
                def _(t=t):
                    when_live(sib_origin(t - 2), give(t - 2).wait_send)

            when_live(origin, put)

    def scatter(t):
        slot = (t + 1) % chips

        def move():
            give(slot).wait_recv()
            for piece in range(pieces):
                here = span(piece)
                total = part[slot, here, :].astype(jnp.float32) + near_in[slot, here, :].astype(
                    jnp.float32
                )
                if not (isinstance(t, int) and t == 0):
                    pass_on(t - 1, piece).wait_recv()
                    total = total + ring_in[t - 1, here, :].astype(jnp.float32)
                if isinstance(t, int) and t == chips - 1:
                    o_ref[here, :] = total.astype(o_ref.dtype)
                else:
                    part[slot, here, :] = total.astype(part.dtype)
                    pass_on(t, piece).start()

        when_live(own_origin(slot), move)

    def unit(u, carry):
        @pl.when(u == chips - 2)
        def _():
            scatter(0)

        @pl.when(u < chips - 1)
        def _():
            tick(u)

        @pl.when(u < chips)
        def _():
            pick(u)

        @pl.when(u == 1)
        def _():
            for load in loads:
                load.wait()

        @pl.when(u >= 1)
        def _():
            expert((u - 1) // 2, (u - 1) % 2)

        @pl.when((u >= 1) & (u % 2 == 0))
        def _():
            back((u - 1) // 2)

        @pl.when(u == chips - 1)
        def _():
            scatter(1)

        @pl.when(u == chips)
        def _():
            scatter(2)

        return carry

    lax.fori_loop(0, chips + 1, unit, 0)

    def later(t, carry):
        scatter(t)
        return carry

    lax.fori_loop(3, chips - 1, later, 0)
    if live < chips:
        o_ref[...] = jnp.zeros(o_ref.shape, o_ref.dtype)
    scatter(chips - 1)

    def settle(t, carry):
        def own():
            for piece in range(pieces):
                near(t, piece).wait_send()

                @pl.when(t < chips - 1)
                def _(piece=piece):
                    hop(t, piece).wait_send()

                @pl.when(t > 0)
                def _(piece=piece):
                    pass_on(t - 1, piece).wait_send()

        def sib():
            @pl.when(t >= chips - 2)
            def _():
                give(t).wait_send()

        when_live(own_origin(t), own)
        when_live(sib_origin(t), sib)
        return carry

    lax.fori_loop(0, chips, settle, 0)


def moe(count, x, routes, w_gate, w_up, w_down, devices, cap, live, collective_id, pieces=2):
    rows, depth = x.shape
    chips = devices // 2
    local = w_gate.shape[0]
    dma = pltpu.SemaphoreType.DMA
    both = dma((chips, pieces))
    hbm = pl.BlockSpec(memory_space=pltpu.HBM)
    vmem = pl.BlockSpec(memory_space=pltpu.VMEM)
    block = (rows, depth)
    half = jnp.bfloat16
    return pl.pallas_call(
        functools.partial(moe_kernel, devices, live, cap, pieces),
        out_shape=(
            jax.ShapeDtypeStruct(block, half),
            jax.ShapeDtypeStruct((devices,) + block, half),
        ),
        in_specs=[pl.BlockSpec(memory_space=pltpu.SMEM), hbm, vmem, hbm, hbm, hbm],
        out_specs=(vmem, hbm),
        scratch_shapes=[
            pltpu.VMEM(w_gate.shape, half),
            pltpu.VMEM(w_up.shape, half),
            pltpu.VMEM(w_down.shape, half),
            pltpu.VMEM((2,) + block, half),
            pltpu.VMEM((2, local, 4 * cap, depth), half),
            pltpu.VMEM((2, 4, local * cap, rows), half),
            pltpu.VMEM((chips,) + block, half),
            pltpu.VMEM((2,) + block, half),
            pltpu.VMEM((chips,) + block, half),
            pltpu.VMEM((chips - 1,) + block, half),
            dma((3,)),
            dma((2,)),
            both, both, both, both, both, both,
            dma((chips,)),
            dma((chips,)),
        ],
        compiler_params=pltpu.CompilerParams(
            collective_id=collective_id, has_side_effects=True, vmem_limit_bytes=63 << 20
        ),
    )(count, x, routes, w_gate, w_up, w_down)[0]


def per_device(
    hidden,
    query_rows,
    key_rows,
    value_rows,
    counts,
    out_weight,
    norm_gain,
    route_ids,
    route_weights,
    w_gate,
    w_up,
    w_down,
):
    devices = lax.axis_size("shard")
    me = lax.axis_index("shard")
    tok_dev, depth = hidden.shape
    topk = route_ids.shape[1]
    local = w_gate.shape[0]
    experts = local * devices
    capacity = max(2, tok_dev * topk * 5 // (4 * experts))
    capacity = -(-capacity // 16) * 16

    routes = jnp.concatenate([route_ids.astype(jnp.bfloat16), route_weights], axis=1).T
    normed, mixed_rows, routes_all = front(
        counts, query_rows, key_rows, value_rows, routes, out_weight, hidden, norm_gain[None, :],
        devices, 1,
    )
    summed = moe(
        counts, normed, routes_all, w_gate, w_up, w_down, devices, capacity, devices // 2, 2
    )
    return (mixed_rows + summed.astype(jnp.float32)).astype(jnp.bfloat16)


def solution(mesh):
    rows = P(("groups", "shard"), None)
    weights = P("shard", None, None)
    return jax.shard_map(
        per_device,
        mesh=mesh,
        in_specs=(
            rows,
            rows,
            rows,
            rows,
            P("groups"),
            P("shard", None),
            P(),
            rows,
            rows,
            weights,
            weights,
            weights,
        ),
        out_specs=rows,
        check_vma=False,
    )
```

```python
import functools
import math

import jax
import jax.numpy as jnp
from jax import lax
from jax.experimental import pallas as pl
from jax.experimental.pallas import tpu as pltpu
from jax.sharding import PartitionSpec as P

HD = 128
SEQ_LEN = 4096
NEG = -1e30
MESH = pl.DeviceIdType.MESH


def ring_place(chips, index):
    if chips == 8:
        z, y = index // 2, index % 2
        return z + y * (7 - 2 * z)
    return index


def ring_chip(chips, place):
    if chips == 8:
        half = place // 4
        z = place + half * (7 - 2 * place)
        return 2 * z + half
    return place


def front_kernel(
    devices, kv_count, heads,
    count_ref, q_ref, k_ref, v_ref, ids_ref, weights_ref, w_ref, hidden_ref, gain_ref,
    normed_ref, mixed_ref, allr,
    r_ref, allk, allv, allw, top, total, att,
    own_sem, kv_send, kv_recv, kn_send, kn_recv,
    w_send, w_recv, n_send, n_recv, x_send, x_recv, m_send, m_recv,
):
    chips = devices // 2
    me = lax.axis_index("shard")
    group = lax.axis_index("groups")
    core = me % 2
    way = 1 - 2 * core
    place = ring_place(chips, me // 2)
    rows = q_ref.shape[0]
    depth = w_ref.shape[1]
    scale = math.log2(math.e) / math.sqrt(HD)
    deep = w_ref.shape[0]
    lone = deep * 3 // 8 // 16 * 16
    shared = deep - 2 * lone
    side = group % 2
    partner = group + 1 - 2 * side

    def chip_at(offset):
        return ring_chip(chips, (place + offset + 2 * chips) % chips)

    def own_origin(t):
        return chip_at(-way * t) * 2 + core

    def sib_origin(t):
        return chip_at(way * t) * 2 + 1 - core

    ahead, behind, sibling = own_origin(-1), own_origin(1), me + way
    edge = deep - lone
    pieces = (pl.ds(pl.multiple_of(side * edge, 16), lone), pl.ds(lone, shared))
    theirs = pl.ds(pl.multiple_of((1 - side) * edge, 16), lone)
    small = ((k_ref, allk), (v_ref, allv), (r_ref, allr))

    def remote(src, dst, send, recv, to, to_group=None):
        return pltpu.make_async_remote_copy(
            src_ref=src, dst_ref=dst, send_sem=send, recv_sem=recv,
            device_id=(group if to_group is None else to_group, to), device_id_type=MESH,
        )

    def kv_hop(t, i, src=None):
        at = small[i][1].at[own_origin(t)]
        return remote(at if src is None else src, at, kv_send.at[t, i], kv_recv.at[t, i], ahead)

    def kv_landing(t, i):
        at = small[i][1].at[own_origin(t)]
        return remote(at, at, kv_send.at[t - 1, i], kv_recv.at[t - 1, i], ahead)

    def kv_near(t, i, src=None):
        at = small[i][1].at[own_origin(t)]
        return remote(at if src is None else src, at, kn_send.at[t, i], kn_recv.at[t, i], sibling)

    def kv_near_landing(t, i):
        at = small[i][1].at[sib_origin(t)]
        return remote(at, at, kn_send.at[t, i], kn_recv.at[t, i], sibling)

    def w_hop(t, i, src=None):
        at = allw.at[own_origin(t), pieces[i]]
        src = at if src is None else src.at[pieces[i]]
        return remote(src, at, w_send.at[t, i], w_recv.at[t, i], ahead)

    def w_landing(t, i):
        at = allw.at[own_origin(t), pieces[i]]
        return remote(at, at, w_send.at[t - 1, i], w_recv.at[t - 1, i], ahead)

    def w_near(t, i):
        at = allw.at[own_origin(t), pieces[i]]
        return remote(at, at, n_send.at[t, i], n_recv.at[t, i], sibling)

    def w_near_landing(t, i):
        at = allw.at[sib_origin(t), pieces[i]]
        return remote(at, at, n_send.at[t, i], n_recv.at[t, i], sibling)

    def w_near_all(origin, src):
        return remote(src, allw.at[origin], n_send.at[0, 0], n_recv.at[0, 0], sibling)

    def cross(t):
        at = allw.at[own_origin(t), pieces[0]]
        return remote(at, at, x_send.at[t], x_recv.at[t], me, partner)

    def cross_landing(t):
        at = allw.at[own_origin(t), theirs]
        return remote(at, at, x_send.at[t], x_recv.at[t], me, partner)

    def cross_near(t):
        at = allw.at[own_origin(t), theirs]
        return remote(at, at, m_send.at[t], m_recv.at[t], sibling)

    def cross_near_landing(t):
        at = allw.at[sib_origin(t), theirs]
        return remote(at, at, m_send.at[t], m_recv.at[t], sibling)

    own = [
        pltpu.make_async_copy(src, dst.at[me], own_sem.at[i])
        for i, (src, dst) in enumerate(small + ((w_ref, allw),))
    ]

    barrier = pltpu.get_barrier_semaphore()
    for other in (ahead, behind, sibling):
        pl.semaphore_signal(barrier, inc=1, device_id=(group, other), device_id_type=MESH)
    pl.semaphore_signal(barrier, inc=1, device_id=(partner, me), device_id_type=MESH)

    r_ref[...] = jnp.concatenate(
        [ids_ref[...].astype(jnp.float32), weights_ref[...].astype(jnp.float32)], axis=0
    ).astype(jnp.bfloat16)
    pl.semaphore_wait(barrier, 4)

    for i in range(3):
        kv_hop(0, i, small[i][0]).start()
    for i in range(3):
        kv_near(0, i, small[i][0]).start()
    for copy in own:
        copy.start()
    w_near_all(me, w_ref).start()

    def kv_tick(t):
        for i in range(3):
            kv_landing(t, i).wait_recv()

            @pl.when(t < chips - 1)
            def _(i=i):
                kv_hop(t, i).start()

            kv_near(t, i).start()

    def w_tick(t):
        for i in range(2):
            w_landing(t, i).wait_recv()

            @pl.when(t < chips - 1)
            def _(i=i):
                w_hop(t, i).start()

            if i == 0:
                cross(t).start()
            w_near(t, i).start()

        @pl.when(t > 1)
        def _():
            cross_tick(t - 1)

    def cross_tick(t):
        cross_landing(t).wait_recv()
        cross_near(t).start()

    apart = lax.broadcasted_iota(jnp.int32, (rows, rows), 1) - lax.broadcasted_iota(
        jnp.int32, (rows, rows), 0
    )
    cut = 2
    part_heads = heads // cut
    per_set = kv_count * cut

    def fold(n, g, part, first, masked):
        origins = []
        for t in (2 * n, 2 * n + 1):
            origins += [own_origin(t), sib_origin(t)]
        lanes = pl.ds(pl.multiple_of(g * HD, HD), HD)
        keys = jnp.concatenate([allk[o, :, lanes] for o in origins], axis=0)
        values = jnp.concatenate([allv[o, :, lanes] for o in origins], axis=0)
        values = jnp.concatenate([values, jnp.ones(values.shape, jnp.bfloat16)], axis=1)
        width = part_heads * HD
        q_here = q_ref[:, pl.ds(pl.multiple_of((g * cut + part) * width, width), width)]

        def scores_of(h):
            scores = lax.dot_general(
                q_here[:, h * HD : (h + 1) * HD], keys, (((1,), (1,)), ((), ())),
                preferred_element_type=jnp.float32,
            )
            if not masked:
                return scores
            return jnp.concatenate(
                [
                    jnp.where(apart <= (me - o) * rows, scores[:, j * rows : (j + 1) * rows], NEG)
                    for j, o in enumerate(origins)
                ],
                axis=1,
            )

        later = scores_of(0)
        for h in range(part_heads):
            at = (g * cut + part) * part_heads + h
            scores = later
            if h + 1 < part_heads:
                later = scores_of(h + 1)
            new = jnp.max(scores, axis=1, keepdims=True) * scale
            if first:
                new = jnp.broadcast_to(new, (rows, HD))
            else:
                old = top[at]
                new = jnp.maximum(old, new)
            expo = jnp.exp2(scores * scale - new[:, :1]).astype(jnp.bfloat16)
            both = jnp.dot(expo, values, preferred_element_type=jnp.float32)
            if not first:
                factor = jnp.exp2(old - new)
                both = total[at] * jnp.concatenate([factor, factor], axis=1) + both
            total[at] = both
            top[at] = new

    segments = chips // 2 * per_set
    lag = 3

    kv_tick(1)
    for copy in own:
        copy.wait()

    def segment(i, carry):
        n = i // per_set
        g = (i % per_set) // cut
        part = i % cut

        turn = i % per_set
        early, late = per_set // 2 - 1, per_set - 1
        t = jnp.where(turn == late, 2 * n + 3, 2 * n + 2)
        ticks = (turn == early) | (turn == late)

        @pl.when(ticks & (t < chips))
        def _():
            kv_tick(t)

        @pl.when(ticks & (t == lag))
        def _():
            for k in range(2):
                w_hop(0, k, w_ref).start()

        @pl.when(ticks & (t > lag))
        def _():
            w_tick(t - lag)

        @pl.when(i % per_set == 0)
        def _():
            for slot in (2 * n, 2 * n + 1):
                for k in range(3):
                    kv_near_landing(slot, k).wait_recv()

        some, every = False, True
        for slot in (2 * n, 2 * n + 1):
            for o in (own_origin(slot), sib_origin(slot)):
                some = (o <= me) | some
                every = (o < me) & every

        @pl.when(n == 0)
        def _():
            fold(n, g, part, True, True)

        @pl.when((n > 0) & every)
        def _():
            fold(n, g, part, False, False)

        @pl.when((n > 0) & some & jnp.logical_not(every))
        def _():
            fold(n, g, part, False, True)

        return carry

    lax.fori_loop(0, segments, segment, 0)

    alive = me * rows + lax.broadcasted_iota(jnp.int32, (rows, HD), 0) < count_ref[0]

    def close(at, carry):
        both = total[at]
        result = jnp.where(alive, both[:, :HD] / jnp.where(alive, both[:, HD:], 1.0), 0.0)
        att[:, pl.ds(pl.multiple_of(at * HD, HD), HD)] = result.astype(jnp.bfloat16)
        return carry

    sets = chips // 2
    tile = 256

    def project(b):
        for t in (2 * b, 2 * b + 1):

            @pl.when(t == 0)
            def _():
                w_near_all(sibling, allw.at[sibling]).wait_recv()

            @pl.when(t > 0)
            def _(t=t):
                for i in range(2):
                    w_near_landing(t, i).wait_recv()
                cross_near_landing(t).wait_recv()

        origins = []
        for t in (2 * b, 2 * b + 1):
            origins += [own_origin(t), sib_origin(t)]
        left = jnp.concatenate(
            [att[:, pl.ds(pl.multiple_of(o * deep, deep), deep)] for o in origins], axis=1
        )

        def column(c, carry):
            lanes = pl.ds(pl.multiple_of(c * tile, tile), tile)
            right = jnp.concatenate([allw[o, :, lanes] for o in origins], axis=0)
            mixed_ref[:, lanes] += jnp.dot(left, right, preferred_element_type=jnp.float32)
            return carry

        lax.fori_loop(0, depth // tile, column, 0)

    lax.fori_loop(0, kv_count * heads, close, 0)
    mixed_ref[...] = hidden_ref[...].astype(jnp.float32)

    def tail(b, carry):
        @pl.when(b == sets - 2)
        def _():
            w_tick(chips - 1)

        @pl.when(b == sets - 1)
        def _():
            cross_tick(chips - 1)

        project(b)
        return carry

    lax.fori_loop(0, sets, tail, 0)

    step = 32
    gain = gain_ref[...].astype(jnp.float32).reshape(1, depth)

    def norm(c, carry):
        here = pl.ds(pl.multiple_of(c * step, step), step)
        mixed = mixed_ref[here, :]
        mean_square = jnp.mean(mixed * mixed, axis=1, keepdims=True)
        normed_ref[here, :] = (mixed * lax.rsqrt(mean_square + 1e-06) * gain).astype(jnp.bfloat16)
        return carry

    lax.fori_loop(0, rows // step, norm, 0)

    w_near_all(sibling, w_ref).wait_send()
    for i in range(2):
        w_hop(0, i, w_ref).wait_send()
    for i in range(3):
        kv_hop(0, i).wait_send()
        kv_near(0, i).wait_send()

    def settle(t, carry):
        for i in range(3):
            kv_near(t, i).wait_send()
        cross(t).wait_send()
        for i in range(2):
            w_near(t, i).wait_send()
        cross_near(t).wait_send()

        @pl.when(t < chips - 1)
        def _():
            for i in range(3):
                kv_hop(t, i).wait_send()
            for i in range(2):
                w_hop(t, i).wait_send()

        return carry

    lax.fori_loop(1, chips, settle, 0)


def front(count, q, k, v, ids, weights, w, hidden, gain, devices, collective_id):
    rows, width = q.shape
    depth = w.shape[1]
    chips = devices // 2
    kv_count = k.shape[1] // HD
    all_heads = width // HD
    half = jnp.bfloat16
    dma = pltpu.SemaphoreType.DMA
    hbm = pl.BlockSpec(memory_space=pltpu.HBM)
    vmem = pl.BlockSpec(memory_space=pltpu.VMEM)
    return pl.pallas_call(
        functools.partial(front_kernel, devices, kv_count, all_heads // kv_count),
        out_shape=(
            jax.ShapeDtypeStruct(hidden.shape, half),
            jax.ShapeDtypeStruct(hidden.shape, jnp.float32),
            jax.ShapeDtypeStruct((devices, 2 * ids.shape[0], rows), half),
        ),
        in_specs=[pl.BlockSpec(memory_space=pltpu.SMEM), vmem, hbm, hbm, vmem, vmem, hbm, vmem, vmem],
        out_specs=(vmem, vmem, vmem),
        scratch_shapes=[
            pltpu.VMEM((2 * ids.shape[0], rows), half),
            pltpu.VMEM((devices,) + k.shape, half),
            pltpu.VMEM((devices,) + v.shape, half),
            pltpu.VMEM((devices,) + w.shape, half),
            pltpu.VMEM((all_heads, rows, HD), jnp.float32),
            pltpu.VMEM((all_heads, rows, 2 * HD), jnp.float32),
            pltpu.VMEM((rows, width), half),
            dma((4,)),
        ]
        + [dma((chips, 3))] * 4
        + [dma((chips, 2))] * 4
        + [dma((chips,))] * 4,
        compiler_params=pltpu.CompilerParams(
            collective_id=collective_id, has_side_effects=True, vmem_limit_bytes=62 << 20
        ),
    )(count, q, k, v, ids, weights, w, hidden, gain)


def moe_kernel(
    devices, live, cap, pieces,
    count_ref, x_ref, mixed_ref, route_ref, wg_ref, wu_ref, wd_ref, o_ref, all_ref,
    mixed, acts, wg, wu, wd, xb, picked, chosen, part, away, near_in, ring_in,
    w_sem, x_sem, g_send, g_recv, n_send, n_recv, s_send, s_recv, a_send, a_recv,
):
    chips = devices // 2
    me = lax.axis_index("shard")
    group = lax.axis_index("groups")
    core = me % 2
    way = 1 - 2 * core
    place = ring_place(chips, me // 2)
    rows, depth = x_ref.shape
    local = wg.shape[0]
    topk = route_ref.shape[1] // 2

    def chip_at(offset):
        return ring_chip(chips, (place + offset + 2 * chips) % chips)

    def own_origin(t):
        return chip_at(-way * t) * 2 + core

    def sib_origin(t):
        return chip_at(way * t) * 2 + 1 - core

    def when_live(origin, action):
        if live == chips:
            action()
        else:
            pl.when(origin // 2 < live)(action)

    ahead, behind, sibling = own_origin(-1), own_origin(1), me + way

    def span(piece):
        size = rows // pieces
        return pl.ds(piece * size, size)

    def remote(src, dst, send, recv, to):
        return pltpu.make_async_remote_copy(
            src_ref=src, dst_ref=dst, send_sem=send, recv_sem=recv,
            device_id=(group, to), device_id_type=MESH,
        )

    def hop(t, piece, src=None):
        place_of = all_ref.at[own_origin(t), span(piece)]
        src = place_of if src is None else src.at[span(piece)]
        return remote(src, place_of, g_send.at[t, piece], g_recv.at[t, piece], ahead)

    def near(t, piece, src=None):
        place_of = all_ref.at[own_origin(t), span(piece)]
        src = place_of if src is None else src.at[span(piece)]
        return remote(src, place_of, n_send.at[t, piece], n_recv.at[t, piece], sibling)

    def near_landing(t, piece):
        place_of = all_ref.at[sib_origin(t), span(piece)]
        return remote(place_of, place_of, n_send.at[t, piece], n_recv.at[t, piece], sibling)

    def landing(t, piece):
        place_of = all_ref.at[own_origin(t + 1), span(piece)]
        return remote(place_of, place_of, g_send.at[t, piece], g_recv.at[t, piece], ahead)

    def give(t):
        return remote(away.at[t % 2], near_in.at[t], a_send.at[t], a_recv.at[t], sibling)

    def pass_on(t, piece):
        return remote(
            part.at[t + 1, span(piece)], ring_in.at[t, span(piece)],
            s_send.at[t, piece], s_recv.at[t, piece], ahead,
        )

    loads = [
        pltpu.make_async_copy(src, dst, w_sem.at[i])
        for i, (src, dst) in enumerate(
            ((wg_ref, wg), (wu_ref, wu), (wd_ref, wd), (mixed_ref, mixed))
        )
    ]

    barrier = pltpu.get_barrier_semaphore()
    for other in (ahead, behind, sibling):
        pl.semaphore_signal(barrier, inc=1, device_id=(group, other), device_id_type=MESH)
    pl.semaphore_wait(barrier, 3)

    def begin():
        for piece in range(pieces):
            hop(0, piece, x_ref).start()
        for piece in range(pieces):
            near(0, piece, x_ref).start()

    when_live(me, begin)
    for load in loads:
        load.start()

    def over(size, most, action):
        tile = math.gcd(size, most)

        def one(c, carry):
            action(pl.ds(pl.multiple_of(c * tile, tile), tile))
            return carry

        lax.fori_loop(0, size // tile, one, 0)

    def tick(t):
        def move():
            for piece in range(pieces):
                landing(t, piece).wait_recv()

                @pl.when(t + 1 < chips - 1)
                def _(piece=piece):
                    hop(t + 1, piece).start()

                near(t + 1, piece).start()

        when_live(own_origin(t + 1), move)

    def pick(t):
        parity = (t // 2) % 2

        def fetch(k, origin):
            return pltpu.make_async_copy(all_ref.at[origin], xb.at[k], x_sem.at[k])

        def fetch_own():
            @pl.when(t == 0)
            def _():
                pltpu.make_async_copy(x_ref, xb.at[0], x_sem.at[0]).start()

            @pl.when(t > 0)
            def _():
                fetch(0, own_origin(t)).start()

        def fetch_sib():
            for piece in range(pieces):
                near_landing(t, piece).wait_recv()
            fetch(1, sib_origin(t)).start()

        when_live(own_origin(t), fetch_own)
        when_live(sib_origin(t), fetch_sib)
        before = (
            lax.broadcasted_iota(jnp.int32, (rows, rows), 0)
            < lax.broadcasted_iota(jnp.int32, (rows, rows), 1)
        ).astype(jnp.bfloat16)
        slot_at = lax.broadcasted_iota(jnp.int32, (cap, rows), 0).astype(jnp.float32)
        for k, origin in ((0, own_origin(t)), (1, sib_origin(t))):
            q = 2 * (t % 2) + k
            place_of = pl.ds(pl.multiple_of(q * cap, 16), cap)

            def choose(k=k, origin=origin, q=q, place_of=place_of):
                fetch(k, origin).wait()
                route = route_ref[origin].astype(jnp.float32)
                ids, weights = route[:topk], route[topk:]
                at = origin * rows + lax.broadcasted_iota(jnp.int32, (1, rows), 1)
                alive = at < count_ref[0]
                hits, gains = [], []
                for e in range(local):
                    match = ids == (me * local + e).astype(jnp.float32)
                    hits.append(jnp.sum(jnp.where(match, 1.0, 0.0), axis=0, keepdims=True))
                    gain = jnp.sum(jnp.where(match, weights, 0.0), axis=0, keepdims=True)
                    gains.append(jnp.where(alive, gain, 0.0))
                rest = jnp.zeros((-local % 8, rows), jnp.float32)
                slots = jnp.dot(
                    jnp.concatenate(hits + [rest], axis=0).astype(jnp.bfloat16),
                    before,
                    preferred_element_type=jnp.float32,
                )
                mine, weighted = [], []
                for e in range(local):
                    hit = (slot_at == slots[e : e + 1]) & (hits[e] > 0.5)
                    mine.append(jnp.where(hit, 1.0, 0.0))
                    weighted.append(jnp.where(hit, gains[e], 0.0))
                choice = jnp.concatenate(mine, axis=0).astype(jnp.bfloat16)
                chosen[parity, q] = jnp.concatenate(weighted, axis=0).astype(jnp.bfloat16)

                def take(lanes):
                    rows_here = jnp.dot(choice, xb[k, :, lanes], preferred_element_type=jnp.float32)
                    rows_here = rows_here.astype(jnp.bfloat16)
                    for e in range(local):
                        picked[parity, e, place_of, lanes] = rows_here[e * cap : (e + 1) * cap]

                over(depth, 512, take)

            when_live(origin, choose)
            if live < chips:

                @pl.when(origin // 2 >= live)
                def _(place_of=place_of):
                    for e in range(local):
                        picked[parity, e, place_of, :] = jnp.zeros((cap, depth), jnp.bfloat16)

    def expert(b, e):
        parity = b % 2

        def hidden(lanes):
            mine = picked[parity, e]
            gate = jnp.dot(mine, wg[e, :, lanes], preferred_element_type=jnp.float32)
            up = jnp.dot(mine, wu[e, :, lanes], preferred_element_type=jnp.float32)
            acts[:, lanes] = (gate / (1.0 + jnp.exp(-gate)) * up).astype(jnp.bfloat16)

        def down(lanes):
            rows_here = jnp.dot(acts[...], wd[e, :, lanes], preferred_element_type=jnp.float32)
            picked[parity, e, :, lanes] = rows_here.astype(jnp.bfloat16)

        over(wg.shape[2], 256, hidden)
        over(depth, 512, down)

    def back(b):
        parity = b % 2
        for q in range(4):
            t = 2 * b + q // 2
            origin = own_origin(t) if q % 2 == 0 else sib_origin(t)

            def put(t=t, q=q):
                def spread(target, lanes):
                    rows_here = jnp.concatenate(
                        [picked[parity, e, q * cap : (q + 1) * cap, lanes] for e in range(local)],
                        axis=0,
                    )
                    target[:, lanes] = lax.dot_general(
                        chosen[parity, q], rows_here, (((0,), (0,)), ((), ())),
                        preferred_element_type=jnp.float32,
                    ).astype(jnp.bfloat16)

                if q % 2 == 0:
                    over(depth, 512, functools.partial(spread, part.at[t]))
                else:

                    @pl.when(t >= 2)
                    def _():
                        when_live(sib_origin(t - 2), give(t - 2).wait_send)

                    over(depth, 512, functools.partial(spread, away.at[t % 2]))
                    give(t).start()

            if q % 2 == 1 and live < chips:

                @pl.when((origin // 2 >= live) & (t >= 2))
                def _(t=t):
                    when_live(sib_origin(t - 2), give(t - 2).wait_send)

            when_live(origin, put)

    def scatter(t):
        slot = (t + 1) % chips

        def move():
            give(slot).wait_recv()
            for piece in range(pieces):
                here = span(piece)
                total = part[slot, here, :].astype(jnp.float32) + near_in[slot, here, :].astype(
                    jnp.float32
                )
                if not (isinstance(t, int) and t == 0):
                    pass_on(t - 1, piece).wait_recv()
                    total = total + ring_in[t - 1, here, :].astype(jnp.float32)
                if isinstance(t, int) and t == chips - 1:
                    o_ref[here, :] = (mixed[here, :] + total).astype(o_ref.dtype)
                else:
                    part[slot, here, :] = total.astype(part.dtype)
                    pass_on(t, piece).start()

        when_live(own_origin(slot), move)

    def unit(u, carry):
        @pl.when(u == chips - 2)
        def _():
            scatter(0)

        @pl.when(u < chips - 1)
        def _():
            tick(u)

        @pl.when(u < chips)
        def _():
            pick(u)

        @pl.when(u == 1)
        def _():
            for load in loads:
                load.wait()

        @pl.when(u >= 1)
        def _():
            expert((u - 1) // 2, (u - 1) % 2)

        @pl.when((u >= 1) & (u % 2 == 0))
        def _():
            back((u - 1) // 2)

        @pl.when(u == chips - 1)
        def _():
            scatter(1)

        @pl.when(u == chips)
        def _():
            scatter(2)

        return carry

    lax.fori_loop(0, chips + 1, unit, 0)

    def later(t, carry):
        scatter(t)
        return carry

    lax.fori_loop(3, chips - 1, later, 0)
    if live < chips:
        o_ref[...] = mixed[...].astype(o_ref.dtype)
    scatter(chips - 1)

    def settle(t, carry):
        def own():
            for piece in range(pieces):
                near(t, piece).wait_send()

                @pl.when(t < chips - 1)
                def _(piece=piece):
                    hop(t, piece).wait_send()

                @pl.when(t > 0)
                def _(piece=piece):
                    pass_on(t - 1, piece).wait_send()

        def sib():
            @pl.when(t >= chips - 2)
            def _():
                give(t).wait_send()

        when_live(own_origin(t), own)
        when_live(sib_origin(t), sib)
        return carry

    lax.fori_loop(0, chips, settle, 0)


def moe(count, x, mixed, routes, w_gate, w_up, w_down, devices, cap, live, collective_id, pieces=2):
    rows, depth = x.shape
    chips = devices // 2
    local = w_gate.shape[0]
    dma = pltpu.SemaphoreType.DMA
    both = dma((chips, pieces))
    hbm = pl.BlockSpec(memory_space=pltpu.HBM)
    vmem = pl.BlockSpec(memory_space=pltpu.VMEM)
    block = (rows, depth)
    half = jnp.bfloat16
    return pl.pallas_call(
        functools.partial(moe_kernel, devices, live, cap, pieces),
        out_shape=(
            jax.ShapeDtypeStruct(block, half),
            jax.ShapeDtypeStruct((devices,) + block, half),
        ),
        in_specs=[pl.BlockSpec(memory_space=pltpu.SMEM), hbm, hbm, vmem, hbm, hbm, hbm],
        out_specs=(vmem, hbm),
        scratch_shapes=[
            pltpu.VMEM(block, jnp.float32),
            pltpu.VMEM((4 * cap, w_gate.shape[2]), half),
            pltpu.VMEM(w_gate.shape, half),
            pltpu.VMEM(w_up.shape, half),
            pltpu.VMEM(w_down.shape, half),
            pltpu.VMEM((2,) + block, half),
            pltpu.VMEM((2, local, 4 * cap, depth), half),
            pltpu.VMEM((2, 4, local * cap, rows), half),
            pltpu.VMEM((chips,) + block, half),
            pltpu.VMEM((2,) + block, half),
            pltpu.VMEM((chips,) + block, half),
            pltpu.VMEM((chips - 1,) + block, half),
            dma((4,)),
            dma((2,)),
            both, both, both, both, both, both,
            dma((chips,)),
            dma((chips,)),
        ],
        compiler_params=pltpu.CompilerParams(
            collective_id=collective_id, has_side_effects=True, vmem_limit_bytes=63 << 20
        ),
    )(count, x, mixed, routes, w_gate, w_up, w_down)[0]


def per_device(
    hidden,
    query_rows,
    key_rows,
    value_rows,
    counts,
    out_weight,
    norm_gain,
    route_ids,
    route_weights,
    w_gate,
    w_up,
    w_down,
):
    devices = lax.axis_size("shard")
    me = lax.axis_index("shard")
    tok_dev, depth = hidden.shape
    topk = route_ids.shape[1]
    local = w_gate.shape[0]
    experts = local * devices
    capacity = max(2, tok_dev * topk * 5 // (4 * experts))
    capacity = -(-capacity // 16) * 16

    normed, mixed_rows, routes_all = front(
        counts, query_rows, key_rows, value_rows, route_ids.T, route_weights.T, out_weight, hidden,
        norm_gain, devices, 1,
    )
    return moe(
        counts, normed, mixed_rows, routes_all, w_gate, w_up, w_down, devices, capacity,
        devices // 2, 2,
    )


def solution(mesh):
    rows = P(("groups", "shard"), None)
    weights = P("shard", None, None)
    return jax.shard_map(
        per_device,
        mesh=mesh,
        in_specs=(
            rows,
            rows,
            rows,
            rows,
            P("groups"),
            P("shard", None),
            P(),
            rows,
            rows,
            weights,
            weights,
            weights,
        ),
        out_specs=rows,
        check_vma=False,
    )
```

```python
import functools
import math

import jax
import jax.numpy as jnp
from jax import lax
from jax.experimental import pallas as pl
from jax.experimental.pallas import tpu as pltpu
from jax.sharding import PartitionSpec as P

HD = 128
SEQ_LEN = 4096
NEG = -1e30
MESH = pl.DeviceIdType.MESH


def ring_place(chips, index):
    if chips == 8:
        z, y = index // 2, index % 2
        return z + y * (7 - 2 * z)
    return index


def ring_chip(chips, place):
    if chips == 8:
        half = place // 4
        z = place + half * (7 - 2 * place)
        return 2 * z + half
    return place


def front_kernel(
    devices, kv_count, heads,
    count_ref, q_ref, k_ref, v_ref, ids_ref, weights_ref, w_ref, hidden_ref, gain_ref,
    normed_ref, mixed_ref, allr,
    r_ref, allk, allv, allw, top, total, att,
    own_sem, kv_send, kv_recv, kn_send, kn_recv,
    w_send, w_recv, n_send, n_recv, x_send, x_recv, m_send, m_recv,
):
    chips = devices // 2
    me = lax.axis_index("shard")
    group = lax.axis_index("groups")
    core = me % 2
    way = 1 - 2 * core
    place = ring_place(chips, me // 2)
    rows = q_ref.shape[0]
    depth = w_ref.shape[1]
    scale = math.log2(math.e) / math.sqrt(HD)
    deep = w_ref.shape[0]
    lone = deep * 3 // 8 // 16 * 16
    shared = deep - 2 * lone
    side = group % 2
    partner = group + 1 - 2 * side

    def chip_at(offset):
        return ring_chip(chips, (place + offset + 2 * chips) % chips)

    def own_origin(t):
        return chip_at(-way * t) * 2 + core

    def sib_origin(t):
        return chip_at(way * t) * 2 + 1 - core

    ahead, behind, sibling = own_origin(-1), own_origin(1), me + way
    edge = deep - lone
    pieces = (pl.ds(pl.multiple_of(side * edge, 16), lone), pl.ds(lone, shared))
    theirs = pl.ds(pl.multiple_of((1 - side) * edge, 16), lone)
    small = ((k_ref, allk), (v_ref, allv), (r_ref, allr))

    def remote(src, dst, send, recv, to, to_group=None):
        return pltpu.make_async_remote_copy(
            src_ref=src, dst_ref=dst, send_sem=send, recv_sem=recv,
            device_id=(group if to_group is None else to_group, to), device_id_type=MESH,
        )

    def kv_hop(t, i, src=None):
        at = small[i][1].at[own_origin(t)]
        return remote(at if src is None else src, at, kv_send.at[t, i], kv_recv.at[t, i], ahead)

    def kv_landing(t, i):
        at = small[i][1].at[own_origin(t)]
        return remote(at, at, kv_send.at[t - 1, i], kv_recv.at[t - 1, i], ahead)

    def kv_near(t, i, src=None):
        at = small[i][1].at[own_origin(t)]
        return remote(at if src is None else src, at, kn_send.at[t, i], kn_recv.at[t, i], sibling)

    def kv_near_landing(t, i):
        at = small[i][1].at[sib_origin(t)]
        return remote(at, at, kn_send.at[t, i], kn_recv.at[t, i], sibling)

    def w_hop(t, i, src=None):
        at = allw.at[own_origin(t), pieces[i]]
        src = at if src is None else src.at[pieces[i]]
        return remote(src, at, w_send.at[t, i], w_recv.at[t, i], ahead)

    def w_landing(t, i):
        at = allw.at[own_origin(t), pieces[i]]
        return remote(at, at, w_send.at[t - 1, i], w_recv.at[t - 1, i], ahead)

    def w_near(t, i):
        at = allw.at[own_origin(t), pieces[i]]
        return remote(at, at, n_send.at[t, i], n_recv.at[t, i], sibling)

    def w_near_landing(t, i):
        at = allw.at[sib_origin(t), pieces[i]]
        return remote(at, at, n_send.at[t, i], n_recv.at[t, i], sibling)

    def w_near_all(origin, src):
        return remote(src, allw.at[origin], n_send.at[0, 0], n_recv.at[0, 0], sibling)

    def cross(t):
        at = allw.at[own_origin(t), pieces[0]]
        return remote(at, at, x_send.at[t], x_recv.at[t], me, partner)

    def cross_landing(t):
        at = allw.at[own_origin(t), theirs]
        return remote(at, at, x_send.at[t], x_recv.at[t], me, partner)

    def cross_near(t):
        at = allw.at[own_origin(t), theirs]
        return remote(at, at, m_send.at[t], m_recv.at[t], sibling)

    def cross_near_landing(t):
        at = allw.at[sib_origin(t), theirs]
        return remote(at, at, m_send.at[t], m_recv.at[t], sibling)

    own = [
        pltpu.make_async_copy(src, dst.at[me], own_sem.at[i])
        for i, (src, dst) in enumerate(small + ((w_ref, allw),))
    ]

    barrier = pltpu.get_barrier_semaphore()
    for other in (ahead, behind, sibling):
        pl.semaphore_signal(barrier, inc=1, device_id=(group, other), device_id_type=MESH)
    pl.semaphore_signal(barrier, inc=1, device_id=(partner, me), device_id_type=MESH)

    r_ref[...] = jnp.concatenate(
        [ids_ref[...].astype(jnp.float32), weights_ref[...].astype(jnp.float32)], axis=0
    ).astype(jnp.bfloat16)
    pl.semaphore_wait(barrier, 4)

    for i in range(3):
        kv_hop(0, i, small[i][0]).start()
    for i in range(3):
        kv_near(0, i, small[i][0]).start()
    for copy in own:
        copy.start()
    w_near_all(me, w_ref).start()

    def kv_tick(t):
        for i in range(3):
            kv_landing(t, i).wait_recv()

            @pl.when(t < chips - 1)
            def _(i=i):
                kv_hop(t, i).start()

            kv_near(t, i).start()

    def w_tick(t):
        for i in range(2):
            w_landing(t, i).wait_recv()

            @pl.when(t < chips - 1)
            def _(i=i):
                w_hop(t, i).start()

            if i == 0:
                cross(t).start()
            w_near(t, i).start()

        @pl.when(t > 1)
        def _():
            cross_tick(t - 1)

    def cross_tick(t):
        cross_landing(t).wait_recv()
        cross_near(t).start()

    apart = lax.broadcasted_iota(jnp.int32, (rows, rows), 1) - lax.broadcasted_iota(
        jnp.int32, (rows, rows), 0
    )
    cut = 2
    part_heads = heads // cut
    per_set = kv_count * cut

    def fold(n, g, part, first, masked):
        origins = []
        for t in (2 * n, 2 * n + 1):
            origins += [own_origin(t), sib_origin(t)]
        lanes = pl.ds(pl.multiple_of(g * HD, HD), HD)
        keys = jnp.concatenate([allk[o, :, lanes] for o in origins], axis=0)
        values = jnp.concatenate([allv[o, :, lanes] for o in origins], axis=0)
        values = jnp.concatenate([values, jnp.ones(values.shape, jnp.bfloat16)], axis=1)
        width = part_heads * HD
        q_here = q_ref[:, pl.ds(pl.multiple_of((g * cut + part) * width, width), width)]

        def scores_of(h):
            scores = lax.dot_general(
                q_here[:, h * HD : (h + 1) * HD], keys, (((1,), (1,)), ((), ())),
                preferred_element_type=jnp.float32,
            )
            if not masked:
                return scores
            return jnp.concatenate(
                [
                    jnp.where(apart <= (me - o) * rows, scores[:, j * rows : (j + 1) * rows], NEG)
                    for j, o in enumerate(origins)
                ],
                axis=1,
            )

        later = scores_of(0)
        for h in range(part_heads):
            at = (g * cut + part) * part_heads + h
            scores = later
            if h + 1 < part_heads:
                later = scores_of(h + 1)
            new = jnp.max(scores, axis=1, keepdims=True) * scale
            if first:
                new = jnp.broadcast_to(new, (rows, HD))
            else:
                old = top[at]
                new = jnp.maximum(old, new)
            expo = jnp.exp2(scores * scale - new[:, :1]).astype(jnp.bfloat16)
            both = jnp.dot(expo, values, preferred_element_type=jnp.float32)
            if not first:
                factor = jnp.exp2(old - new)
                both = total[at] * jnp.concatenate([factor, factor], axis=1) + both
            total[at] = both
            top[at] = new

    segments = chips // 2 * per_set
    lag = 3

    kv_tick(1)
    for copy in own:
        copy.wait()

    def segment(i, carry):
        n = i // per_set
        g = (i % per_set) // cut
        part = i % cut

        turn = i % per_set
        early, late = per_set // 2 - 1, per_set - 1
        t = jnp.where(turn == late, 2 * n + 3, 2 * n + 2)
        ticks = (turn == early) | (turn == late)

        @pl.when(ticks & (t < chips))
        def _():
            kv_tick(t)

        @pl.when(ticks & (t == lag))
        def _():
            for k in range(2):
                w_hop(0, k, w_ref).start()

        @pl.when(ticks & (t > lag))
        def _():
            w_tick(t - lag)

        @pl.when(i % per_set == 0)
        def _():
            for slot in (2 * n, 2 * n + 1):
                for k in range(3):
                    kv_near_landing(slot, k).wait_recv()

        some, every = False, True
        for slot in (2 * n, 2 * n + 1):
            for o in (own_origin(slot), sib_origin(slot)):
                some = (o <= me) | some
                every = (o < me) & every

        @pl.when(n == 0)
        def _():
            fold(n, g, part, True, True)

        @pl.when((n > 0) & every)
        def _():
            fold(n, g, part, False, False)

        @pl.when((n > 0) & some & jnp.logical_not(every))
        def _():
            fold(n, g, part, False, True)

        return carry

    lax.fori_loop(0, segments, segment, 0)

    alive = me * rows + lax.broadcasted_iota(jnp.int32, (rows, HD), 0) < count_ref[0]

    def close(at, carry):
        both = total[at]
        result = jnp.where(alive, both[:, :HD] / jnp.where(alive, both[:, HD:], 1.0), 0.0)
        att[:, pl.ds(pl.multiple_of(at * HD, HD), HD)] = result.astype(jnp.bfloat16)
        return carry

    sets = chips // 2
    tile = 256

    def project(b):
        for t in (2 * b, 2 * b + 1):

            @pl.when(t == 0)
            def _():
                w_near_all(sibling, allw.at[sibling]).wait_recv()

            @pl.when(t > 0)
            def _(t=t):
                for i in range(2):
                    w_near_landing(t, i).wait_recv()
                cross_near_landing(t).wait_recv()

        origins = []
        for t in (2 * b, 2 * b + 1):
            origins += [own_origin(t), sib_origin(t)]
        left = jnp.concatenate(
            [att[:, pl.ds(pl.multiple_of(o * deep, deep), deep)] for o in origins], axis=1
        )

        def column(c, carry):
            lanes = pl.ds(pl.multiple_of(c * tile, tile), tile)
            right = jnp.concatenate([allw[o, :, lanes] for o in origins], axis=0)
            mixed_ref[:, lanes] += jnp.dot(left, right, preferred_element_type=jnp.float32)
            return carry

        lax.fori_loop(0, depth // tile, column, 0)

    lax.fori_loop(0, kv_count * heads, close, 0)
    mixed_ref[...] = hidden_ref[...].astype(jnp.float32)

    def tail(b, carry):
        @pl.when(b == sets - 2)
        def _():
            w_tick(chips - 1)

        @pl.when(b == sets - 1)
        def _():
            cross_tick(chips - 1)

        project(b)
        return carry

    lax.fori_loop(0, sets, tail, 0)

    step = 32
    gain = gain_ref[...].astype(jnp.float32).reshape(1, depth)

    def norm(c, carry):
        here = pl.ds(pl.multiple_of(c * step, step), step)
        mixed = mixed_ref[here, :]
        mean_square = jnp.mean(mixed * mixed, axis=1, keepdims=True)
        normed_ref[here, :] = (mixed * lax.rsqrt(mean_square + 1e-06) * gain).astype(jnp.bfloat16)
        return carry

    lax.fori_loop(0, rows // step, norm, 0)

    w_near_all(sibling, w_ref).wait_send()
    for i in range(2):
        w_hop(0, i, w_ref).wait_send()
    for i in range(3):
        kv_hop(0, i).wait_send()
        kv_near(0, i).wait_send()

    def settle(t, carry):
        for i in range(3):
            kv_near(t, i).wait_send()
        cross(t).wait_send()
        for i in range(2):
            w_near(t, i).wait_send()
        cross_near(t).wait_send()

        @pl.when(t < chips - 1)
        def _():
            for i in range(3):
                kv_hop(t, i).wait_send()
            for i in range(2):
                w_hop(t, i).wait_send()

        return carry

    lax.fori_loop(1, chips, settle, 0)


def front(count, q, k, v, ids, weights, w, hidden, gain, devices, collective_id):
    rows, width = q.shape
    depth = w.shape[1]
    chips = devices // 2
    kv_count = k.shape[1] // HD
    all_heads = width // HD
    half = jnp.bfloat16
    dma = pltpu.SemaphoreType.DMA
    hbm = pl.BlockSpec(memory_space=pltpu.HBM)
    vmem = pl.BlockSpec(memory_space=pltpu.VMEM)
    return pl.pallas_call(
        functools.partial(front_kernel, devices, kv_count, all_heads // kv_count),
        out_shape=(
            jax.ShapeDtypeStruct(hidden.shape, half),
            jax.ShapeDtypeStruct(hidden.shape, jnp.float32),
            jax.ShapeDtypeStruct((devices, 2 * ids.shape[0], rows), half),
        ),
        in_specs=[pl.BlockSpec(memory_space=pltpu.SMEM), vmem, hbm, hbm, vmem, vmem, hbm, vmem, vmem],
        out_specs=(vmem, vmem, vmem),
        scratch_shapes=[
            pltpu.VMEM((2 * ids.shape[0], rows), half),
            pltpu.VMEM((devices,) + k.shape, half),
            pltpu.VMEM((devices,) + v.shape, half),
            pltpu.VMEM((devices,) + w.shape, half),
            pltpu.VMEM((all_heads, rows, HD), jnp.float32),
            pltpu.VMEM((all_heads, rows, 2 * HD), jnp.float32),
            pltpu.VMEM((rows, width), half),
            dma((4,)),
        ]
        + [dma((chips, 3))] * 4
        + [dma((chips, 2))] * 4
        + [dma((chips,))] * 4,
        compiler_params=pltpu.CompilerParams(
            collective_id=collective_id, has_side_effects=True, vmem_limit_bytes=62 << 20
        ),
    )(count, q, k, v, ids, weights, w, hidden, gain)


def moe_kernel(
    devices, live, cap, pieces,
    count_ref, x_ref, mixed_ref, route_ref, wg_ref, wu_ref, wd_ref, o_ref, all_ref,
    mixed, wg, wu, wd, xb, picked, chosen, part, away, near_in, ring_in,
    w_sem, x_sem, g_send, g_recv, n_send, n_recv, s_send, s_recv, a_send, a_recv,
):
    chips = devices // 2
    me = lax.axis_index("shard")
    group = lax.axis_index("groups")
    core = me % 2
    way = 1 - 2 * core
    place = ring_place(chips, me // 2)
    rows, depth = x_ref.shape
    local = wg.shape[0]
    topk = route_ref.shape[1] // 2

    def chip_at(offset):
        return ring_chip(chips, (place + offset + 2 * chips) % chips)

    def own_origin(t):
        return chip_at(-way * t) * 2 + core

    def sib_origin(t):
        return chip_at(way * t) * 2 + 1 - core

    def when_live(origin, action):
        if live == chips:
            action()
        else:
            pl.when(origin // 2 < live)(action)

    ahead, behind, sibling = own_origin(-1), own_origin(1), me + way

    def span(piece):
        size = rows // pieces
        return pl.ds(piece * size, size)

    def remote(src, dst, send, recv, to):
        return pltpu.make_async_remote_copy(
            src_ref=src, dst_ref=dst, send_sem=send, recv_sem=recv,
            device_id=(group, to), device_id_type=MESH,
        )

    def hop(t, piece, src=None):
        place_of = all_ref.at[own_origin(t), span(piece)]
        src = place_of if src is None else src.at[span(piece)]
        return remote(src, place_of, g_send.at[t, piece], g_recv.at[t, piece], ahead)

    def near(t, piece, src=None):
        place_of = all_ref.at[own_origin(t), span(piece)]
        src = place_of if src is None else src.at[span(piece)]
        return remote(src, place_of, n_send.at[t, piece], n_recv.at[t, piece], sibling)

    def near_landing(t, piece):
        place_of = all_ref.at[sib_origin(t), span(piece)]
        return remote(place_of, place_of, n_send.at[t, piece], n_recv.at[t, piece], sibling)

    def landing(t, piece):
        place_of = all_ref.at[own_origin(t + 1), span(piece)]
        return remote(place_of, place_of, g_send.at[t, piece], g_recv.at[t, piece], ahead)

    def give(t):
        return remote(away.at[t % 2], near_in.at[t], a_send.at[t], a_recv.at[t], sibling)

    def pass_on(t, piece):
        return remote(
            part.at[t + 1, span(piece)], ring_in.at[t, span(piece)],
            s_send.at[t, piece], s_recv.at[t, piece], ahead,
        )

    loads = [
        pltpu.make_async_copy(src, dst, w_sem.at[i])
        for i, (src, dst) in enumerate(
            ((wg_ref, wg), (wu_ref, wu), (wd_ref, wd), (mixed_ref, mixed))
        )
    ]

    barrier = pltpu.get_barrier_semaphore()
    for other in (ahead, behind, sibling):
        pl.semaphore_signal(barrier, inc=1, device_id=(group, other), device_id_type=MESH)
    pl.semaphore_wait(barrier, 3)

    def begin():
        for piece in range(pieces):
            hop(0, piece, x_ref).start()
        for piece in range(pieces):
            near(0, piece, x_ref).start()

    when_live(me, begin)
    for load in loads:
        load.start()

    def tick(t):
        def move():
            for piece in range(pieces):
                landing(t, piece).wait_recv()

                @pl.when(t + 1 < chips - 1)
                def _(piece=piece):
                    hop(t + 1, piece).start()

                near(t + 1, piece).start()

        when_live(own_origin(t + 1), move)

    def pick(t):
        parity = (t // 2) % 2

        def fetch(k, origin):
            return pltpu.make_async_copy(all_ref.at[origin], xb.at[k], x_sem.at[k])

        def fetch_own():
            @pl.when(t == 0)
            def _():
                pltpu.make_async_copy(x_ref, xb.at[0], x_sem.at[0]).start()

            @pl.when(t > 0)
            def _():
                fetch(0, own_origin(t)).start()

        def fetch_sib():
            for piece in range(pieces):
                near_landing(t, piece).wait_recv()
            fetch(1, sib_origin(t)).start()

        when_live(own_origin(t), fetch_own)
        when_live(sib_origin(t), fetch_sib)
        before = (
            lax.broadcasted_iota(jnp.int32, (rows, rows), 0)
            < lax.broadcasted_iota(jnp.int32, (rows, rows), 1)
        ).astype(jnp.bfloat16)
        slot_at = lax.broadcasted_iota(jnp.int32, (cap, rows), 0).astype(jnp.float32)
        for k, origin in ((0, own_origin(t)), (1, sib_origin(t))):
            q = 2 * (t % 2) + k
            place_of = pl.ds(pl.multiple_of(q * cap, 16), cap)

            def choose(k=k, origin=origin, q=q, place_of=place_of):
                fetch(k, origin).wait()
                route = route_ref[origin].astype(jnp.float32)
                ids, weights = route[:topk], route[topk:]
                at = origin * rows + lax.broadcasted_iota(jnp.int32, (1, rows), 1)
                alive = at < count_ref[0]
                hits, gains = [], []
                for e in range(local):
                    match = ids == (me * local + e).astype(jnp.float32)
                    hits.append(jnp.sum(jnp.where(match, 1.0, 0.0), axis=0, keepdims=True))
                    gain = jnp.sum(jnp.where(match, weights, 0.0), axis=0, keepdims=True)
                    gains.append(jnp.where(alive, gain, 0.0))
                rest = jnp.zeros((-local % 8, rows), jnp.float32)
                slots = jnp.dot(
                    jnp.concatenate(hits + [rest], axis=0).astype(jnp.bfloat16),
                    before,
                    preferred_element_type=jnp.float32,
                )
                mine, weighted = [], []
                for e in range(local):
                    hit = (slot_at == slots[e : e + 1]) & (hits[e] > 0.5)
                    mine.append(jnp.where(hit, 1.0, 0.0))
                    weighted.append(jnp.where(hit, gains[e], 0.0))
                choice = jnp.concatenate(mine, axis=0).astype(jnp.bfloat16)
                chosen[parity, q] = jnp.concatenate(weighted, axis=0).astype(jnp.bfloat16)
                rows_here = jnp.dot(choice, xb[k], preferred_element_type=jnp.float32)
                rows_here = rows_here.astype(jnp.bfloat16)
                for e in range(local):
                    picked[parity, e, place_of, :] = rows_here[e * cap : (e + 1) * cap]

            when_live(origin, choose)
            if live < chips:

                @pl.when(origin // 2 >= live)
                def _(place_of=place_of):
                    for e in range(local):
                        picked[parity, e, place_of, :] = jnp.zeros((cap, depth), jnp.bfloat16)

    def expert(b, e):
        parity = b % 2
        mine = picked[parity, e]
        gate = jnp.dot(mine, wg[e], preferred_element_type=jnp.float32)
        up = jnp.dot(mine, wu[e], preferred_element_type=jnp.float32)
        act = (gate / (1.0 + jnp.exp(-gate)) * up).astype(jnp.bfloat16)
        down = jnp.dot(act, wd[e], preferred_element_type=jnp.float32)
        picked[parity, e] = down.astype(jnp.bfloat16)

    def back(b):
        parity = b % 2
        for q in range(4):
            t = 2 * b + q // 2
            origin = own_origin(t) if q % 2 == 0 else sib_origin(t)

            def put(t=t, q=q):
                rows_here = jnp.concatenate(
                    [picked[parity, e, q * cap : (q + 1) * cap, :] for e in range(local)], axis=0
                )
                total = lax.dot_general(
                    chosen[parity, q], rows_here, (((0,), (0,)), ((), ())),
                    preferred_element_type=jnp.float32,
                ).astype(jnp.bfloat16)
                if q % 2 == 0:
                    part[t] = total
                else:

                    @pl.when(t >= 2)
                    def _():
                        when_live(sib_origin(t - 2), give(t - 2).wait_send)

                    away[t % 2] = total
                    give(t).start()

            if q % 2 == 1 and live < chips:

                @pl.when((origin // 2 >= live) & (t >= 2))
                def _(t=t):
                    when_live(sib_origin(t - 2), give(t - 2).wait_send)

            when_live(origin, put)

    def scatter(t):
        slot = (t + 1) % chips

        def move():
            give(slot).wait_recv()
            for piece in range(pieces):
                here = span(piece)
                total = part[slot, here, :].astype(jnp.float32) + near_in[slot, here, :].astype(
                    jnp.float32
                )
                if not (isinstance(t, int) and t == 0):
                    pass_on(t - 1, piece).wait_recv()
                    total = total + ring_in[t - 1, here, :].astype(jnp.float32)
                if isinstance(t, int) and t == chips - 1:
                    o_ref[here, :] = (mixed[here, :] + total).astype(o_ref.dtype)
                else:
                    part[slot, here, :] = total.astype(part.dtype)
                    pass_on(t, piece).start()

        when_live(own_origin(slot), move)

    def unit(u, carry):
        @pl.when(u == chips - 2)
        def _():
            scatter(0)

        @pl.when(u < chips - 1)
        def _():
            tick(u)

        @pl.when(u < chips)
        def _():
            pick(u)

        @pl.when(u == 1)
        def _():
            for load in loads:
                load.wait()

        @pl.when(u >= 1)
        def _():
            expert((u - 1) // 2, (u - 1) % 2)

        @pl.when((u >= 1) & (u % 2 == 0))
        def _():
            back((u - 1) // 2)

        @pl.when(u == chips - 1)
        def _():
            scatter(1)

        @pl.when(u == chips)
        def _():
            scatter(2)

        return carry

    lax.fori_loop(0, chips + 1, unit, 0)

    def later(t, carry):
        scatter(t)
        return carry

    lax.fori_loop(3, chips - 1, later, 0)
    if live < chips:
        o_ref[...] = mixed[...].astype(o_ref.dtype)
    scatter(chips - 1)

    def settle(t, carry):
        def own():
            for piece in range(pieces):
                near(t, piece).wait_send()

                @pl.when(t < chips - 1)
                def _(piece=piece):
                    hop(t, piece).wait_send()

                @pl.when(t > 0)
                def _(piece=piece):
                    pass_on(t - 1, piece).wait_send()

        def sib():
            @pl.when(t >= chips - 2)
            def _():
                give(t).wait_send()

        when_live(own_origin(t), own)
        when_live(sib_origin(t), sib)
        return carry

    lax.fori_loop(0, chips, settle, 0)


def moe(count, x, mixed, routes, w_gate, w_up, w_down, devices, cap, live, collective_id, pieces=2):
    rows, depth = x.shape
    chips = devices // 2
    local = w_gate.shape[0]
    dma = pltpu.SemaphoreType.DMA
    both = dma((chips, pieces))
    hbm = pl.BlockSpec(memory_space=pltpu.HBM)
    vmem = pl.BlockSpec(memory_space=pltpu.VMEM)
    block = (rows, depth)
    half = jnp.bfloat16
    return pl.pallas_call(
        functools.partial(moe_kernel, devices, live, cap, pieces),
        out_shape=(
            jax.ShapeDtypeStruct(block, half),
            jax.ShapeDtypeStruct((devices,) + block, half),
        ),
        in_specs=[pl.BlockSpec(memory_space=pltpu.SMEM), hbm, hbm, vmem, hbm, hbm, hbm],
        out_specs=(vmem, hbm),
        scratch_shapes=[
            pltpu.VMEM(block, jnp.float32),
            pltpu.VMEM(w_gate.shape, half),
            pltpu.VMEM(w_up.shape, half),
            pltpu.VMEM(w_down.shape, half),
            pltpu.VMEM((2,) + block, half),
            pltpu.VMEM((2, local, 4 * cap, depth), half),
            pltpu.VMEM((2, 4, local * cap, rows), half),
            pltpu.VMEM((chips,) + block, half),
            pltpu.VMEM((2,) + block, half),
            pltpu.VMEM((chips,) + block, half),
            pltpu.VMEM((chips - 1,) + block, half),
            dma((4,)),
            dma((2,)),
            both, both, both, both, both, both,
            dma((chips,)),
            dma((chips,)),
        ],
        compiler_params=pltpu.CompilerParams(
            collective_id=collective_id, has_side_effects=True, vmem_limit_bytes=63 << 20
        ),
    )(count, x, mixed, routes, w_gate, w_up, w_down)[0]


def per_device(
    hidden,
    query_rows,
    key_rows,
    value_rows,
    counts,
    out_weight,
    norm_gain,
    route_ids,
    route_weights,
    w_gate,
    w_up,
    w_down,
):
    devices = lax.axis_size("shard")
    me = lax.axis_index("shard")
    tok_dev, depth = hidden.shape
    topk = route_ids.shape[1]
    local = w_gate.shape[0]
    experts = local * devices
    capacity = max(2, tok_dev * topk * 5 // (4 * experts))
    capacity = -(-capacity // 16) * 16

    normed, mixed_rows, routes_all = front(
        counts, query_rows, key_rows, value_rows, route_ids.T, route_weights.T, out_weight, hidden,
        norm_gain, devices, 1,
    )
    return moe(
        counts, normed, mixed_rows, routes_all, w_gate, w_up, w_down, devices, capacity,
        devices // 2, 2,
    )


def solution(mesh):
    rows = P(("groups", "shard"), None)
    weights = P("shard", None, None)
    return jax.shard_map(
        per_device,
        mesh=mesh,
        in_specs=(
            rows,
            rows,
            rows,
            rows,
            P("groups"),
            P("shard", None),
            P(),
            rows,
            rows,
            weights,
            weights,
            weights,
        ),
        out_specs=rows,
        check_vma=False,
    )
```

```python
import functools
import math

import jax
import jax.numpy as jnp
from jax import lax
from jax.experimental import pallas as pl
from jax.experimental.pallas import tpu as pltpu
from jax.sharding import PartitionSpec as P

HD = 128
SEQ_LEN = 4096
NEG = -1e30
MESH = pl.DeviceIdType.MESH


def ring_place(chips, index):
    if chips == 8:
        z, y = index // 2, index % 2
        return z + y * (7 - 2 * z)
    return index


def ring_chip(chips, place):
    if chips == 8:
        half = place // 4
        z = place + half * (7 - 2 * place)
        return 2 * z + half
    return place


def front_kernel(
    devices, kv_count, heads,
    count_ref, q_ref, k_ref, v_ref, ids_ref, weights_ref, w_ref, hidden_ref, gain_ref,
    normed_ref, mixed_ref, allr,
    r_ref, allk, allv, allw, top, total, att,
    own_sem, kv_send, kv_recv, kn_send, kn_recv,
    w_send, w_recv, n_send, n_recv, x_send, x_recv, m_send, m_recv,
):
    chips = devices // 2
    me = lax.axis_index("shard")
    group = lax.axis_index("groups")
    core = me % 2
    way = 1 - 2 * core
    place = ring_place(chips, me // 2)
    rows = q_ref.shape[0]
    depth = w_ref.shape[1]
    scale = math.log2(math.e) / math.sqrt(HD)
    deep = w_ref.shape[0]
    lone = deep * 3 // 8 // 16 * 16
    shared = deep - 2 * lone
    side = group % 2
    partner = group + 1 - 2 * side

    def chip_at(offset):
        return ring_chip(chips, (place + offset + 2 * chips) % chips)

    def own_origin(t):
        return chip_at(-way * t) * 2 + core

    def sib_origin(t):
        return chip_at(way * t) * 2 + 1 - core

    ahead, behind, sibling = own_origin(-1), own_origin(1), me + way
    edge = deep - lone
    pieces = (pl.ds(pl.multiple_of(side * edge, 16), lone), pl.ds(lone, shared))
    theirs = pl.ds(pl.multiple_of((1 - side) * edge, 16), lone)
    small = ((k_ref, allk), (v_ref, allv), (r_ref, allr))

    def remote(src, dst, send, recv, to, to_group=None):
        return pltpu.make_async_remote_copy(
            src_ref=src, dst_ref=dst, send_sem=send, recv_sem=recv,
            device_id=(group if to_group is None else to_group, to), device_id_type=MESH,
        )

    def kv_hop(t, i, src=None):
        at = small[i][1].at[own_origin(t)]
        return remote(at if src is None else src, at, kv_send.at[t, i], kv_recv.at[t, i], ahead)

    def kv_landing(t, i):
        at = small[i][1].at[own_origin(t)]
        return remote(at, at, kv_send.at[t - 1, i], kv_recv.at[t - 1, i], ahead)

    def kv_near(t, i, src=None):
        at = small[i][1].at[own_origin(t)]
        return remote(at if src is None else src, at, kn_send.at[t, i], kn_recv.at[t, i], sibling)

    def kv_near_landing(t, i):
        at = small[i][1].at[sib_origin(t)]
        return remote(at, at, kn_send.at[t, i], kn_recv.at[t, i], sibling)

    def w_hop(t, i, src=None):
        at = allw.at[own_origin(t), pieces[i]]
        src = at if src is None else src.at[pieces[i]]
        return remote(src, at, w_send.at[t, i], w_recv.at[t, i], ahead)

    def w_landing(t, i):
        at = allw.at[own_origin(t), pieces[i]]
        return remote(at, at, w_send.at[t - 1, i], w_recv.at[t - 1, i], ahead)

    def w_near(t, i):
        at = allw.at[own_origin(t), pieces[i]]
        return remote(at, at, n_send.at[t, i], n_recv.at[t, i], sibling)

    def w_near_landing(t, i):
        at = allw.at[sib_origin(t), pieces[i]]
        return remote(at, at, n_send.at[t, i], n_recv.at[t, i], sibling)

    def w_near_all(origin, src):
        return remote(src, allw.at[origin], n_send.at[0, 0], n_recv.at[0, 0], sibling)

    def cross(t):
        at = allw.at[own_origin(t), pieces[0]]
        return remote(at, at, x_send.at[t], x_recv.at[t], me, partner)

    def cross_landing(t):
        at = allw.at[own_origin(t), theirs]
        return remote(at, at, x_send.at[t], x_recv.at[t], me, partner)

    def cross_near(t):
        at = allw.at[own_origin(t), theirs]
        return remote(at, at, m_send.at[t], m_recv.at[t], sibling)

    def cross_near_landing(t):
        at = allw.at[sib_origin(t), theirs]
        return remote(at, at, m_send.at[t], m_recv.at[t], sibling)

    own = [
        pltpu.make_async_copy(src, dst.at[me], own_sem.at[i])
        for i, (src, dst) in enumerate(small + ((w_ref, allw),))
    ]

    barrier = pltpu.get_barrier_semaphore()
    for other in (ahead, behind, sibling):
        pl.semaphore_signal(barrier, inc=1, device_id=(group, other), device_id_type=MESH)
    pl.semaphore_signal(barrier, inc=1, device_id=(partner, me), device_id_type=MESH)

    r_ref[...] = jnp.concatenate(
        [ids_ref[...].astype(jnp.float32), weights_ref[...].astype(jnp.float32)], axis=0
    ).astype(jnp.bfloat16)
    pl.semaphore_wait(barrier, 4)

    for i in range(3):
        kv_hop(0, i, small[i][0]).start()
    for i in range(3):
        kv_near(0, i, small[i][0]).start()
    for copy in own:
        copy.start()
    w_near_all(me, w_ref).start()

    def kv_tick(t):
        for i in range(3):
            kv_landing(t, i).wait_recv()

            @pl.when(t < chips - 1)
            def _(i=i):
                kv_hop(t, i).start()

            kv_near(t, i).start()

    def w_tick(t):
        for i in range(2):
            w_landing(t, i).wait_recv()

            @pl.when(t < chips - 1)
            def _(i=i):
                w_hop(t, i).start()

            if i == 0:
                cross(t).start()
            w_near(t, i).start()

        @pl.when(t > 1)
        def _():
            cross_tick(t - 1)

    def cross_tick(t):
        cross_landing(t).wait_recv()
        cross_near(t).start()

    apart = lax.broadcasted_iota(jnp.int32, (rows, rows), 1) - lax.broadcasted_iota(
        jnp.int32, (rows, rows), 0
    )
    cut = 2
    part_heads = heads // cut
    per_set = kv_count * cut

    def fold(n, g, part, first, masked):
        origins = []
        for t in (2 * n, 2 * n + 1):
            origins += [own_origin(t), sib_origin(t)]
        lanes = pl.ds(pl.multiple_of(g * HD, HD), HD)
        keys = jnp.concatenate([allk[o, :, lanes] for o in origins], axis=0)
        values = jnp.concatenate([allv[o, :, lanes] for o in origins], axis=0)
        values = jnp.concatenate([values, jnp.ones(values.shape, jnp.bfloat16)], axis=1)
        width = part_heads * HD
        q_here = q_ref[:, pl.ds(pl.multiple_of((g * cut + part) * width, width), width)]

        def scores_of(h):
            scores = lax.dot_general(
                q_here[:, h * HD : (h + 1) * HD], keys, (((1,), (1,)), ((), ())),
                preferred_element_type=jnp.float32,
            )
            if not masked:
                return scores
            return jnp.concatenate(
                [
                    jnp.where(apart <= (me - o) * rows, scores[:, j * rows : (j + 1) * rows], NEG)
                    for j, o in enumerate(origins)
                ],
                axis=1,
            )

        later = scores_of(0)
        for h in range(part_heads):
            at = (g * cut + part) * part_heads + h
            scores = later
            if h + 1 < part_heads:
                later = scores_of(h + 1)
            new = jnp.max(scores, axis=1, keepdims=True) * scale
            if first:
                new = jnp.broadcast_to(new, (rows, HD))
            else:
                old = top[at]
                new = jnp.maximum(old, new)
            expo = jnp.exp2(scores * scale - new[:, :1]).astype(jnp.bfloat16)
            both = jnp.dot(expo, values, preferred_element_type=jnp.float32)
            if not first:
                factor = jnp.exp2(old - new)
                both = total[at] * jnp.concatenate([factor, factor], axis=1) + both
            total[at] = both
            top[at] = new

    segments = chips // 2 * per_set

    kv_tick(1)
    for copy in own:
        copy.wait()

    def segment(i, carry):
        n = i // per_set
        g = (i % per_set) // cut
        part = i % cut

        turn = i % per_set
        early, late = per_set // 2 - 1, per_set - 1
        t = jnp.where(turn == late, 2 * n + 3, 2 * n + 2)
        ticks = (turn == early) | (turn == late)

        @pl.when(ticks & (t < chips))
        def _():
            kv_tick(t)

        swift = (turn == early // 2) | (turn == early + 2)
        w_turn = 2 * n + jnp.where(turn == early + 2, 1, 0)

        @pl.when(swift & (w_turn == 1))
        def _():
            for k in range(2):
                w_hop(0, k, w_ref).start()

        @pl.when(swift & (w_turn > 1))
        def _():
            w_tick(w_turn - 1)

        @pl.when(i % per_set == 0)
        def _():
            for slot in (2 * n, 2 * n + 1):
                for k in range(3):
                    kv_near_landing(slot, k).wait_recv()

        some, every = False, True
        for slot in (2 * n, 2 * n + 1):
            for o in (own_origin(slot), sib_origin(slot)):
                some = (o <= me) | some
                every = (o < me) & every

        @pl.when(n == 0)
        def _():
            fold(n, g, part, True, True)

        @pl.when((n > 0) & every)
        def _():
            fold(n, g, part, False, False)

        @pl.when((n > 0) & some & jnp.logical_not(every))
        def _():
            fold(n, g, part, False, True)

        return carry

    lax.fori_loop(0, segments, segment, 0)

    alive = me * rows + lax.broadcasted_iota(jnp.int32, (rows, HD), 0) < count_ref[0]

    def close(at, carry):
        both = total[at]
        result = jnp.where(alive, both[:, :HD] / jnp.where(alive, both[:, HD:], 1.0), 0.0)
        att[:, pl.ds(pl.multiple_of(at * HD, HD), HD)] = result.astype(jnp.bfloat16)
        return carry

    sets = chips // 2
    tile = 256

    def project(b):
        for t in (2 * b, 2 * b + 1):

            @pl.when(t == 0)
            def _():
                w_near_all(sibling, allw.at[sibling]).wait_recv()

            @pl.when(t > 0)
            def _(t=t):
                for i in range(2):
                    w_near_landing(t, i).wait_recv()
                cross_near_landing(t).wait_recv()

        origins = []
        for t in (2 * b, 2 * b + 1):
            origins += [own_origin(t), sib_origin(t)]
        left = jnp.concatenate(
            [att[:, pl.ds(pl.multiple_of(o * deep, deep), deep)] for o in origins], axis=1
        )

        def column(c, carry):
            lanes = pl.ds(pl.multiple_of(c * tile, tile), tile)
            right = jnp.concatenate([allw[o, :, lanes] for o in origins], axis=0)
            mixed_ref[:, lanes] += jnp.dot(left, right, preferred_element_type=jnp.float32)
            return carry

        lax.fori_loop(0, depth // tile, column, 0)

    lax.fori_loop(0, kv_count * heads, close, 0)
    mixed_ref[...] = hidden_ref[...].astype(jnp.float32)

    def tail(b, carry):
        @pl.when(b == max(sets - 3, 0))
        def _():
            w_tick(chips - 1)

        @pl.when(b == sets - 1)
        def _():
            cross_tick(chips - 1)

        project(b)
        return carry

    lax.fori_loop(0, sets, tail, 0)

    step = 32
    gain = gain_ref[...].astype(jnp.float32).reshape(1, depth)

    def norm(c, carry):
        here = pl.ds(pl.multiple_of(c * step, step), step)
        mixed = mixed_ref[here, :]
        mean_square = jnp.mean(mixed * mixed, axis=1, keepdims=True)
        normed_ref[here, :] = (mixed * lax.rsqrt(mean_square + 1e-06) * gain).astype(jnp.bfloat16)
        return carry

    lax.fori_loop(0, rows // step, norm, 0)

    w_near_all(sibling, w_ref).wait_send()
    for i in range(2):
        w_hop(0, i, w_ref).wait_send()
    for i in range(3):
        kv_hop(0, i).wait_send()
        kv_near(0, i).wait_send()

    def settle(t, carry):
        for i in range(3):
            kv_near(t, i).wait_send()
        cross(t).wait_send()
        for i in range(2):
            w_near(t, i).wait_send()
        cross_near(t).wait_send()

        @pl.when(t < chips - 1)
        def _():
            for i in range(3):
                kv_hop(t, i).wait_send()
            for i in range(2):
                w_hop(t, i).wait_send()

        return carry

    lax.fori_loop(1, chips, settle, 0)


def front(count, q, k, v, ids, weights, w, hidden, gain, devices, collective_id):
    rows, width = q.shape
    depth = w.shape[1]
    chips = devices // 2
    kv_count = k.shape[1] // HD
    all_heads = width // HD
    half = jnp.bfloat16
    dma = pltpu.SemaphoreType.DMA
    hbm = pl.BlockSpec(memory_space=pltpu.HBM)
    vmem = pl.BlockSpec(memory_space=pltpu.VMEM)
    return pl.pallas_call(
        functools.partial(front_kernel, devices, kv_count, all_heads // kv_count),
        out_shape=(
            jax.ShapeDtypeStruct(hidden.shape, half),
            jax.ShapeDtypeStruct(hidden.shape, jnp.float32),
            jax.ShapeDtypeStruct((devices, 2 * ids.shape[0], rows), half),
        ),
        in_specs=[pl.BlockSpec(memory_space=pltpu.SMEM), vmem, hbm, hbm, vmem, vmem, hbm, vmem, vmem],
        out_specs=(vmem, vmem, vmem),
        scratch_shapes=[
            pltpu.VMEM((2 * ids.shape[0], rows), half),
            pltpu.VMEM((devices,) + k.shape, half),
            pltpu.VMEM((devices,) + v.shape, half),
            pltpu.VMEM((devices,) + w.shape, half),
            pltpu.VMEM((all_heads, rows, HD), jnp.float32),
            pltpu.VMEM((all_heads, rows, 2 * HD), jnp.float32),
            pltpu.VMEM((rows, width), half),
            dma((4,)),
        ]
        + [dma((chips, 3))] * 4
        + [dma((chips, 2))] * 4
        + [dma((chips,))] * 4,
        compiler_params=pltpu.CompilerParams(
            collective_id=collective_id, has_side_effects=True, vmem_limit_bytes=62 << 20
        ),
    )(count, q, k, v, ids, weights, w, hidden, gain)


def moe_kernel(
    devices, live, cap, pieces,
    count_ref, x_ref, mixed_ref, route_ref, wg_ref, wu_ref, wd_ref, o_ref, all_ref,
    mixed, wg, wu, wd, xb, picked, chosen, part, away, near_in, ring_in,
    w_sem, x_sem, g_send, g_recv, n_send, n_recv, s_send, s_recv, a_send, a_recv,
):
    chips = devices // 2
    me = lax.axis_index("shard")
    group = lax.axis_index("groups")
    core = me % 2
    way = 1 - 2 * core
    place = ring_place(chips, me // 2)
    rows, depth = x_ref.shape
    local = wg.shape[0]
    topk = route_ref.shape[1] // 2

    def chip_at(offset):
        return ring_chip(chips, (place + offset + 2 * chips) % chips)

    def own_origin(t):
        return chip_at(-way * t) * 2 + core

    def sib_origin(t):
        return chip_at(way * t) * 2 + 1 - core

    def when_live(origin, action):
        if live == chips:
            action()
        else:
            pl.when(origin // 2 < live)(action)

    ahead, behind, sibling = own_origin(-1), own_origin(1), me + way

    def span(piece):
        size = rows // pieces
        return pl.ds(piece * size, size)

    def remote(src, dst, send, recv, to):
        return pltpu.make_async_remote_copy(
            src_ref=src, dst_ref=dst, send_sem=send, recv_sem=recv,
            device_id=(group, to), device_id_type=MESH,
        )

    def hop(t, piece, src=None):
        place_of = all_ref.at[own_origin(t), span(piece)]
        src = place_of if src is None else src.at[span(piece)]
        return remote(src, place_of, g_send.at[t, piece], g_recv.at[t, piece], ahead)

    def near(t, piece, src=None):
        place_of = all_ref.at[own_origin(t), span(piece)]
        src = place_of if src is None else src.at[span(piece)]
        return remote(src, place_of, n_send.at[t, piece], n_recv.at[t, piece], sibling)

    def near_landing(t, piece):
        place_of = all_ref.at[sib_origin(t), span(piece)]
        return remote(place_of, place_of, n_send.at[t, piece], n_recv.at[t, piece], sibling)

    def landing(t, piece):
        place_of = all_ref.at[own_origin(t + 1), span(piece)]
        return remote(place_of, place_of, g_send.at[t, piece], g_recv.at[t, piece], ahead)

    def give(t):
        return remote(away.at[t % 2], near_in.at[t], a_send.at[t], a_recv.at[t], sibling)

    def pass_on(t, piece):
        return remote(
            part.at[t + 1, span(piece)], ring_in.at[t, span(piece)],
            s_send.at[t, piece], s_recv.at[t, piece], ahead,
        )

    loads = [
        pltpu.make_async_copy(src, dst, w_sem.at[i])
        for i, (src, dst) in enumerate(
            ((wg_ref, wg), (wu_ref, wu), (wd_ref, wd), (mixed_ref, mixed))
        )
    ]

    barrier = pltpu.get_barrier_semaphore()
    for other in (ahead, behind, sibling):
        pl.semaphore_signal(barrier, inc=1, device_id=(group, other), device_id_type=MESH)
    pl.semaphore_wait(barrier, 3)

    def begin():
        for piece in range(pieces):
            hop(0, piece, x_ref).start()
        for piece in range(pieces):
            near(0, piece, x_ref).start()

    when_live(me, begin)
    for load in loads:
        load.start()

    def tick(t):
        def move():
            for piece in range(pieces):
                landing(t, piece).wait_recv()

                @pl.when(t + 1 < chips - 1)
                def _(piece=piece):
                    hop(t + 1, piece).start()

                near(t + 1, piece).start()

        when_live(own_origin(t + 1), move)

    def pick(t):
        parity = (t // 2) % 2

        def fetch(k, origin):
            return pltpu.make_async_copy(all_ref.at[origin], xb.at[k], x_sem.at[k])

        def fetch_own():
            @pl.when(t == 0)
            def _():
                pltpu.make_async_copy(x_ref, xb.at[0], x_sem.at[0]).start()

            @pl.when(t > 0)
            def _():
                fetch(0, own_origin(t)).start()

        def fetch_sib():
            for piece in range(pieces):
                near_landing(t, piece).wait_recv()
            fetch(1, sib_origin(t)).start()

        when_live(own_origin(t), fetch_own)
        when_live(sib_origin(t), fetch_sib)
        before = (
            lax.broadcasted_iota(jnp.int32, (rows, rows), 0)
            < lax.broadcasted_iota(jnp.int32, (rows, rows), 1)
        ).astype(jnp.bfloat16)
        slot_at = lax.broadcasted_iota(jnp.int32, (cap, rows), 0).astype(jnp.float32)
        for k, origin in ((0, own_origin(t)), (1, sib_origin(t))):
            q = 2 * (t % 2) + k
            place_of = pl.ds(pl.multiple_of(q * cap, 16), cap)

            def choose(k=k, origin=origin, q=q, place_of=place_of):
                fetch(k, origin).wait()
                route = route_ref[origin].astype(jnp.float32)
                ids, weights = route[:topk], route[topk:]
                at = origin * rows + lax.broadcasted_iota(jnp.int32, (1, rows), 1)
                alive = at < count_ref[0]
                hits, gains = [], []
                for e in range(local):
                    match = ids == (me * local + e).astype(jnp.float32)
                    hits.append(jnp.sum(jnp.where(match, 1.0, 0.0), axis=0, keepdims=True))
                    gain = jnp.sum(jnp.where(match, weights, 0.0), axis=0, keepdims=True)
                    gains.append(jnp.where(alive, gain, 0.0))
                rest = jnp.zeros((-local % 8, rows), jnp.float32)
                slots = jnp.dot(
                    jnp.concatenate(hits + [rest], axis=0).astype(jnp.bfloat16),
                    before,
                    preferred_element_type=jnp.float32,
                )
                mine, weighted = [], []
                for e in range(local):
                    hit = (slot_at == slots[e : e + 1]) & (hits[e] > 0.5)
                    mine.append(jnp.where(hit, 1.0, 0.0))
                    weighted.append(jnp.where(hit, gains[e], 0.0))
                choice = jnp.concatenate(mine, axis=0).astype(jnp.bfloat16)
                chosen[parity, q] = jnp.concatenate(weighted, axis=0).astype(jnp.bfloat16)
                rows_here = jnp.dot(choice, xb[k], preferred_element_type=jnp.float32)
                rows_here = rows_here.astype(jnp.bfloat16)
                for e in range(local):
                    picked[parity, e, place_of, :] = rows_here[e * cap : (e + 1) * cap]

            when_live(origin, choose)
            if live < chips:

                @pl.when(origin // 2 >= live)
                def _(place_of=place_of):
                    for e in range(local):
                        picked[parity, e, place_of, :] = jnp.zeros((cap, depth), jnp.bfloat16)

    def expert(b, e):
        parity = b % 2
        mine = picked[parity, e]
        gate = jnp.dot(mine, wg[e], preferred_element_type=jnp.float32)
        up = jnp.dot(mine, wu[e], preferred_element_type=jnp.float32)
        act = (gate / (1.0 + jnp.exp(-gate)) * up).astype(jnp.bfloat16)
        down = jnp.dot(act, wd[e], preferred_element_type=jnp.float32)
        picked[parity, e] = down.astype(jnp.bfloat16)

    def back(b):
        parity = b % 2
        for q in range(4):
            t = 2 * b + q // 2
            origin = own_origin(t) if q % 2 == 0 else sib_origin(t)

            def put(t=t, q=q):
                rows_here = jnp.concatenate(
                    [picked[parity, e, q * cap : (q + 1) * cap, :] for e in range(local)], axis=0
                )
                total = lax.dot_general(
                    chosen[parity, q], rows_here, (((0,), (0,)), ((), ())),
                    preferred_element_type=jnp.float32,
                ).astype(jnp.bfloat16)
                if q % 2 == 0:
                    part[t] = total
                else:

                    @pl.when(t >= 2)
                    def _():
                        when_live(sib_origin(t - 2), give(t - 2).wait_send)

                    away[t % 2] = total
                    give(t).start()

            if q % 2 == 1 and live < chips:

                @pl.when((origin // 2 >= live) & (t >= 2))
                def _(t=t):
                    when_live(sib_origin(t - 2), give(t - 2).wait_send)

            when_live(origin, put)

    def scatter(t):
        slot = (t + 1) % chips

        def move():
            give(slot).wait_recv()
            for piece in range(pieces):
                here = span(piece)
                total = part[slot, here, :].astype(jnp.float32) + near_in[slot, here, :].astype(
                    jnp.float32
                )
                if not (isinstance(t, int) and t == 0):
                    pass_on(t - 1, piece).wait_recv()
                    total = total + ring_in[t - 1, here, :].astype(jnp.float32)
                if isinstance(t, int) and t == chips - 1:
                    o_ref[here, :] = (mixed[here, :] + total).astype(o_ref.dtype)
                else:
                    part[slot, here, :] = total.astype(part.dtype)
                    pass_on(t, piece).start()

        when_live(own_origin(slot), move)

    def unit(u, carry):
        @pl.when(u == chips - 2)
        def _():
            scatter(0)

        @pl.when(u < chips - 1)
        def _():
            tick(u)

        @pl.when(u < chips)
        def _():
            pick(u)

        @pl.when(u == 1)
        def _():
            for load in loads:
                load.wait()

        @pl.when(u >= 1)
        def _():
            expert((u - 1) // 2, (u - 1) % 2)

        @pl.when((u >= 1) & (u % 2 == 0))
        def _():
            back((u - 1) // 2)

        @pl.when(u == chips - 1)
        def _():
            scatter(1)

        @pl.when(u == chips)
        def _():
            scatter(2)

        return carry

    lax.fori_loop(0, chips + 1, unit, 0)

    def later(t, carry):
        scatter(t)
        return carry

    lax.fori_loop(3, chips - 1, later, 0)
    if live < chips:
        o_ref[...] = mixed[...].astype(o_ref.dtype)
    scatter(chips - 1)

    def settle(t, carry):
        def own():
            for piece in range(pieces):
                near(t, piece).wait_send()

                @pl.when(t < chips - 1)
                def _(piece=piece):
                    hop(t, piece).wait_send()

                @pl.when(t > 0)
                def _(piece=piece):
                    pass_on(t - 1, piece).wait_send()

        def sib():
            @pl.when(t >= chips - 2)
            def _():
                give(t).wait_send()

        when_live(own_origin(t), own)
        when_live(sib_origin(t), sib)
        return carry

    lax.fori_loop(0, chips, settle, 0)


def moe(count, x, mixed, routes, w_gate, w_up, w_down, devices, cap, live, collective_id, pieces=2):
    rows, depth = x.shape
    chips = devices // 2
    local = w_gate.shape[0]
    dma = pltpu.SemaphoreType.DMA
    both = dma((chips, pieces))
    hbm = pl.BlockSpec(memory_space=pltpu.HBM)
    vmem = pl.BlockSpec(memory_space=pltpu.VMEM)
    block = (rows, depth)
    half = jnp.bfloat16
    return pl.pallas_call(
        functools.partial(moe_kernel, devices, live, cap, pieces),
        out_shape=(
            jax.ShapeDtypeStruct(block, half),
            jax.ShapeDtypeStruct((devices,) + block, half),
        ),
        in_specs=[pl.BlockSpec(memory_space=pltpu.SMEM), hbm, hbm, vmem, hbm, hbm, hbm],
        out_specs=(vmem, hbm),
        scratch_shapes=[
            pltpu.VMEM(block, jnp.float32),
            pltpu.VMEM(w_gate.shape, half),
            pltpu.VMEM(w_up.shape, half),
            pltpu.VMEM(w_down.shape, half),
            pltpu.VMEM((2,) + block, half),
            pltpu.VMEM((2, local, 4 * cap, depth), half),
            pltpu.VMEM((2, 4, local * cap, rows), half),
            pltpu.VMEM((chips,) + block, half),
            pltpu.VMEM((2,) + block, half),
            pltpu.VMEM((chips,) + block, half),
            pltpu.VMEM((chips - 1,) + block, half),
            dma((4,)),
            dma((2,)),
            both, both, both, both, both, both,
            dma((chips,)),
            dma((chips,)),
        ],
        compiler_params=pltpu.CompilerParams(
            collective_id=collective_id, has_side_effects=True, vmem_limit_bytes=63 << 20
        ),
    )(count, x, mixed, routes, w_gate, w_up, w_down)[0]


def per_device(
    hidden,
    query_rows,
    key_rows,
    value_rows,
    counts,
    out_weight,
    norm_gain,
    route_ids,
    route_weights,
    w_gate,
    w_up,
    w_down,
):
    devices = lax.axis_size("shard")
    me = lax.axis_index("shard")
    tok_dev, depth = hidden.shape
    topk = route_ids.shape[1]
    local = w_gate.shape[0]
    experts = local * devices
    capacity = max(2, tok_dev * topk * 5 // (4 * experts))
    capacity = -(-capacity // 16) * 16

    normed, mixed_rows, routes_all = front(
        counts, query_rows, key_rows, value_rows, route_ids.T, route_weights.T, out_weight, hidden,
        norm_gain, devices, 1,
    )
    return moe(
        counts, normed, mixed_rows, routes_all, w_gate, w_up, w_down, devices, capacity,
        devices // 2, 2,
    )


def solution(mesh):
    rows = P(("groups", "shard"), None)
    weights = P("shard", None, None)
    return jax.shard_map(
        per_device,
        mesh=mesh,
        in_specs=(
            rows,
            rows,
            rows,
            rows,
            P("groups"),
            P("shard", None),
            P(),
            rows,
            rows,
            weights,
            weights,
            weights,
        ),
        out_specs=rows,
        check_vma=False,
    )
```

```python
import functools
import math

import jax
import jax.numpy as jnp
from jax import lax
from jax.experimental import pallas as pl
from jax.experimental.pallas import tpu as pltpu
from jax.sharding import PartitionSpec as P

HD = 128
SEQ_LEN = 4096
NEG = -1e30
MESH = pl.DeviceIdType.MESH


def ring_place(chips, index):
    if chips == 8:
        z, y = index // 2, index % 2
        return z + y * (7 - 2 * z)
    return index


def ring_chip(chips, place):
    if chips == 8:
        half = place // 4
        z = place + half * (7 - 2 * place)
        return 2 * z + half
    return place


def front_kernel(
    devices, kv_count, heads,
    count_ref, q_ref, k_ref, v_ref, ids_ref, weights_ref, w_ref, hidden_ref, gain_ref,
    normed_ref, mixed_out, allr,
    mixed_ref, r_ref, allk, allv, allw, top, total, att,
    own_sem, kv_send, kv_recv, kn_send, kn_recv,
    w_send, w_recv, n_send, n_recv, x_send, x_recv, m_send, m_recv,
):
    chips = devices // 2
    me = lax.axis_index("shard")
    group = lax.axis_index("groups")
    core = me % 2
    way = 1 - 2 * core
    place = ring_place(chips, me // 2)
    rows = q_ref.shape[0]
    depth = w_ref.shape[1]
    scale = math.log2(math.e) / math.sqrt(HD)
    deep = w_ref.shape[0]
    lone = deep * 3 // 8 // 16 * 16
    shared = deep - 2 * lone
    side = group % 2
    partner = group + 1 - 2 * side

    def chip_at(offset):
        return ring_chip(chips, (place + offset + 2 * chips) % chips)

    def own_origin(t):
        return chip_at(-way * t) * 2 + core

    def sib_origin(t):
        return chip_at(way * t) * 2 + 1 - core

    ahead, behind, sibling = own_origin(-1), own_origin(1), me + way
    edge = deep - lone
    pieces = (pl.ds(pl.multiple_of(side * edge, 16), lone), pl.ds(lone, shared))
    theirs = pl.ds(pl.multiple_of((1 - side) * edge, 16), lone)
    small = ((k_ref, allk), (v_ref, allv), (r_ref, allr))

    def remote(src, dst, send, recv, to, to_group=None):
        return pltpu.make_async_remote_copy(
            src_ref=src, dst_ref=dst, send_sem=send, recv_sem=recv,
            device_id=(group if to_group is None else to_group, to), device_id_type=MESH,
        )

    def kv_hop(t, i, src=None):
        at = small[i][1].at[own_origin(t)]
        return remote(at if src is None else src, at, kv_send.at[t, i], kv_recv.at[t, i], ahead)

    def kv_landing(t, i):
        at = small[i][1].at[own_origin(t)]
        return remote(at, at, kv_send.at[t - 1, i], kv_recv.at[t - 1, i], ahead)

    def kv_near(t, i, src=None):
        at = small[i][1].at[own_origin(t)]
        return remote(at if src is None else src, at, kn_send.at[t, i], kn_recv.at[t, i], sibling)

    def kv_near_landing(t, i):
        at = small[i][1].at[sib_origin(t)]
        return remote(at, at, kn_send.at[t, i], kn_recv.at[t, i], sibling)

    def w_hop(t, i, src=None):
        at = allw.at[own_origin(t), pieces[i]]
        src = at if src is None else src.at[pieces[i]]
        return remote(src, at, w_send.at[t, i], w_recv.at[t, i], ahead)

    def w_landing(t, i):
        at = allw.at[own_origin(t), pieces[i]]
        return remote(at, at, w_send.at[t - 1, i], w_recv.at[t - 1, i], ahead)

    def w_near(t, i):
        at = allw.at[own_origin(t), pieces[i]]
        return remote(at, at, n_send.at[t, i], n_recv.at[t, i], sibling)

    def w_near_landing(t, i):
        at = allw.at[sib_origin(t), pieces[i]]
        return remote(at, at, n_send.at[t, i], n_recv.at[t, i], sibling)

    def w_near_all(origin, src):
        return remote(src, allw.at[origin], n_send.at[0, 0], n_recv.at[0, 0], sibling)

    def cross(t):
        at = allw.at[own_origin(t), pieces[0]]
        return remote(at, at, x_send.at[t], x_recv.at[t], me, partner)

    def cross_landing(t):
        at = allw.at[own_origin(t), theirs]
        return remote(at, at, x_send.at[t], x_recv.at[t], me, partner)

    def cross_near(t):
        at = allw.at[own_origin(t), theirs]
        return remote(at, at, m_send.at[t], m_recv.at[t], sibling)

    def cross_near_landing(t):
        at = allw.at[sib_origin(t), theirs]
        return remote(at, at, m_send.at[t], m_recv.at[t], sibling)

    own = [
        pltpu.make_async_copy(src, dst.at[me], own_sem.at[i])
        for i, (src, dst) in enumerate(small + ((w_ref, allw),))
    ]

    barrier = pltpu.get_barrier_semaphore()
    for other in (ahead, behind, sibling):
        pl.semaphore_signal(barrier, inc=1, device_id=(group, other), device_id_type=MESH)
    pl.semaphore_signal(barrier, inc=1, device_id=(partner, me), device_id_type=MESH)

    r_ref[...] = jnp.concatenate(
        [ids_ref[...].astype(jnp.float32), weights_ref[...].astype(jnp.float32)], axis=0
    ).astype(jnp.bfloat16)
    pl.semaphore_wait(barrier, 4)

    for i in range(3):
        kv_hop(0, i, small[i][0]).start()
    for i in range(3):
        kv_near(0, i, small[i][0]).start()
    for copy in own:
        copy.start()
    w_near_all(me, w_ref).start()

    def kv_tick(t):
        for i in range(3):
            kv_landing(t, i).wait_recv()

            @pl.when(t < chips - 1)
            def _(i=i):
                kv_hop(t, i).start()

            kv_near(t, i).start()

    def w_tick(t):
        for i in range(2):
            w_landing(t, i).wait_recv()

            @pl.when(t < chips - 1)
            def _(i=i):
                w_hop(t, i).start()

            if i == 0:
                cross(t).start()
            w_near(t, i).start()

        @pl.when(t > 1)
        def _():
            cross_tick(t - 1)

    def cross_tick(t):
        cross_landing(t).wait_recv()
        cross_near(t).start()

    apart = lax.broadcasted_iota(jnp.int32, (rows, rows), 1) - lax.broadcasted_iota(
        jnp.int32, (rows, rows), 0
    )
    cut = 2
    part_heads = heads // cut
    per_set = kv_count * cut

    def fold(n, g, part, first, masked):
        origins = []
        for t in (2 * n, 2 * n + 1):
            origins += [own_origin(t), sib_origin(t)]
        lanes = pl.ds(pl.multiple_of(g * HD, HD), HD)
        keys = jnp.concatenate([allk[o, :, lanes] for o in origins], axis=0)
        values = jnp.concatenate([allv[o, :, lanes] for o in origins], axis=0)
        values = jnp.concatenate([values, jnp.ones(values.shape, jnp.bfloat16)], axis=1)
        width = part_heads * HD
        q_here = q_ref[:, pl.ds(pl.multiple_of((g * cut + part) * width, width), width)]

        def scores_of(h):
            scores = lax.dot_general(
                q_here[:, h * HD : (h + 1) * HD], keys, (((1,), (1,)), ((), ())),
                preferred_element_type=jnp.float32,
            )
            if not masked:
                return scores
            return jnp.concatenate(
                [
                    jnp.where(apart <= (me - o) * rows, scores[:, j * rows : (j + 1) * rows], NEG)
                    for j, o in enumerate(origins)
                ],
                axis=1,
            )

        later = scores_of(0)
        for h in range(part_heads):
            at = (g * cut + part) * part_heads + h
            scores = later
            if h + 1 < part_heads:
                later = scores_of(h + 1)
            new = jnp.max(scores, axis=1, keepdims=True) * scale
            if first:
                new = jnp.broadcast_to(new, (rows, HD))
            else:
                old = top[at]
                new = jnp.maximum(old, new)
            expo = jnp.exp2(scores * scale - new[:, :1]).astype(jnp.bfloat16)
            both = jnp.dot(expo, values, preferred_element_type=jnp.float32)
            if not first:
                factor = jnp.exp2(old - new)
                both = total[at] * jnp.concatenate([factor, factor], axis=1) + both
            total[at] = both
            top[at] = new

    segments = chips // 2 * per_set

    kv_tick(1)
    for copy in own:
        copy.wait()

    def segment(i, carry):
        n = i // per_set
        g = (i % per_set) // cut
        part = i % cut

        turn = i % per_set
        early, late = per_set // 2 - 1, per_set - 1
        t = jnp.where(turn == late, 2 * n + 3, 2 * n + 2)
        ticks = (turn == early) | (turn == late)

        @pl.when(ticks & (t < chips))
        def _():
            kv_tick(t)

        swift = (turn == early // 2) | (turn == early + 2)
        w_turn = 2 * n + jnp.where(turn == early + 2, 1, 0)

        @pl.when(swift & (w_turn == 1))
        def _():
            for k in range(2):
                w_hop(0, k, w_ref).start()

        @pl.when(swift & (w_turn > 1))
        def _():
            w_tick(w_turn - 1)

        @pl.when(i % per_set == 0)
        def _():
            for slot in (2 * n, 2 * n + 1):
                for k in range(3):
                    kv_near_landing(slot, k).wait_recv()

        some, every = False, True
        for slot in (2 * n, 2 * n + 1):
            for o in (own_origin(slot), sib_origin(slot)):
                some = (o <= me) | some
                every = (o < me) & every

        @pl.when(n == 0)
        def _():
            fold(n, g, part, True, True)

        @pl.when((n > 0) & every)
        def _():
            fold(n, g, part, False, False)

        @pl.when((n > 0) & some & jnp.logical_not(every))
        def _():
            fold(n, g, part, False, True)

        return carry

    lax.fori_loop(0, segments, segment, 0)

    alive = me * rows + lax.broadcasted_iota(jnp.int32, (rows, HD), 0) < count_ref[0]

    def close(at, carry):
        both = total[at]
        result = jnp.where(alive, both[:, :HD] / jnp.where(alive, both[:, HD:], 1.0), 0.0)
        att[:, pl.ds(pl.multiple_of(at * HD, HD), HD)] = result.astype(jnp.bfloat16)
        return carry

    sets = chips // 2
    tile = 256

    def project(b):
        for t in (2 * b, 2 * b + 1):

            @pl.when(t == 0)
            def _():
                w_near_all(sibling, allw.at[sibling]).wait_recv()

            @pl.when(t > 0)
            def _(t=t):
                for i in range(2):
                    w_near_landing(t, i).wait_recv()
                cross_near_landing(t).wait_recv()

        origins = []
        for t in (2 * b, 2 * b + 1):
            origins += [own_origin(t), sib_origin(t)]
        left = jnp.concatenate(
            [att[:, pl.ds(pl.multiple_of(o * deep, deep), deep)] for o in origins], axis=1
        )

        def column(c, carry):
            lanes = pl.ds(pl.multiple_of(c * tile, tile), tile)
            right = jnp.concatenate([allw[o, :, lanes] for o in origins], axis=0)
            mixed_ref[:, lanes] += jnp.dot(left, right, preferred_element_type=jnp.float32)
            return carry

        lax.fori_loop(0, depth // tile, column, 0)

    lax.fori_loop(0, kv_count * heads, close, 0)
    mixed_ref[...] = hidden_ref[...].astype(jnp.float32)

    def tail(b, carry):
        @pl.when(b == max(sets - 3, 0))
        def _():
            w_tick(chips - 1)

        @pl.when(b == sets - 1)
        def _():
            cross_tick(chips - 1)

        project(b)
        return carry

    lax.fori_loop(0, sets, tail, 0)

    keep = pltpu.make_async_copy(mixed_ref, mixed_out, own_sem.at[4])
    keep.start()
    step = 32
    gain = gain_ref[...].astype(jnp.float32).reshape(1, depth)

    def norm(c, carry):
        here = pl.ds(pl.multiple_of(c * step, step), step)
        mixed = mixed_ref[here, :]
        mean_square = jnp.mean(mixed * mixed, axis=1, keepdims=True)
        normed_ref[here, :] = (mixed * lax.rsqrt(mean_square + 1e-06) * gain).astype(jnp.bfloat16)
        return carry

    lax.fori_loop(0, rows // step, norm, 0)
    keep.wait()

    w_near_all(sibling, w_ref).wait_send()
    for i in range(2):
        w_hop(0, i, w_ref).wait_send()
    for i in range(3):
        kv_hop(0, i).wait_send()
        kv_near(0, i).wait_send()

    def settle(t, carry):
        for i in range(3):
            kv_near(t, i).wait_send()
        cross(t).wait_send()
        for i in range(2):
            w_near(t, i).wait_send()
        cross_near(t).wait_send()

        @pl.when(t < chips - 1)
        def _():
            for i in range(3):
                kv_hop(t, i).wait_send()
            for i in range(2):
                w_hop(t, i).wait_send()

        return carry

    lax.fori_loop(1, chips, settle, 0)


def front(count, q, k, v, ids, weights, w, hidden, gain, devices, collective_id):
    rows, width = q.shape
    depth = w.shape[1]
    chips = devices // 2
    kv_count = k.shape[1] // HD
    all_heads = width // HD
    half = jnp.bfloat16
    dma = pltpu.SemaphoreType.DMA
    hbm = pl.BlockSpec(memory_space=pltpu.HBM)
    vmem = pl.BlockSpec(memory_space=pltpu.VMEM)
    return pl.pallas_call(
        functools.partial(front_kernel, devices, kv_count, all_heads // kv_count),
        out_shape=(
            jax.ShapeDtypeStruct(hidden.shape, half),
            jax.ShapeDtypeStruct(hidden.shape, jnp.float32),
            jax.ShapeDtypeStruct((devices, 2 * ids.shape[0], rows), half),
        ),
        in_specs=[pl.BlockSpec(memory_space=pltpu.SMEM), vmem, hbm, hbm, vmem, vmem, hbm, vmem, vmem],
        out_specs=(vmem, hbm, vmem),
        scratch_shapes=[
            pltpu.VMEM(hidden.shape, jnp.float32),
            pltpu.VMEM((2 * ids.shape[0], rows), half),
            pltpu.VMEM((devices,) + k.shape, half),
            pltpu.VMEM((devices,) + v.shape, half),
            pltpu.VMEM((devices,) + w.shape, half),
            pltpu.VMEM((all_heads, rows, HD), jnp.float32),
            pltpu.VMEM((all_heads, rows, 2 * HD), jnp.float32),
            pltpu.VMEM((rows, width), half),
            dma((5,)),
        ]
        + [dma((chips, 3))] * 4
        + [dma((chips, 2))] * 4
        + [dma((chips,))] * 4,
        compiler_params=pltpu.CompilerParams(
            collective_id=collective_id, has_side_effects=True, vmem_limit_bytes=62 << 20
        ),
    )(count, q, k, v, ids, weights, w, hidden, gain)


def moe_kernel(
    devices, live, cap, pieces,
    count_ref, x_ref, mixed_ref, route_ref, wg_ref, wu_ref, wd_ref, o_ref, all_ref,
    mixed, wg, wu, wd, xb, picked, chosen, part, away, near_in, ring_in,
    w_sem, x_sem, g_send, g_recv, n_send, n_recv, s_send, s_recv, a_send, a_recv,
):
    chips = devices // 2
    me = lax.axis_index("shard")
    group = lax.axis_index("groups")
    core = me % 2
    way = 1 - 2 * core
    place = ring_place(chips, me // 2)
    rows, depth = x_ref.shape
    local = wg.shape[0]
    topk = route_ref.shape[1] // 2

    def chip_at(offset):
        return ring_chip(chips, (place + offset + 2 * chips) % chips)

    def own_origin(t):
        return chip_at(-way * t) * 2 + core

    def sib_origin(t):
        return chip_at(way * t) * 2 + 1 - core

    def when_live(origin, action):
        if live == chips:
            action()
        else:
            pl.when(origin // 2 < live)(action)

    ahead, behind, sibling = own_origin(-1), own_origin(1), me + way

    def span(piece):
        size = rows // pieces
        return pl.ds(piece * size, size)

    def remote(src, dst, send, recv, to):
        return pltpu.make_async_remote_copy(
            src_ref=src, dst_ref=dst, send_sem=send, recv_sem=recv,
            device_id=(group, to), device_id_type=MESH,
        )

    def hop(t, piece, src=None):
        place_of = all_ref.at[own_origin(t), span(piece)]
        src = place_of if src is None else src.at[span(piece)]
        return remote(src, place_of, g_send.at[t, piece], g_recv.at[t, piece], ahead)

    def near(t, piece, src=None):
        place_of = all_ref.at[own_origin(t), span(piece)]
        src = place_of if src is None else src.at[span(piece)]
        return remote(src, place_of, n_send.at[t, piece], n_recv.at[t, piece], sibling)

    def near_landing(t, piece):
        place_of = all_ref.at[sib_origin(t), span(piece)]
        return remote(place_of, place_of, n_send.at[t, piece], n_recv.at[t, piece], sibling)

    def landing(t, piece):
        place_of = all_ref.at[own_origin(t + 1), span(piece)]
        return remote(place_of, place_of, g_send.at[t, piece], g_recv.at[t, piece], ahead)

    def give(t):
        return remote(away.at[t % 2], near_in.at[t], a_send.at[t], a_recv.at[t], sibling)

    def pass_on(t, piece):
        return remote(
            part.at[t + 1, span(piece)], ring_in.at[t, span(piece)],
            s_send.at[t, piece], s_recv.at[t, piece], ahead,
        )

    loads = [
        pltpu.make_async_copy(src, dst, w_sem.at[i])
        for i, (src, dst) in enumerate(
            ((wg_ref, wg), (wu_ref, wu), (wd_ref, wd), (mixed_ref, mixed))
        )
    ]

    barrier = pltpu.get_barrier_semaphore()
    for other in (ahead, behind, sibling):
        pl.semaphore_signal(barrier, inc=1, device_id=(group, other), device_id_type=MESH)
    pl.semaphore_wait(barrier, 3)

    def begin():
        for piece in range(pieces):
            hop(0, piece, x_ref).start()
        for piece in range(pieces):
            near(0, piece, x_ref).start()

    when_live(me, begin)
    for load in loads:
        load.start()

    def tick(t):
        def move():
            for piece in range(pieces):
                landing(t, piece).wait_recv()

                @pl.when(t + 1 < chips - 1)
                def _(piece=piece):
                    hop(t + 1, piece).start()

                near(t + 1, piece).start()

        when_live(own_origin(t + 1), move)

    def pick(t):
        parity = (t // 2) % 2

        def fetch(k, origin):
            return pltpu.make_async_copy(all_ref.at[origin], xb.at[k], x_sem.at[k])

        def fetch_own():
            @pl.when(t == 0)
            def _():
                pltpu.make_async_copy(x_ref, xb.at[0], x_sem.at[0]).start()

            @pl.when(t > 0)
            def _():
                fetch(0, own_origin(t)).start()

        def fetch_sib():
            for piece in range(pieces):
                near_landing(t, piece).wait_recv()
            fetch(1, sib_origin(t)).start()

        when_live(own_origin(t), fetch_own)
        when_live(sib_origin(t), fetch_sib)
        before = (
            lax.broadcasted_iota(jnp.int32, (rows, rows), 0)
            < lax.broadcasted_iota(jnp.int32, (rows, rows), 1)
        ).astype(jnp.bfloat16)
        slot_at = lax.broadcasted_iota(jnp.int32, (cap, rows), 0).astype(jnp.float32)
        for k, origin in ((0, own_origin(t)), (1, sib_origin(t))):
            q = 2 * (t % 2) + k
            place_of = pl.ds(pl.multiple_of(q * cap, 16), cap)

            def choose(k=k, origin=origin, q=q, place_of=place_of):
                fetch(k, origin).wait()
                route = route_ref[origin].astype(jnp.float32)
                ids, weights = route[:topk], route[topk:]
                at = origin * rows + lax.broadcasted_iota(jnp.int32, (1, rows), 1)
                alive = at < count_ref[0]
                hits, gains = [], []
                for e in range(local):
                    match = ids == (me * local + e).astype(jnp.float32)
                    hits.append(jnp.sum(jnp.where(match, 1.0, 0.0), axis=0, keepdims=True))
                    gain = jnp.sum(jnp.where(match, weights, 0.0), axis=0, keepdims=True)
                    gains.append(jnp.where(alive, gain, 0.0))
                rest = jnp.zeros((-local % 8, rows), jnp.float32)
                slots = jnp.dot(
                    jnp.concatenate(hits + [rest], axis=0).astype(jnp.bfloat16),
                    before,
                    preferred_element_type=jnp.float32,
                )
                mine, weighted = [], []
                for e in range(local):
                    hit = (slot_at == slots[e : e + 1]) & (hits[e] > 0.5)
                    mine.append(jnp.where(hit, 1.0, 0.0))
                    weighted.append(jnp.where(hit, gains[e], 0.0))
                choice = jnp.concatenate(mine, axis=0).astype(jnp.bfloat16)
                chosen[parity, q] = jnp.concatenate(weighted, axis=0).astype(jnp.bfloat16)
                rows_here = jnp.dot(choice, xb[k], preferred_element_type=jnp.float32)
                rows_here = rows_here.astype(jnp.bfloat16)
                for e in range(local):
                    picked[parity, e, place_of, :] = rows_here[e * cap : (e + 1) * cap]

            when_live(origin, choose)
            if live < chips:

                @pl.when(origin // 2 >= live)
                def _(place_of=place_of):
                    for e in range(local):
                        picked[parity, e, place_of, :] = jnp.zeros((cap, depth), jnp.bfloat16)

    def expert(b, e):
        parity = b % 2
        mine = picked[parity, e]
        gate = jnp.dot(mine, wg[e], preferred_element_type=jnp.float32)
        up = jnp.dot(mine, wu[e], preferred_element_type=jnp.float32)
        act = (gate / (1.0 + jnp.exp(-gate)) * up).astype(jnp.bfloat16)
        down = jnp.dot(act, wd[e], preferred_element_type=jnp.float32)
        picked[parity, e] = down.astype(jnp.bfloat16)

    def back(b):
        parity = b % 2
        for q in range(4):
            t = 2 * b + q // 2
            origin = own_origin(t) if q % 2 == 0 else sib_origin(t)

            def put(t=t, q=q):
                rows_here = jnp.concatenate(
                    [picked[parity, e, q * cap : (q + 1) * cap, :] for e in range(local)], axis=0
                )
                total = lax.dot_general(
                    chosen[parity, q], rows_here, (((0,), (0,)), ((), ())),
                    preferred_element_type=jnp.float32,
                ).astype(jnp.bfloat16)
                if q % 2 == 0:
                    part[t] = total
                else:

                    @pl.when(t >= 2)
                    def _():
                        when_live(sib_origin(t - 2), give(t - 2).wait_send)

                    away[t % 2] = total
                    give(t).start()

            if q % 2 == 1 and live < chips:

                @pl.when((origin // 2 >= live) & (t >= 2))
                def _(t=t):
                    when_live(sib_origin(t - 2), give(t - 2).wait_send)

            when_live(origin, put)

    def scatter(t):
        slot = (t + 1) % chips

        def move():
            give(slot).wait_recv()
            for piece in range(pieces):
                here = span(piece)
                total = part[slot, here, :].astype(jnp.float32) + near_in[slot, here, :].astype(
                    jnp.float32
                )
                if not (isinstance(t, int) and t == 0):
                    pass_on(t - 1, piece).wait_recv()
                    total = total + ring_in[t - 1, here, :].astype(jnp.float32)
                if isinstance(t, int) and t == chips - 1:
                    o_ref[here, :] = (mixed[here, :] + total).astype(o_ref.dtype)
                else:
                    part[slot, here, :] = total.astype(part.dtype)
                    pass_on(t, piece).start()

        when_live(own_origin(slot), move)

    def unit(u, carry):
        @pl.when(u == chips - 2)
        def _():
            scatter(0)

        @pl.when(u < chips - 1)
        def _():
            tick(u)

        @pl.when(u < chips)
        def _():
            pick(u)

        @pl.when(u == 1)
        def _():
            for load in loads:
                load.wait()

        @pl.when(u >= 1)
        def _():
            expert((u - 1) // 2, (u - 1) % 2)

        @pl.when((u >= 1) & (u % 2 == 0))
        def _():
            back((u - 1) // 2)

        @pl.when(u == chips - 1)
        def _():
            scatter(1)

        @pl.when(u == chips)
        def _():
            scatter(2)

        return carry

    lax.fori_loop(0, chips + 1, unit, 0)

    def later(t, carry):
        scatter(t)
        return carry

    lax.fori_loop(3, chips - 1, later, 0)
    if live < chips:
        o_ref[...] = mixed[...].astype(o_ref.dtype)
    scatter(chips - 1)

    def settle(t, carry):
        def own():
            for piece in range(pieces):
                near(t, piece).wait_send()

                @pl.when(t < chips - 1)
                def _(piece=piece):
                    hop(t, piece).wait_send()

                @pl.when(t > 0)
                def _(piece=piece):
                    pass_on(t - 1, piece).wait_send()

        def sib():
            @pl.when(t >= chips - 2)
            def _():
                give(t).wait_send()

        when_live(own_origin(t), own)
        when_live(sib_origin(t), sib)
        return carry

    lax.fori_loop(0, chips, settle, 0)


def moe(count, x, mixed, routes, w_gate, w_up, w_down, devices, cap, live, collective_id, pieces=2):
    rows, depth = x.shape
    chips = devices // 2
    local = w_gate.shape[0]
    dma = pltpu.SemaphoreType.DMA
    both = dma((chips, pieces))
    hbm = pl.BlockSpec(memory_space=pltpu.HBM)
    vmem = pl.BlockSpec(memory_space=pltpu.VMEM)
    block = (rows, depth)
    half = jnp.bfloat16
    return pl.pallas_call(
        functools.partial(moe_kernel, devices, live, cap, pieces),
        out_shape=(
            jax.ShapeDtypeStruct(block, half),
            jax.ShapeDtypeStruct((devices,) + block, half),
        ),
        in_specs=[pl.BlockSpec(memory_space=pltpu.SMEM), hbm, hbm, vmem, hbm, hbm, hbm],
        out_specs=(vmem, hbm),
        scratch_shapes=[
            pltpu.VMEM(block, jnp.float32),
            pltpu.VMEM(w_gate.shape, half),
            pltpu.VMEM(w_up.shape, half),
            pltpu.VMEM(w_down.shape, half),
            pltpu.VMEM((2,) + block, half),
            pltpu.VMEM((2, local, 4 * cap, depth), half),
            pltpu.VMEM((2, 4, local * cap, rows), half),
            pltpu.VMEM((chips,) + block, half),
            pltpu.VMEM((2,) + block, half),
            pltpu.VMEM((chips,) + block, half),
            pltpu.VMEM((chips - 1,) + block, half),
            dma((4,)),
            dma((2,)),
            both, both, both, both, both, both,
            dma((chips,)),
            dma((chips,)),
        ],
        compiler_params=pltpu.CompilerParams(
            collective_id=collective_id, has_side_effects=True, vmem_limit_bytes=63 << 20
        ),
    )(count, x, mixed, routes, w_gate, w_up, w_down)[0]


def per_device(
    hidden,
    query_rows,
    key_rows,
    value_rows,
    counts,
    out_weight,
    norm_gain,
    route_ids,
    route_weights,
    w_gate,
    w_up,
    w_down,
):
    devices = lax.axis_size("shard")
    me = lax.axis_index("shard")
    tok_dev, depth = hidden.shape
    topk = route_ids.shape[1]
    local = w_gate.shape[0]
    experts = local * devices
    capacity = max(2, tok_dev * topk * 5 // (4 * experts))
    capacity = -(-capacity // 16) * 16

    normed, mixed_rows, routes_all = front(
        counts, query_rows, key_rows, value_rows, route_ids.T, route_weights.T, out_weight, hidden,
        norm_gain, devices, 1,
    )
    return moe(
        counts, normed, mixed_rows, routes_all, w_gate, w_up, w_down, devices, capacity,
        devices // 2, 2,
    )


def solution(mesh):
    rows = P(("groups", "shard"), None)
    weights = P("shard", None, None)
    return jax.shard_map(
        per_device,
        mesh=mesh,
        in_specs=(
            rows,
            rows,
            rows,
            rows,
            P("groups"),
            P("shard", None),
            P(),
            rows,
            rows,
            weights,
            weights,
            weights,
        ),
        out_specs=rows,
        check_vma=False,
    )
```
